128 devices in a mesh: pairs: 128 (over x, z, y, core).
Axes of the slice: x: 4, y: 4, z: 4, core: 2. Of those that a mesh axis runs over, the one named last changes fastest.
Arguments:
- blocks: bfloat16 [2048, 512, 512], P('pairs'), may hold values from -6 to 6
- pair_orbitals: int32 [4096, 2], replicated, may hold values from 0 to 2047, as said below
- block_sizes: int32 [2048], replicated, may hold values from 256 to 512, as said below
- pno_maps: bfloat16 [4096, 512, 128], P('pairs'), may hold values from -0.25 to 0.25
- pno_sizes: int32 [4096], P('pairs'), may hold values from 32 to 128, as said below
- pno_energy: float32 [4096, 128], P('pairs'), may hold values from 0.3 to 3
- pair_shift: float32 [4096], P('pairs'), may hold values from 0.5 to 2
- neighbours: int32 [4096, 8], P('pairs'), may hold values from 0 to 4095, as said below
- intersections: bfloat16 [4096, 8, 128, 128], P('pairs'), may hold values from -0.5 to 0.5
Outputs:
- amplitudes: float32 [4096, 128, 128], P('pairs')
- pair_energy: float32 [4096], P('pairs')
The draws below stay inside these ranges and needn't reach their ends.
Inputs may be any that keep to these rules, and one draw needn't show every extreme that they name: `pair_orbitals`: pair p is owned by device p // 32; its first orbital is one of the 16 orbitals that this device holds (orbital o is held by device o // 16), and its second orbital is held by the owner or by one of the two devices next to it. On every device but the first, its first owned pair takes its second orbital from the device on the left; on every device but the last, its second owned pair takes it from the device on the right. `neighbours`: every listed coupled pair is owned by the pair's owner or by one of the two devices next to it. `block_sizes`: some orbital has all 512 rows live in every draw. `pno_sizes`: some pair has all 128 natural orbitals live in every draw.
All inputs are finite; a program needn't handle non-finite values.
Results may differ from the reference program's by a relative error of at most 0.0038.
Values may be sent and summed in bfloat16 or wider, within the bound.
No kernel may reach another device: no remote copies, remote signals or barrier semaphores. Data moves between devices by JAX's collectives and lax.ppermute only.
A program may use at most 192 MiB of HBM per device.

```python
import math
import jax
import jax.numpy as jnp
from jax import lax

NAUX = 512
NPAO = 512
NPNO = 128
OCC_DEV = 16
PAIR_DEV = 32
NEIGH = 8
ITERS = 2
OCC = 2048
PAIRS = 4096


def draw_pair_orbitals(key, part):
    key_one, key_two, key_three = jax.random.split(jax.random.fold_in(key, 11), 3)
    devices = PAIRS // PAIR_DEV
    pair_index = jnp.arange(PAIRS, dtype=jnp.int32)
    owner_device = pair_index // PAIR_DEV
    slot_index = pair_index % PAIR_DEV
    first_orbital = owner_device * OCC_DEV + jax.random.randint(key_one, (PAIRS,), 0, OCC_DEV)
    offset = jax.random.randint(key_two, (PAIRS,), -1, 2)
    offset = jnp.where(slot_index == 0, -1, jnp.where(slot_index == 1, 1, offset))
    other_device = jnp.clip(owner_device + offset, 0, devices - 1)
    second_orbital = other_device * OCC_DEV + jax.random.randint(key_three, (PAIRS,), 0, OCC_DEV)
    return jnp.stack([first_orbital, second_orbital], axis=1).astype(jnp.int32)


def draw_neighbours(key, part):
    key_one, key_two = jax.random.split(jax.random.fold_in(key, 23), 2)
    devices = PAIRS // PAIR_DEV
    owner_device = jnp.arange(PAIRS, dtype=jnp.int32) // PAIR_DEV
    other_device = jnp.clip(owner_device[:, None] + jax.random.randint(key_one, (PAIRS, NEIGH), -1, 2), 0, devices - 1)
    chosen = other_device * PAIR_DEV + jax.random.randint(key_two, (PAIRS, NEIGH), 0, PAIR_DEV)
    return chosen.astype(jnp.int32)


def draw_block_sizes(key, part):
    key_one, key_two = jax.random.split(jax.random.fold_in(key, 37), 2)
    sizes = jax.random.randint(key_one, (OCC,), NAUX // 2, NAUX + 1)
    full_spot = jax.random.randint(key_two, (), 0, OCC)
    return jnp.where(jnp.arange(OCC) == full_spot, NAUX, sizes).astype(jnp.int32)


def draw_pno_sizes(key, part):
    key_one, key_two = jax.random.split(jax.random.fold_in(key, 41), 2)
    sizes = jax.random.randint(key_one, (PAIRS,), NPNO // 4, NPNO + 1)
    full_spot = jax.random.randint(key_two, (), 0, PAIRS)
    return jnp.where(jnp.arange(PAIRS) == full_spot, NPNO, sizes).astype(jnp.int32)


def block_scale(rng, shape, pieces, smallest, top_value):
    loudness = 1.0
    for dim, blocks in pieces:
        steps = jax.random.uniform(jax.random.fold_in(jax.random.fold_in(rng, 6), dim), (blocks,), jnp.float32, smallest / len(pieces), top_value / len(pieces))
        loudness = loudness * jnp.repeat(jnp.exp(steps), shape[dim] // blocks).reshape((-1,) + (1,) * (len(shape) - 1 - dim))
    return loudness


def gaussian(own_key, dims, deviation, reach, pieces=(), kind=jnp.bfloat16):
    level = block_scale(own_key, dims, pieces, -0.22, 0.18) if pieces else 1.0
    result = jax.random.normal(own_key, dims, jnp.float32) * deviation * level
    return jnp.minimum(jnp.maximum(result, -reach), reach).astype(kind)


def setup_inputs(seed: int = 0) -> dict:
    key_of = jax.random.split(jax.random.key(seed), 10)
    blocks = gaussian(key_of[0], (OCC, NAUX, NPAO), 1.0, 6.0, ((0, 128),))
    pair_orbitals = draw_pair_orbitals(jax.random.fold_in(key_of[9], 71), 0)
    block_sizes = draw_block_sizes(jax.random.fold_in(key_of[9], 71), 0)
    pno_maps = gaussian(key_of[3], (PAIRS, NPAO, NPNO), NPAO ** -0.5, 0.25, ((0, 128),))
    pno_sizes = draw_pno_sizes(jax.random.fold_in(key_of[9], 71), 0)
    pno_energy = jnp.clip(jnp.exp(math.log(3.0) - 2.3025851 * jax.random.uniform(key_of[5], (PAIRS, NPNO), jnp.float32) ** block_scale(key_of[5], (PAIRS, NPNO), ((0, 128),), -0.2, 0.2)), 0.3, 3.0)
    pair_shift = jnp.clip(jnp.exp(math.log(2.0) - 1.3862944 * jax.random.uniform(key_of[6], (PAIRS,), jnp.float32) ** block_scale(key_of[6], (PAIRS,), ((0, 128),), -0.2, 0.2)), 0.5, 2.0)
    neighbours = draw_neighbours(jax.random.fold_in(key_of[9], 71), 0)
    intersections = gaussian(key_of[8], (PAIRS, NEIGH, NPNO, NPNO), NPNO ** -0.5, 0.5, ((0, 128),))
    return dict(blocks=blocks, pair_orbitals=pair_orbitals, block_sizes=block_sizes, pno_maps=pno_maps, pno_sizes=pno_sizes, pno_energy=pno_energy, pair_shift=pair_shift, neighbours=neighbours, intersections=intersections)


coupling_weight = 0.35

def reference(blocks, pair_orbitals, block_sizes, pno_maps, pno_sizes, pno_energy, pair_shift, neighbours, intersections):
    largest_value = lax.Precision.HIGHEST
    aux_rows = jnp.arange(NAUX, dtype=jnp.int32)
    inverse = 1.0 / math.sqrt(NAUX)

    def masked_block_list(orbital_ids):
        chosen = blocks[orbital_ids]
        keep_rows = aux_rows[None, :] < block_sizes[orbital_ids][:, None]
        return jnp.where(keep_rows[:, :, None], chosen, jnp.zeros((), blocks.dtype))

    def group_integrals(operands):
        orbital_list, maps = operands
        maps_factor = maps.astype(jnp.float32)
        left_half_slice = jnp.einsum('zde,zen->zdn', masked_block_list(orbital_list[:, 0]).astype(jnp.float32), maps_factor, precision=largest_value).astype(jnp.bfloat16)
        right_half_slice = jnp.einsum('zde,zen->zdn', masked_block_list(orbital_list[:, 1]).astype(jnp.float32), maps_factor, precision=largest_value).astype(jnp.bfloat16)
        return jnp.einsum('pqa,pqb->pab', left_half_slice.astype(jnp.float32), right_half_slice.astype(jnp.float32), precision=largest_value) * inverse
    group_total = PAIRS // PAIR_DEV
    integrals = lax.map(group_integrals, (pair_orbitals.reshape(group_total, PAIR_DEV, 2), pno_maps.reshape(group_total, PAIR_DEV, NPAO, NPNO)))
    integrals = integrals.reshape(PAIRS, NPNO, NPNO)
    pno_index = jnp.arange(NPNO, dtype=jnp.int32)
    live = pno_index[None, :] < pno_sizes[:, None]
    pno_mask = live[:, :, None] & live[:, None, :]
    denominator = pno_energy[:, :, None] + pno_energy[:, None, :] + pair_shift[:, None, None]
    amplitudes = jnp.where(pno_mask, -integrals / denominator, jnp.zeros((), jnp.float32))
    grouped_neighbours = neighbours.reshape(group_total, PAIR_DEV, NEIGH)
    grouped_intersections = intersections.reshape(group_total, PAIR_DEV, NEIGH, NPNO, NPNO)
    for iteration in range(ITERS):
        previous = amplitudes

        def group_coupling(operands):
            neighbour_ids, intersection_group = operands
            nearby = previous[neighbour_ids]
            intersection_factor = intersection_group.astype(jnp.float32)
            mixed = jnp.einsum('pnac,pncd->pnad', intersection_factor, nearby, precision=largest_value)
            return jnp.einsum('pnad,pnbd->pab', mixed, intersection_factor, precision=largest_value)
        coupling = lax.map(group_coupling, (grouped_neighbours, grouped_intersections)).reshape(PAIRS, NPNO, NPNO)
        amplitudes = jnp.where(pno_mask, -(integrals + coupling_weight * coupling) / denominator, jnp.zeros((), jnp.float32))
    pair_energy = lax.optimization_barrier(jnp.sum(integrals * amplitudes, axis=(1, 2))) / (NPNO * NPNO)
    return (amplitudes, pair_energy)
```

```python
import functools
import math

import jax
import jax.numpy as jnp
from jax import lax
from jax.experimental import pallas as pl
from jax.experimental.pallas import tpu as pltpu
from jax.sharding import PartitionSpec as P

ITERS = 2
COUPLING = 0.35
SLOTS = (16, 18, 20, 24, 32)
GROUP = 8
VMEM_LIMIT = 60 * 1024 * 1024

ANY = pl.BlockSpec(memory_space=pl.ANY)
VMEM = pl.BlockSpec(memory_space=pltpu.VMEM)
SMEM = pl.BlockSpec(memory_space=pltpu.SMEM)

ONE, SRC, SERVE, LIVE, PNO, NEAR = 0, 32, 64, 96, 128, 160


def call(body, outs, out_specs, in_specs, scratch, flops=0, moved=0, aliases=None, name=None):
    return pl.pallas_call(
        body,
        out_shape=outs,
        in_specs=in_specs,
        out_specs=out_specs,
        scratch_shapes=scratch,
        input_output_aliases=aliases or {},
        compiler_params=pltpu.CompilerParams(vmem_limit_bytes=VMEM_LIMIT),
        cost_estimate=pl.CostEstimate(flops=int(flops), bytes_accessed=int(moved), transcendentals=0),
        name=name,
    )


def dot(left, right):
    return jnp.dot(left, right, preferred_element_type=jnp.float32)


def dot_nt(left, right):
    return lax.dot_general(left, right, (((1,), (1,)), ((), ())), preferred_element_type=jnp.float32)


def collect(count, wanted, begin, slots):
    def step(index, found):
        chosen = wanted(index)

        @pl.when(chosen)
        def _():
            slots[found] = index
            begin(index, found)

        return found + chosen.astype(jnp.int32)

    return lax.fori_loop(0, count, step, jnp.int32(0))


def pack_body(first, table, maps, *refs):
    outs, slots, sem = refs[:-2], refs[-2], refs[-1]
    count = maps.shape[0]
    held = [out.shape[0] for out in outs]

    def begin(pair, slot):
        low = 0
        for out, size in zip(outs, held):
            lo, hi = low, low + size

            @pl.when((slot >= lo) & (slot < hi))
            def _(out=out, lo=lo):
                pltpu.make_async_copy(maps.at[pair], out.at[slot - lo], sem.at[slot]).start()

            low = hi

    found = collect(count, lambda p: table[SRC + p] >= 2 * first, begin, slots)

    @pl.loop(0, found)
    def _(slot):
        pltpu.make_async_copy(maps.at[0], outs[0].at[0], sem.at[slot]).wait()


def pack(table, maps, sizes, orbitals):
    count, depth, width = maps.shape
    return call(
        functools.partial(pack_body, orbitals),
        tuple(jax.ShapeDtypeStruct((s, depth, width), maps.dtype) for s in sizes),
        (VMEM,) * len(sizes),
        [SMEM, ANY],
        [pltpu.SMEM((count,), jnp.int32), pltpu.SemaphoreType.DMA((count,))],
        moved=2 * sum(sizes) * depth * width * 2,
        name="pack",
    )(table, maps)


def local_body(scale, table, shift, blocks, maps, energy, left, integ, inverse, start, early, late,
               held, map_held, sem, map_sem):
    orbitals = blocks.shape[0]
    count, _, width = maps.shape
    depth = blocks.shape[1]
    near = 8

    @pl.loop(0, orbitals)
    def _(o):
        pltpu.make_async_copy(blocks.at[o], held.at[o], sem.at[o]).start()

    @pl.loop(0, count)
    def _(p):
        pltpu.make_async_copy(maps.at[p], map_held.at[p], map_sem.at[p]).start()

    def note(entry, counts):
        soon, after = counts
        pair = entry // near
        where = table[NEAR + entry]
        is_late = where >= 2 * count

        @pl.when(is_late)
        def _():
            late[1 + after] = pair * 65536 + entry * 256 + (where - 2 * count)

        @pl.when(jnp.logical_not(is_late))
        def _():
            early[1 + soon] = pair * 65536 + entry * 256 + where

        step = is_late.astype(jnp.int32)
        return soon + 1 - step, after + step

    soon, after = lax.fori_loop(0, count * near, note, (jnp.int32(0), jnp.int32(0)))
    early[0] = soon
    late[0] = after
    for k in range(GROUP):
        early[1 + soon + k] = count * 65536
        late[1 + after + k] = count * 65536

    @pl.loop(0, count)
    def _(p):
        size = table[PNO + p]
        row = jnp.broadcast_to(energy[pl.ds(p, 1), :], (width, width))
        ids = lax.broadcasted_iota(jnp.int32, (width, width), 0)
        idt = lax.broadcasted_iota(jnp.int32, (width, width), 1)
        bottom = row + row.T + shift[p]
        inverse[p] = jnp.where((ids < size) & (idt < size), -1.0 / bottom, 0.0)

    @pl.loop(0, orbitals)
    def _(o):
        pltpu.make_async_copy(blocks.at[0], held.at[0], sem.at[o]).wait()

    @pl.loop(0, count)
    def _(p):
        pltpu.make_async_copy(maps.at[0], map_held.at[0], map_sem.at[p]).wait()
        half = dot(held[table[ONE + p]], map_held[p])
        rows = lax.broadcasted_iota(jnp.int32, (depth, width), 0)
        half = jnp.where(rows < table[LIVE + p], half, 0.0).astype(jnp.bfloat16).T
        left[p] = half
        where = table[SRC + p]

        @pl.when(where < orbitals)
        def _():
            right = dot(held[where], map_held[p]).astype(jnp.bfloat16)
            value = dot(half, right) * scale
            integ[p] = value
            start[p] = (value * inverse[p]).astype(jnp.bfloat16)


def local(table, shift, blocks, maps, energy, scale):
    orbitals, depth, wide = blocks.shape
    count, _, width = maps.shape
    entries = count * 8 + GROUP + 8
    return call(
        functools.partial(local_body, scale),
        (
            jax.ShapeDtypeStruct((count, width, depth), jnp.bfloat16),
            jax.ShapeDtypeStruct((count, width, width), jnp.float32),
            jax.ShapeDtypeStruct((count, width, width), jnp.float32),
            jax.ShapeDtypeStruct((count, width, width), jnp.bfloat16),
            jax.ShapeDtypeStruct((entries,), jnp.int32),
            jax.ShapeDtypeStruct((entries,), jnp.int32),
        ),
        (VMEM, VMEM, VMEM, VMEM, SMEM, SMEM),
        [SMEM, SMEM, ANY, ANY, VMEM],
        [
            pltpu.VMEM((orbitals, depth, wide), jnp.bfloat16),
            pltpu.VMEM((count, wide, width), jnp.bfloat16),
            pltpu.SemaphoreType.DMA((orbitals,)),
            pltpu.SemaphoreType.DMA((count,)),
        ],
        flops=2 * 1.5 * count * depth * wide * width,
        moved=(blocks.size + 2 * maps.size) * 2,
        name="local",
    )(table, shift, blocks, maps, energy)


def serve_body(low, table, blocks, maps, out, held, slots, sem):
    orbitals = blocks.shape[0]
    size = maps.shape[0]
    count = slots.shape[0]

    def begin(pair, found):
        slot = found - low

        @pl.when((slot >= 0) & (slot < size))
        def _():
            pltpu.make_async_copy(blocks.at[table[SERVE + pair]], held.at[slot], sem.at[slot]).start()

    found = collect(
        count,
        lambda p: (table[SERVE + p] >= 0) & (table[SERVE + p] < orbitals),
        begin,
        slots,
    )

    @pl.loop(0, jnp.clip(found - low, 0, size))
    def _(slot):
        pltpu.make_async_copy(blocks.at[0], held.at[0], sem.at[slot]).wait()
        out[slot] = dot(held[slot], maps[slot]).astype(jnp.bfloat16)


def serve(table, blocks, maps, low, count):
    orbitals, depth, wide = blocks.shape
    size, _, width = maps.shape
    return call(
        functools.partial(serve_body, low),
        jax.ShapeDtypeStruct((size, depth, width), jnp.bfloat16),
        VMEM,
        [SMEM, ANY, VMEM],
        [
            pltpu.VMEM((size, depth, wide), jnp.bfloat16),
            pltpu.SMEM((count,), jnp.int32),
            pltpu.SemaphoreType.DMA((size,)),
        ],
        flops=2 * size * depth * wide * width,
        moved=size * depth * (wide + 2 * width) * 2,
        name="serve",
    )(table, blocks, maps)


def beside_body(scale, orbitals, table, blocks, maps, left, inverse, integ_in, start_in, integ, start,
                blk, mp, lf, inv, val, amp, slots, sem, osem):
    del integ_in, start_in
    count = maps.shape[0]

    def copies(pair, slot):
        return (
            pltpu.make_async_copy(blocks.at[table[SRC + pair] - orbitals], blk.at[slot], sem.at[0, slot]),
            pltpu.make_async_copy(maps.at[pair], mp.at[slot], sem.at[1, slot]),
            pltpu.make_async_copy(left.at[pair], lf.at[slot], sem.at[2, slot]),
            pltpu.make_async_copy(inverse.at[pair], inv.at[slot], sem.at[3, slot]),
        )

    def begin(pair, slot):
        for copy in copies(pair, slot):
            copy.start()

    def results(pair, slot):
        return (
            pltpu.make_async_copy(val.at[slot], integ.at[pair], osem.at[0, slot]),
            pltpu.make_async_copy(amp.at[slot], start.at[pair], osem.at[1, slot]),
        )

    found = collect(
        count,
        lambda p: (table[SRC + p] >= orbitals) & (table[SRC + p] < 2 * orbitals),
        begin,
        slots,
    )

    @pl.loop(0, found)
    def _(slot):
        pair = slots[slot]
        for copy in copies(pair, slot):
            copy.wait()
        right = dot(blk[slot], mp[slot]).astype(jnp.bfloat16)
        value = dot(lf[slot], right) * scale
        val[slot] = value
        amp[slot] = (value * inv[slot]).astype(jnp.bfloat16)
        for copy in results(pair, slot):
            copy.start()

    @pl.loop(0, found)
    def _(slot):
        for copy in results(slots[slot], slot):
            copy.wait()


def beside(table, blocks, maps, left, inverse, integ, start, scale):
    orbitals, depth, wide = blocks.shape
    count, _, width = maps.shape
    return call(
        functools.partial(beside_body, scale, orbitals),
        (
            jax.ShapeDtypeStruct(integ.shape, integ.dtype),
            jax.ShapeDtypeStruct(start.shape, start.dtype),
        ),
        (ANY, ANY),
        [SMEM, ANY, ANY, ANY, ANY, ANY, ANY],
        [
            pltpu.VMEM((count, depth, wide), jnp.bfloat16),
            pltpu.VMEM((count, wide, width), jnp.bfloat16),
            pltpu.VMEM((count, width, depth), jnp.bfloat16),
            pltpu.VMEM((count, width, width), jnp.float32),
            pltpu.VMEM((count, width, width), jnp.float32),
            pltpu.VMEM((count, width, width), jnp.bfloat16),
            pltpu.SMEM((count,), jnp.int32),
            pltpu.SemaphoreType.DMA((4, count)),
            pltpu.SemaphoreType.DMA((2, count)),
        ],
        flops=count * depth * wide * width,
        moved=count * depth * wide,
        aliases={5: 0, 6: 1},
        name="beside",
    )(table, blocks, maps, left, inverse, integ, start)


def across_body(scale, orbitals, table, *refs):
    n = len(refs) - 13
    halves = refs[:n]
    left, inverse, _, _, integ, start, rt, lf, inv, val, amp, slots, sem = refs[n:]
    count = left.shape[0]

    def copies(pair, slot):
        return (
            pltpu.make_async_copy(left.at[pair], lf.at[slot], sem.at[1, slot]),
            pltpu.make_async_copy(inverse.at[pair], inv.at[slot], sem.at[2, slot]),
        )

    def begin(pair, slot):
        low = 0
        for half in halves:
            lo, hi = low, low + half.shape[0]

            @pl.when((slot >= lo) & (slot < hi))
            def _(half=half, lo=lo):
                pltpu.make_async_copy(half.at[slot - lo], rt.at[slot], sem.at[0, slot]).start()

            low = hi
        for copy in copies(pair, slot):
            copy.start()

    def results(pair, slot):
        return (
            pltpu.make_async_copy(val.at[slot], integ.at[pair], sem.at[3, slot]),
            pltpu.make_async_copy(amp.at[slot], start.at[pair], sem.at[4, slot]),
        )

    found = collect(count, lambda p: table[SRC + p] >= 2 * orbitals, begin, slots)

    @pl.loop(0, found)
    def _(slot):
        pair = slots[slot]
        pltpu.make_async_copy(halves[0].at[0], rt.at[slot], sem.at[0, slot]).wait()
        for copy in copies(pair, slot):
            copy.wait()
        value = dot(lf[slot], rt[slot]) * scale
        val[slot] = value
        amp[slot] = (value * inv[slot]).astype(jnp.bfloat16)
        for copy in results(pair, slot):
            copy.start()

    @pl.loop(0, found)
    def _(slot):
        for copy in results(slots[slot], slot):
            copy.wait()


def across(table, halves, left, inverse, integ, start, scale, orbitals):
    count, width, depth = left.shape
    n = len(halves)
    return call(
        functools.partial(across_body, scale, orbitals),
        (
            jax.ShapeDtypeStruct(integ.shape, integ.dtype),
            jax.ShapeDtypeStruct(start.shape, start.dtype),
        ),
        (ANY, ANY),
        [SMEM] + [ANY] * (n + 4),
        [
            pltpu.VMEM((count, depth, width), jnp.bfloat16),
            pltpu.VMEM((count, width, depth), jnp.bfloat16),
            pltpu.VMEM((count, width, width), jnp.float32),
            pltpu.VMEM((count, width, width), jnp.float32),
            pltpu.VMEM((count, width, width), jnp.bfloat16),
            pltpu.SMEM((count,), jnp.int32),
            pltpu.SemaphoreType.DMA((5, count)),
        ],
        flops=count * depth * width * width,
        moved=count * depth * width * 2,
        aliases={n + 3: 0, n + 4: 1},
        name="across",
    )(table, *halves, left, inverse, integ, start)


CHUNK = 4


def gather_coupling(listed, inter, tables, total, held, amps, sem, tsem):
    near = 8
    chunks = inter.shape[0] // (CHUNK * near)
    rows = CHUNK * near
    number = listed[0]
    for k, tab in enumerate(tables):
        size = tab.shape[0]
        pltpu.make_async_copy(tab, amps.at[pl.ds(k * size, size)], tsem.at[k]).start()

    @pl.loop(0, chunks)
    def _(c):
        pltpu.make_async_copy(
            inter.at[pl.ds(c * rows, rows)], held.at[pl.ds(c * rows, rows)], sem.at[c]
        ).start()

    def wait_chunk(c):
        pltpu.make_async_copy(inter.at[pl.ds(0, rows)], held.at[pl.ds(0, rows)], sem.at[c]).wait()

    def ready():
        for k, tab in enumerate(tables):
            size = tab.shape[0]
            pltpu.make_async_copy(tab, amps.at[pl.ds(k * size, size)], tsem.at[k]).wait()

    def group(g, waited):
        codes = [listed[1 + g * GROUP + k] for k in range(GROUP)]
        last = codes[0] // 65536
        for code in codes[1:]:
            last = jnp.maximum(last, jnp.minimum(code // 65536, 31))
        need = jnp.minimum(last // CHUNK + 1, chunks)

        @pl.loop(waited, need)
        def _(c):
            wait_chunk(c)

        mixed = []
        for code in codes:
            entry = (code // 256) % 256
            mixed.append(dot(held[entry], amps[code % 256]).astype(jnp.bfloat16))
        for code, part in zip(codes, mixed):
            entry = (code // 256) % 256
            total[code // 65536] += dot_nt(part, held[entry])
        return jnp.maximum(waited, need)

    return ready, group, wait_chunk, chunks, number


def early_body(listed, inter, here, beside_, integ, out, total, held, amps, sem, tsem):
    count = integ.shape[0]
    ready, group, wait_chunk, chunks, number = gather_coupling(
        listed, inter, (here, beside_), total, held, amps, sem, tsem
    )

    @pl.loop(0, count)
    def _(p):
        total[p] = jnp.zeros(total.shape[1:], jnp.float32)

    total[count] = jnp.zeros(total.shape[1:], jnp.float32)
    ready()
    waited = lax.fori_loop(0, (number + GROUP - 1) // GROUP, group, jnp.int32(0))
    pl.loop(waited, chunks)(wait_chunk)

    @pl.loop(0, count)
    def _(p):
        out[p] = integ[p] + COUPLING * total[p]


def late_body(final, listed, inter, other, so_far, inverse, *refs):
    if final:
        integ, out, energy, total, held, amps, sem, tsem = refs
    else:
        out, total, held, amps, sem, tsem = refs
    count = so_far.shape[0]
    ready, group, wait_chunk, chunks, number = gather_coupling(
        listed, inter, (other,), total, held, amps, sem, tsem
    )

    @pl.loop(0, count)
    def _(p):
        total[p] = jnp.zeros(total.shape[1:], jnp.float32)

    total[count] = jnp.zeros(total.shape[1:], jnp.float32)
    ready()
    waited = lax.fori_loop(0, (number + GROUP - 1) // GROUP, group, jnp.int32(0))
    pl.loop(waited, chunks)(wait_chunk)

    @pl.loop(0, count)
    def _(p):
        value = (so_far[p] + COUPLING * total[p]) * inverse[p]
        out[p] = value.astype(out.dtype)
        if final:
            energy[pl.ds(p, 1), :] = jnp.sum(integ[p] * value, axis=0, keepdims=True)


def coupling_scratch(count, entries, width, tables):
    chunks = count // CHUNK
    return [
        pltpu.VMEM((count + 1, width, width), jnp.float32),
        pltpu.VMEM((entries, width, width), jnp.bfloat16),
        pltpu.VMEM((tables * count, width, width), jnp.bfloat16),
        pltpu.SemaphoreType.DMA((chunks,)),
        pltpu.SemaphoreType.DMA((tables,)),
    ]


def early_part(listed, inter, here, other, integ):
    count, width, _ = integ.shape
    return call(
        early_body,
        jax.ShapeDtypeStruct(integ.shape, jnp.float32),
        VMEM,
        [SMEM, ANY, ANY, ANY, VMEM],
        coupling_scratch(count, inter.shape[0], width, 2),
        flops=2 * inter.shape[0] * width**3,
        moved=inter.size * 2,
        name="early",
    )(listed, inter, here, other, integ)


def late_part(listed, inter, other, so_far, inverse, integ=None):
    count, width, _ = so_far.shape
    final = integ is not None
    outs = jax.ShapeDtypeStruct(so_far.shape, jnp.float32 if final else jnp.bfloat16)
    args = (listed, inter, other, so_far, inverse)
    if final:
        outs = (outs, jax.ShapeDtypeStruct((count, width), jnp.float32))
        args += (integ,)
    return call(
        functools.partial(late_body, final),
        outs,
        (VMEM, VMEM) if final else VMEM,
        [SMEM, ANY, ANY] + [VMEM] * (len(args) - 3),
        coupling_scratch(count, inter.shape[0], width, 1),
        flops=inter.shape[0] * width**3,
        moved=inter.size * 2,
        name="late",
    )(*args)


def shards(
    blocks,
    pair_orbitals,
    block_sizes,
    pno_maps,
    pno_sizes,
    pno_energy,
    pair_shift,
    neighbours,
    intersections,
):
    devices = lax.axis_size("pairs")
    count, wide, width = pno_maps.shape
    orbitals, depth, _ = blocks.shape
    near = neighbours.shape[1]
    scale = 1.0 / math.sqrt(depth)
    device = lax.axis_index("pairs")
    side = 2 * (device % 2) - 1
    partner = device + side

    beside_perm = [(i, i ^ 1) for i in range(devices)]
    across_perm = []
    for i in range(1, devices - 1, 2):
        across_perm += [(i, i + 1), (i + 1, i)]
    swap_beside = lambda x: lax.ppermute(x, "pairs", beside_perm)
    swap_across = lambda x: lax.ppermute(x, "pairs", across_perm)

    def place(local_index, size):
        offset = jnp.where(local_index < 0, -1, jnp.where(local_index >= size, 1, 0))
        kind = jnp.where(offset == 0, 0, jnp.where(offset == side, 2, 1))
        return kind * size + local_index % size

    owner = jnp.arange(devices, dtype=jnp.int32)
    owner_across = owner + 2 * (owner % 2) - 1
    second = pair_orbitals[:, 1].reshape(devices, count)
    crossing = jnp.sum((second // orbitals == owner_across[:, None]).astype(jnp.int32), axis=1)
    most = jnp.max(crossing)
    branch = sum((most > s).astype(jnp.int32) for s in SLOTS[:-1])

    mine = lax.dynamic_slice_in_dim(pair_orbitals, device * count, count, 0)
    theirs = lax.dynamic_slice_in_dim(
        pair_orbitals, jnp.clip(partner, 0, devices - 1) * count, count, 0
    )
    valid = (partner >= 0) & (partner < devices)
    base = device * orbitals
    one = mine[:, 0] - base
    two = mine[:, 1] - base
    window = lax.dynamic_slice_in_dim(jnp.pad(block_sizes, (orbitals, orbitals)), base, 3 * orbitals, 0)
    hot = jnp.arange(3 * orbitals, dtype=jnp.int32)[None, :]
    size_of = lambda ids: jnp.sum(jnp.where(hot == ids[:, None] + orbitals, window[None, :], 0), axis=1)
    table = jnp.concatenate(
        [
            one,
            place(two, orbitals),
            jnp.where(valid, theirs[:, 1] - base, -1),
            jnp.minimum(size_of(one), size_of(two)),
            pno_sizes,
            place((neighbours - device * count).reshape(-1), count),
        ]
    )
    inter = intersections.reshape(count * near, width, width)

    def integrals_with(slots):
        def run(table, blocks, maps, energy, shift):
            sizes = (slots // 2, slots - slots // 2)
            packed = pack(table, maps, sizes, orbitals)
            got = [swap_across(x) for x in packed]
            blocks_beside = swap_beside(blocks)
            left, integ, inverse, start, early, late = local(table, shift, blocks, maps, energy, scale)
            halves = []
            low = 0
            for x in got:
                half = serve(table, blocks, x, low, count)
                low += x.shape[0]
                halves.append(half)
            back = [swap_across(x) for x in halves]
            integ, _ = lax.optimization_barrier((integ, halves[-1]))
            integ, start = beside(table, blocks_beside, maps, left, inverse, integ, start, scale)
            integ, start = across(table, back, left, inverse, integ, start, scale, orbitals)
            return integ, start, inverse, early, late

        return run

    integ, amps, inverse, early, late = lax.switch(
        branch,
        [integrals_with(s) for s in SLOTS],
        table,
        blocks,
        pno_maps,
        pno_energy,
        pair_shift,
    )
    for iteration in range(ITERS):
        far = swap_across(amps)
        close = swap_beside(amps)
        so_far = early_part(early, inter, amps, close, integ)
        if iteration < ITERS - 1:
            amps = late_part(late, inter, far, so_far, inverse)
        else:
            amps, energies = late_part(late, inter, far, so_far, inverse, integ)
    pair_energy = jnp.sum(energies, axis=1) / (width * width)
    return (amps, pair_energy)


def solution(mesh):
    in_specs = (
        P("pairs", None, None),
        P(),
        P(),
        P("pairs", None, None),
        P("pairs"),
        P("pairs", None),
        P("pairs"),
        P("pairs", None),
        P("pairs", None, None, None),
    )
    out_specs = (P("pairs", None, None), P("pairs"))
    return jax.shard_map(shards, mesh=mesh, in_specs=in_specs, out_specs=out_specs, check_vma=False)
```

```python
import functools
import math

import jax
import jax.numpy as jnp
from jax import lax
from jax.experimental import pallas as pl
from jax.experimental.pallas import tpu as pltpu
from jax.sharding import PartitionSpec as P

ITERS = 2
COUPLING = 0.35
SLOTS = (16, 18, 20, 24, 32)

ANY = pl.BlockSpec(memory_space=pl.ANY)
VMEM = pl.BlockSpec(memory_space=pltpu.VMEM)
SMEM = pl.BlockSpec(memory_space=pltpu.SMEM)

ONE, SRC, SERVE, LIVE, PNO, NEAR = 0, 32, 64, 96, 128, 160


def call(body, outs, out_specs, in_specs, scratch, flops=0, moved=0, limit=60, aliases=None, name=None):
    return pl.pallas_call(
        body,
        out_shape=outs,
        in_specs=in_specs,
        out_specs=out_specs,
        scratch_shapes=scratch,
        input_output_aliases=aliases or {},
        compiler_params=pltpu.CompilerParams(vmem_limit_bytes=limit * 1024 * 1024),
        cost_estimate=pl.CostEstimate(flops=int(flops), bytes_accessed=int(moved), transcendentals=0),
        name=name,
    )


def dot(left, right):
    return jnp.dot(left, right, preferred_element_type=jnp.float32)


def dot_nt(left, right):
    return lax.dot_general(left, right, (((1,), (1,)), ((), ())), preferred_element_type=jnp.float32)


def dot_tn_nt(left, right):
    return lax.dot_general(left, right, (((0,), (1,)), ((), ())), preferred_element_type=jnp.float32)


def collect(count, wanted, begin, slots):
    def step(index, found):
        chosen = wanted(index)

        @pl.when(chosen)
        def _():
            slots[found] = index
            begin(index, found)

        return found + chosen.astype(jnp.int32)

    return lax.fori_loop(0, count, step, jnp.int32(0))


def pack_body(first, table, maps, *refs):
    outs, slots, sem = refs[:-2], refs[-2], refs[-1]
    count = maps.shape[0]
    held = [out.shape[0] for out in outs]

    def begin(pair, slot):
        low = 0
        for out, size in zip(outs, held):
            lo, hi = low, low + size

            @pl.when((slot >= lo) & (slot < hi))
            def _(out=out, lo=lo):
                pltpu.make_async_copy(maps.at[pair], out.at[slot - lo], sem.at[slot]).start()

            low = hi

    found = collect(count, lambda p: table[SRC + p] >= 2 * first, begin, slots)

    @pl.loop(0, found)
    def _(slot):
        pltpu.make_async_copy(maps.at[0], outs[0].at[0], sem.at[slot]).wait()


def pack(table, maps, sizes, orbitals):
    count, depth, width = maps.shape
    return call(
        functools.partial(pack_body, orbitals),
        tuple(jax.ShapeDtypeStruct((s, depth, width), maps.dtype) for s in sizes),
        (VMEM,) * len(sizes),
        [SMEM, ANY],
        [pltpu.SMEM((count,), jnp.int32), pltpu.SemaphoreType.DMA((count,))],
        moved=2 * sum(sizes) * depth * width * 2,
        limit=8,
        name="pack",
    )(table, maps)


def local_body(scale, table, shift, blocks, maps, energy, left, integ, inverse, start, early, late,
               held, map_held, sem, map_sem):
    orbitals = blocks.shape[0]
    count, _, width = maps.shape
    depth = blocks.shape[1]
    near = 8

    @pl.loop(0, orbitals)
    def _(o):
        pltpu.make_async_copy(blocks.at[o], held.at[o], sem.at[o]).start()

    @pl.loop(0, count)
    def _(p):
        pltpu.make_async_copy(maps.at[p], map_held.at[p], map_sem.at[p]).start()

    def note(entry, counts):
        soon, after = counts
        where = table[NEAR + entry]
        is_late = where >= 2 * count
        code = (entry // near) * 65536 + entry * 256 + where

        @pl.when(is_late)
        def _():
            late[1 + after] = code - 2 * count

        @pl.when(jnp.logical_not(is_late))
        def _():
            early[1 + soon] = code

        step = is_late.astype(jnp.int32)
        return soon + 1 - step, after + step

    def note_pair(pair, counts):
        for k in range(near):
            counts = note(pair * near + k, counts)
        soon, after = counts
        spare = pair * 65536 + pair * near * 256

        @pl.when(soon % 2 == 1)
        def _():
            early[1 + soon] = spare + 2 * count

        @pl.when(after % 2 == 1)
        def _():
            late[1 + after] = spare + count

        return soon + soon % 2, after + after % 2

    soon, after = lax.fori_loop(0, count, note_pair, (jnp.int32(0), jnp.int32(0)))
    early[0] = soon // 2
    late[0] = after // 2

    @pl.loop(0, 6 * UNIT)
    def _(k):
        early[1 + soon + k] = count * 65536 + 2 * count
        late[1 + after + k] = count * 65536 + count

    @pl.loop(0, count)
    def _(p):
        size = table[PNO + p]
        row = jnp.broadcast_to(energy[pl.ds(p, 1), :], (width, width))
        ids = lax.broadcasted_iota(jnp.int32, (width, width), 0)
        idt = lax.broadcasted_iota(jnp.int32, (width, width), 1)
        bottom = row + row.T + shift[p]
        inverse[p] = jnp.where((ids < size) & (idt < size), -1.0 / bottom, 0.0)

    @pl.loop(0, orbitals)
    def _(o):
        pltpu.make_async_copy(blocks.at[0], held.at[0], sem.at[o]).wait()

    columns = lax.broadcasted_iota(jnp.int32, (width, depth), 1)

    @pl.loop(0, count // 2)
    def _(duo):
        for p in (2 * duo, 2 * duo + 1):
            pltpu.make_async_copy(maps.at[0], map_held.at[0], map_sem.at[p]).wait()
            half = dot_tn_nt(map_held[p], held[table[ONE + p]])
            left[p] = jnp.where(columns < table[LIVE + p], half, 0.0).astype(jnp.bfloat16)

    @pl.loop(0, count)
    def _(p):
        where = table[SRC + p]

        @pl.when(where < orbitals)
        def _():
            right = dot(held[where], map_held[p]).astype(jnp.bfloat16)
            value = dot(left[p], right) * scale
            integ[p] = value
            start[p] = (value * inverse[p]).astype(jnp.bfloat16)


def local(table, shift, blocks, maps, energy, scale):
    orbitals, depth, wide = blocks.shape
    count, _, width = maps.shape
    entries = count * 8 + 6 * UNIT + 8
    return call(
        functools.partial(local_body, scale),
        (
            jax.ShapeDtypeStruct((count, width, depth), jnp.bfloat16),
            jax.ShapeDtypeStruct((count, width, width), jnp.float32),
            jax.ShapeDtypeStruct((count, width, width), jnp.float32),
            jax.ShapeDtypeStruct((count, width, width), jnp.bfloat16),
            jax.ShapeDtypeStruct((entries,), jnp.int32),
            jax.ShapeDtypeStruct((entries,), jnp.int32),
        ),
        (VMEM, VMEM, VMEM, VMEM, SMEM, SMEM),
        [SMEM, SMEM, ANY, ANY, VMEM],
        [
            pltpu.VMEM((orbitals, depth, wide), jnp.bfloat16),
            pltpu.VMEM((count, wide, width), jnp.bfloat16),
            pltpu.SemaphoreType.DMA((orbitals,)),
            pltpu.SemaphoreType.DMA((count,)),
        ],
        flops=2 * 1.5 * count * depth * wide * width,
        moved=(blocks.size + 2 * maps.size) * 2,
        limit=30,
        name="local",
    )(table, shift, blocks, maps, energy)


def serve_body(low, table, blocks, maps, out, held, slots, sem):
    orbitals = blocks.shape[0]
    size = maps.shape[0]
    count = slots.shape[0]

    def begin(pair, found):
        slot = found - low

        @pl.when((slot >= 0) & (slot < size))
        def _():
            pltpu.make_async_copy(blocks.at[table[SERVE + pair]], held.at[slot], sem.at[slot]).start()

    found = collect(
        count,
        lambda p: (table[SERVE + p] >= 0) & (table[SERVE + p] < orbitals),
        begin,
        slots,
    )

    @pl.loop(0, jnp.clip(found - low, 0, size))
    def _(slot):
        pltpu.make_async_copy(blocks.at[0], held.at[0], sem.at[slot]).wait()
        out[slot] = dot(held[slot], maps[slot]).astype(jnp.bfloat16)


def serve(table, blocks, maps, low, count):
    orbitals, depth, wide = blocks.shape
    size, _, width = maps.shape
    return call(
        functools.partial(serve_body, low),
        jax.ShapeDtypeStruct((size, depth, width), jnp.bfloat16),
        VMEM,
        [SMEM, ANY, VMEM],
        [
            pltpu.VMEM((size, depth, wide), jnp.bfloat16),
            pltpu.SMEM((count,), jnp.int32),
            pltpu.SemaphoreType.DMA((size,)),
        ],
        flops=2 * size * depth * wide * width,
        moved=size * depth * (wide + 2 * width) * 2,
        limit=3 * size // 4 + 4,
        name="serve",
    )(table, blocks, maps)


def beside_body(scale, orbitals, table, blocks, maps, left, inverse, integ_in, start_in, integ, start,
                blk, mp, lf, inv, val, amp, slots, sem, osem):
    del integ_in, start_in
    count = maps.shape[0]

    def copies(pair, slot):
        return (
            pltpu.make_async_copy(blocks.at[table[SRC + pair] - orbitals], blk.at[slot], sem.at[0, slot]),
            pltpu.make_async_copy(maps.at[pair], mp.at[slot], sem.at[1, slot]),
            pltpu.make_async_copy(left.at[pair], lf.at[slot], sem.at[2, slot]),
            pltpu.make_async_copy(inverse.at[pair], inv.at[slot], sem.at[3, slot]),
        )

    def begin(pair, slot):
        for copy in copies(pair, slot):
            copy.start()

    def results(pair, slot):
        return (
            pltpu.make_async_copy(val.at[slot], integ.at[pair], osem.at[0, slot]),
            pltpu.make_async_copy(amp.at[slot], start.at[pair], osem.at[1, slot]),
        )

    found = collect(
        count,
        lambda p: (table[SRC + p] >= orbitals) & (table[SRC + p] < 2 * orbitals),
        begin,
        slots,
    )

    @pl.loop(0, found)
    def _(slot):
        pair = slots[slot]
        for copy in copies(pair, slot):
            copy.wait()
        right = dot(blk[slot], mp[slot]).astype(jnp.bfloat16)
        value = dot(lf[slot], right) * scale
        val[slot] = value
        amp[slot] = (value * inv[slot]).astype(jnp.bfloat16)
        for copy in results(pair, slot):
            copy.start()

    @pl.loop(0, found)
    def _(slot):
        for copy in results(slots[slot], slot):
            copy.wait()


def beside(table, blocks, maps, left, inverse, integ, start, scale):
    orbitals, depth, wide = blocks.shape
    count, _, width = maps.shape
    return call(
        functools.partial(beside_body, scale, orbitals),
        (
            jax.ShapeDtypeStruct(integ.shape, integ.dtype),
            jax.ShapeDtypeStruct(start.shape, start.dtype),
        ),
        (ANY, ANY),
        [SMEM, ANY, ANY, ANY, ANY, ANY, ANY],
        [
            pltpu.VMEM((count, depth, wide), jnp.bfloat16),
            pltpu.VMEM((count, wide, width), jnp.bfloat16),
            pltpu.VMEM((count, width, depth), jnp.bfloat16),
            pltpu.VMEM((count, width, width), jnp.float32),
            pltpu.VMEM((count, width, width), jnp.float32),
            pltpu.VMEM((count, width, width), jnp.bfloat16),
            pltpu.SMEM((count,), jnp.int32),
            pltpu.SemaphoreType.DMA((4, count)),
            pltpu.SemaphoreType.DMA((2, count)),
        ],
        flops=count * depth * wide * width,
        moved=count * depth * wide,
        aliases={5: 0, 6: 1},
        limit=34,
        name="beside",
    )(table, blocks, maps, left, inverse, integ, start)


def across_body(scale, orbitals, table, *refs):
    n = len(refs) - 13
    halves = refs[:n]
    left, inverse, _, _, integ, start, rt, lf, inv, val, amp, slots, sem = refs[n:]
    count = left.shape[0]

    def copies(pair, slot):
        return (
            pltpu.make_async_copy(left.at[pair], lf.at[slot], sem.at[1, slot]),
            pltpu.make_async_copy(inverse.at[pair], inv.at[slot], sem.at[2, slot]),
        )

    def begin(pair, slot):
        low = 0
        for half in halves:
            lo, hi = low, low + half.shape[0]

            @pl.when((slot >= lo) & (slot < hi))
            def _(half=half, lo=lo):
                pltpu.make_async_copy(half.at[slot - lo], rt.at[slot], sem.at[0, slot]).start()

            low = hi
        for copy in copies(pair, slot):
            copy.start()

    def results(pair, slot):
        return (
            pltpu.make_async_copy(val.at[slot], integ.at[pair], sem.at[3, slot]),
            pltpu.make_async_copy(amp.at[slot], start.at[pair], sem.at[4, slot]),
        )

    found = collect(count, lambda p: table[SRC + p] >= 2 * orbitals, begin, slots)

    @pl.loop(0, found)
    def _(slot):
        pair = slots[slot]
        pltpu.make_async_copy(halves[0].at[0], rt.at[slot], sem.at[0, slot]).wait()
        for copy in copies(pair, slot):
            copy.wait()
        value = dot(lf[slot], rt[slot]) * scale
        val[slot] = value
        amp[slot] = (value * inv[slot]).astype(jnp.bfloat16)
        for copy in results(pair, slot):
            copy.start()

    @pl.loop(0, found)
    def _(slot):
        for copy in results(slots[slot], slot):
            copy.wait()


def across(table, halves, left, inverse, integ, start, scale, orbitals):
    count, width, depth = left.shape
    n = len(halves)
    return call(
        functools.partial(across_body, scale, orbitals),
        (
            jax.ShapeDtypeStruct(integ.shape, integ.dtype),
            jax.ShapeDtypeStruct(start.shape, start.dtype),
        ),
        (ANY, ANY),
        [SMEM] + [ANY] * (n + 4),
        [
            pltpu.VMEM((count, depth, width), jnp.bfloat16),
            pltpu.VMEM((count, width, depth), jnp.bfloat16),
            pltpu.VMEM((count, width, width), jnp.float32),
            pltpu.VMEM((count, width, width), jnp.float32),
            pltpu.VMEM((count, width, width), jnp.bfloat16),
            pltpu.SMEM((count,), jnp.int32),
            pltpu.SemaphoreType.DMA((5, count)),
        ],
        flops=count * depth * width * width,
        moved=count * depth * width * 2,
        aliases={n + 3: 0, n + 4: 1},
        limit=20,
        name="across",
    )(table, *halves, left, inverse, integ, start)


UNIT = 4


def couple(listed, inter, tables, total, amps, ahead, behind):
    count = total.shape[0] - 1
    width = total.shape[1]
    low = 0
    for table in tables:
        amps[pl.ds(low, table.shape[0])] = table[...]
        low += table.shape[0]
    amps[low] = jnp.zeros(amps.shape[1:], amps.dtype)

    @pl.loop(0, count + 1)
    def _(p):
        total[p] = jnp.zeros(total.shape[1:], jnp.float32)

    def codes(group):
        for k in range(UNIT):
            place = 1 + (group * UNIT + k) * 2
            one, two = listed[place], listed[place + 1]
            yield k, one // 65536, (one // 256) % 256, one % 256, (two // 256) % 256, two % 256

    def first(group, mixed):
        for k, _, one, amp_one, two, amp_two in codes(group):
            mixed[k, :, 0:width] = dot(inter[one], amps[amp_one]).astype(jnp.bfloat16)
            mixed[k, :, width : 2 * width] = dot(inter[two], amps[amp_two]).astype(jnp.bfloat16)

    def second(group, mixed):
        for k, pair, one, _, two, _ in codes(group):
            total[pair] += dot_nt(mixed[k], jnp.concatenate([inter[one], inter[two]], axis=1))

    first(0, ahead)

    @pl.loop(0, (listed[0] + 2 * UNIT - 1) // (2 * UNIT))
    def _(step):
        first(2 * step + 1, behind)
        second(2 * step, ahead)
        first(2 * step + 2, ahead)
        second(2 * step + 1, behind)


def early_body(listed, inter, here, near_by, integ, out, total, *scratch):
    couple(listed, inter, (here, near_by), total, *scratch)

    @pl.loop(0, integ.shape[0])
    def _(p):
        out[p] = integ[p] + COUPLING * total[p]


def late_body(listed, inter, other, so_far, inverse, out, total, *scratch):
    couple(listed, inter, (other,), total, *scratch)

    @pl.loop(0, so_far.shape[0])
    def _(p):
        out[p] = ((so_far[p] + COUPLING * total[p]) * inverse[p]).astype(out.dtype)


def last_body(listed, inter, other, so_far, inverse, integ, out, energy, rows, total, *scratch):
    couple(listed, inter, (other,), total, *scratch)
    width = total.shape[1]

    @pl.loop(0, so_far.shape[0])
    def _(p):
        value = (so_far[p] + COUPLING * total[p]) * inverse[p]
        out[p] = value
        rows[pl.ds(p, 1), :] = jnp.sum(integ[p] * value, axis=0, keepdims=True)

    sums = lax.dot_general(
        jnp.ones((8, width), jnp.float32),
        rows[...],
        (((1,), (1,)), ((), ())),
        precision=lax.Precision.HIGHEST,
        preferred_element_type=jnp.float32,
    )
    energy[...] = sums[0:1, :] * (1.0 / (width * width))


def coupling_scratch(count, width, tables):
    return [
        pltpu.VMEM((count + 1, width, width), jnp.float32),
        pltpu.VMEM((tables * count + 1, width, width), jnp.bfloat16),
        pltpu.VMEM((UNIT, width, 2 * width), jnp.bfloat16),
        pltpu.VMEM((UNIT, width, 2 * width), jnp.bfloat16),
    ]


def early_part(listed, inter, here, other, integ):
    count, width, _ = integ.shape
    return call(
        early_body,
        jax.ShapeDtypeStruct(integ.shape, jnp.float32),
        VMEM,
        [SMEM, VMEM, VMEM, VMEM, VMEM],
        coupling_scratch(count, width, 2),
        flops=2 * inter.shape[0] * width**3,
        moved=inter.size * 2,
        limit=24,
        name="early",
    )(listed, inter, here, other, integ)


def late_part(listed, inter, other, so_far, inverse):
    count, width, _ = so_far.shape
    return call(
        late_body,
        jax.ShapeDtypeStruct(so_far.shape, jnp.bfloat16),
        VMEM,
        [SMEM, VMEM, VMEM, VMEM, VMEM],
        coupling_scratch(count, width, 1),
        flops=inter.shape[0] * width**3,
        moved=inter.size * 2,
        limit=24,
        name="late",
    )(listed, inter, other, so_far, inverse)


def last_part(listed, inter, other, so_far, inverse, integ):
    count, width, _ = so_far.shape
    return call(
        last_body,
        (
            jax.ShapeDtypeStruct(so_far.shape, jnp.float32),
            jax.ShapeDtypeStruct((1, count), jnp.float32),
        ),
        (VMEM, VMEM),
        [SMEM, VMEM, VMEM, VMEM, VMEM, VMEM],
        [pltpu.VMEM((count, width), jnp.float32)] + coupling_scratch(count, width, 1),
        flops=inter.shape[0] * width**3,
        moved=inter.size * 2,
        limit=24,
        name="last",
    )(listed, inter, other, so_far, inverse, integ)


def shards(
    blocks,
    pair_orbitals,
    block_sizes,
    pno_maps,
    pno_sizes,
    pno_energy,
    pair_shift,
    neighbours,
    intersections,
):
    devices = lax.axis_size("pairs")
    count, wide, width = pno_maps.shape
    orbitals, depth, _ = blocks.shape
    near = neighbours.shape[1]
    scale = 1.0 / math.sqrt(depth)
    device = lax.axis_index("pairs")
    side = 2 * (device % 2) - 1
    partner = device + side

    beside_perm = [(i, i ^ 1) for i in range(devices)]
    across_perm = []
    for i in range(1, devices - 1, 2):
        across_perm += [(i, i + 1), (i + 1, i)]
    swap_beside = lambda x: lax.ppermute(x, "pairs", beside_perm)
    swap_across = lambda x: lax.ppermute(x, "pairs", across_perm)

    def place(local_index, size):
        offset = jnp.where(local_index < 0, -1, jnp.where(local_index >= size, 1, 0))
        kind = jnp.where(offset == 0, 0, jnp.where(offset == side, 2, 1))
        return kind * size + local_index % size

    owner = jnp.arange(devices, dtype=jnp.int32)
    owner_across = owner + 2 * (owner % 2) - 1
    second = pair_orbitals[:, 1].reshape(devices, count)
    crossing = jnp.sum((second // orbitals == owner_across[:, None]).astype(jnp.int32), axis=1)
    most = jnp.max(crossing)
    branch = sum((most > s).astype(jnp.int32) for s in SLOTS[:-1])

    mine = lax.dynamic_slice_in_dim(pair_orbitals, device * count, count, 0)
    theirs = lax.dynamic_slice_in_dim(
        pair_orbitals, jnp.clip(partner, 0, devices - 1) * count, count, 0
    )
    valid = (partner >= 0) & (partner < devices)
    base = device * orbitals
    one = mine[:, 0] - base
    two = mine[:, 1] - base
    window = lax.dynamic_slice_in_dim(jnp.pad(block_sizes, (orbitals, orbitals)), base, 3 * orbitals, 0)
    hot = jnp.arange(3 * orbitals, dtype=jnp.int32)[None, :]
    size_of = lambda ids: jnp.sum(jnp.where(hot == ids[:, None] + orbitals, window[None, :], 0), axis=1)
    table = jnp.concatenate(
        [
            one,
            place(two, orbitals),
            jnp.where(valid, theirs[:, 1] - base, -1),
            jnp.minimum(size_of(one), size_of(two)),
            pno_sizes,
            place((neighbours - device * count).reshape(-1), count),
        ]
    )
    inter = intersections.reshape(count * near, width, width)

    def integrals_with(slots):
        def run(table, blocks, maps, energy, shift):
            sizes = (slots // 2, slots - slots // 2)
            packed = pack(table, maps, sizes, orbitals)
            got = [swap_across(x) for x in packed]
            blocks_beside = swap_beside(blocks)
            left, integ, inverse, start, early, late = local(table, shift, blocks, maps, energy, scale)
            halves = []
            low = 0
            table, _ = lax.optimization_barrier((table, late))
            for x in got:
                half = serve(table, blocks, x, low, count)
                low += x.shape[0]
                halves.append(half)
            back = [swap_across(x) for x in halves]
            integ, _ = lax.optimization_barrier((integ, halves[-1]))
            integ, start = beside(table, blocks_beside, maps, left, inverse, integ, start, scale)
            integ, start = across(table, back, left, inverse, integ, start, scale, orbitals)
            return integ, start, inverse, early, late

        return run

    integ, amps, inverse, early, late = lax.switch(
        branch,
        [integrals_with(s) for s in SLOTS],
        table,
        blocks,
        pno_maps,
        pno_energy,
        pair_shift,
    )
    for iteration in range(ITERS):
        far = swap_across(amps)
        close = swap_beside(amps)
        so_far = early_part(early, inter, amps, close, integ)
        if iteration < ITERS - 1:
            amps = late_part(late, inter, far, so_far, inverse)
        else:
            amps, energies = last_part(late, inter, far, so_far, inverse, integ)
    return (amps, energies.reshape(count))


def solution(mesh):
    in_specs = (
        P("pairs", None, None),
        P(),
        P(),
        P("pairs", None, None),
        P("pairs"),
        P("pairs", None),
        P("pairs"),
        P("pairs", None),
        P("pairs", None, None, None),
    )
    out_specs = (P("pairs", None, None), P("pairs"))
    return jax.shard_map(shards, mesh=mesh, in_specs=in_specs, out_specs=out_specs, check_vma=False)
```

```python
import functools
import math

import jax
import jax.numpy as jnp
from jax import lax
from jax.experimental import pallas as pl
from jax.experimental.pallas import tpu as pltpu
from jax.sharding import PartitionSpec as P

ITERS = 2
COUPLING = 0.35
SLOTS = (16, 18, 20, 24, 32)

ANY = pl.BlockSpec(memory_space=pl.ANY)
VMEM = pl.BlockSpec(memory_space=pltpu.VMEM)
SMEM = pl.BlockSpec(memory_space=pltpu.SMEM)

ONE, SRC, SERVE, LIVE = 0, 32, 64, 96


def call(body, outs, out_specs, in_specs, scratch, flops=0, moved=0, limit=60, aliases=None, name=None):
    return pl.pallas_call(
        body,
        out_shape=outs,
        in_specs=in_specs,
        out_specs=out_specs,
        scratch_shapes=scratch,
        input_output_aliases=aliases or {},
        compiler_params=pltpu.CompilerParams(vmem_limit_bytes=limit * 1024 * 1024),
        cost_estimate=pl.CostEstimate(flops=int(flops), bytes_accessed=int(moved), transcendentals=0),
        name=name,
    )


def dot(left, right):
    return jnp.dot(left, right, preferred_element_type=jnp.float32)


def dot_nt(left, right):
    return lax.dot_general(left, right, (((1,), (1,)), ((), ())), preferred_element_type=jnp.float32)


def dot_tn_nt(left, right):
    return lax.dot_general(left, right, (((0,), (1,)), ((), ())), preferred_element_type=jnp.float32)


def collect(count, wanted, slots, begin=None):
    def step(index, found):
        chosen = wanted(index)
        slots[found] = index
        if begin is not None:
            pl.when(chosen)(lambda: begin(index, found))
        return found + chosen.astype(jnp.int32)

    return lax.fori_loop(0, count, step, jnp.int32(0))


def by_twos(number, work, store):
    @pl.loop(0, (number + 1) // 2)
    def _(step):
        both = (2 * step, jnp.minimum(2 * step + 1, number - 1))
        done = [work(k) for k in both]
        for k, values in zip(both, done):
            store(k, values)


def plan_body(orbitals, everyone, pairs_hbm, sizes, table, branch, mine, theirs, sem):
    count = mine.shape[1] // 4
    lanes = mine.shape[1]
    devices = everyone.shape[1] // count
    device = lax.axis_index("pairs")
    side = 2 * (device % 2) - 1
    partner = device + side
    valid = (partner >= 0) & (partner < devices)
    near_by = jnp.clip(partner, 0, devices - 1)

    def fetch(who, place, k):
        start = pl.multiple_of(who // 4 * lanes, lanes)
        return pltpu.make_async_copy(pairs_hbm.at[:, pl.ds(start, lanes)], place, sem.at[k])

    copies = (fetch(device, mine, 0), fetch(near_by, theirs, 1))
    for copy in copies:
        copy.start()

    groups = devices * count // lanes
    second = jnp.concatenate([everyone[1:2, g * lanes : (g + 1) * lanes] for g in range(groups)], axis=0)
    row = lax.broadcasted_iota(jnp.int32, (groups, lanes), 0)
    lane = lax.broadcasted_iota(jnp.int32, (groups, lanes), 1)
    owner = row * (lanes // count) + lane // count
    crossing = jnp.where(second // orbitals == owner + 2 * (owner % 2) - 1, 1.0, 0.0)
    from_lane = lax.broadcasted_iota(jnp.int32, (lanes, lanes), 0) // count
    to_lane = lax.broadcasted_iota(jnp.int32, (lanes, lanes), 1)
    together = jnp.where(from_lane == to_lane, 1.0, 0.0).astype(jnp.bfloat16)
    most = jnp.max(dot(crossing.astype(jnp.bfloat16), together)).astype(jnp.int32)
    branch[0] = sum((most > s).astype(jnp.int32) for s in SLOTS[:-1])

    for copy in copies:
        copy.wait()
    base = device * orbitals
    here = device % 4 * count
    there = near_by % 4 * count

    @pl.loop(0, count)
    def _(p):
        first = mine[0, here + p]
        second = mine[1, here + p]
        local = second - base
        offset = (local >= orbitals).astype(jnp.int32) - (local < 0).astype(jnp.int32)
        kind = jnp.where(offset == 0, 0, jnp.where(offset == side, 2, 1))
        table[ONE + p] = first - base
        table[SRC + p] = kind * orbitals + local - offset * orbitals
        table[SERVE + p] = jnp.where(valid, theirs[1, there + p] - base, -1)
        table[LIVE + p] = jnp.minimum(sizes[first], sizes[second])


def plan(pair_orbitals, block_sizes, orbitals):
    turned = pair_orbitals.T
    return call(
        functools.partial(plan_body, orbitals),
        (jax.ShapeDtypeStruct((128,), jnp.int32), jax.ShapeDtypeStruct((1,), jnp.int32)),
        (SMEM, SMEM),
        [VMEM, ANY, SMEM],
        [pltpu.SMEM((2, 128), jnp.int32), pltpu.SMEM((2, 128), jnp.int32), pltpu.SemaphoreType.DMA((2,))],
        moved=turned.size * 8,
        limit=4,
        name="plan",
    )(turned, turned, block_sizes)


def pack_body(orbitals, table, maps, *refs):
    outs, slots, sem = refs[:-2], refs[-2], refs[-1]
    count = maps.shape[0]

    def begin(pair, slot):
        low = 0
        for out in outs:
            lo, hi = low, low + out.shape[0]

            @pl.when((slot >= lo) & (slot < hi))
            def _(out=out, lo=lo):
                pltpu.make_async_copy(maps.at[pair], out.at[slot - lo], sem.at[slot]).start()

            low = hi

    found = collect(count, lambda p: table[SRC + p] >= 2 * orbitals, slots, begin)

    @pl.loop(0, found)
    def _(slot):
        pltpu.make_async_copy(maps.at[0], outs[0].at[0], sem.at[slot]).wait()


def pack(table, maps, sizes, orbitals):
    count, depth, width = maps.shape
    return call(
        functools.partial(pack_body, orbitals),
        tuple(jax.ShapeDtypeStruct((s, depth, width), maps.dtype) for s in sizes),
        (VMEM,) * len(sizes),
        [SMEM, ANY],
        [pltpu.SMEM((count + 1,), jnp.int32), pltpu.SemaphoreType.DMA((count,))],
        moved=2 * sum(sizes) * depth * width * 2,
        limit=8,
        name="pack",
    )(table, maps)


def left_body(table, blocks, maps, left):
    count, width, depth = left.shape
    columns = lax.broadcasted_iota(jnp.int32, (width, depth), 1)

    def work(p):
        half = dot_tn_nt(maps[p], blocks[table[ONE + p]])
        return jnp.where(columns < table[LIVE + p], half, 0.0).astype(jnp.bfloat16)

    def store(p, half):
        left[p] = half

    by_twos(count, work, store)


def left_part(table, blocks, maps):
    orbitals, depth, wide = blocks.shape
    count, _, width = maps.shape
    return call(
        left_body,
        jax.ShapeDtypeStruct((count, width, depth), jnp.bfloat16),
        VMEM,
        [SMEM, VMEM, VMEM],
        [],
        flops=2 * count * depth * wide * width,
        moved=blocks.size * 2,
        limit=20,
        name="left",
    )(table, blocks, maps)


def own_body(scale, orbitals, table, sizes, shift, near_pairs, blocks, maps, energy, left,
             integ, start, inverse, early, late, slots):
    count, width, _ = left.shape
    near = near_pairs.shape[0]
    device = lax.axis_index("pairs")
    side = 2 * (device % 2) - 1
    ids = lax.broadcasted_iota(jnp.int32, (width, width), 0)
    across_ids = lax.broadcasted_iota(jnp.int32, (width, width), 1)

    def pair_step(pair, counts):
        soon, after = counts
        for k in range(near):
            entry = pair * near + k
            local = near_pairs[k, pair] - device * count
            offset = (local >= count).astype(jnp.int32) - (local < 0).astype(jnp.int32)
            is_late = (offset == side).astype(jnp.int32)
            code = pair * 65536 + entry * 256 + local - offset * count
            early[1 + soon] = code + jnp.where(offset == 0, 0, count)
            late[1 + after] = code
            soon = soon + 1 - is_late
            after = after + is_late
        spare = pair * 65536 + pair * near * 256
        early[1 + soon] = spare + 2 * count
        late[1 + after] = spare + count
        row = jnp.broadcast_to(energy[pl.ds(pair, 1), :], (width, width))
        bottom = row + row.T + shift[pair]
        size = sizes[pair]
        inverse[pair] = jnp.where((ids < size) & (across_ids < size), -1.0 / bottom, 0.0)
        return soon + soon % 2, after + after % 2

    soon, after = lax.fori_loop(0, count, pair_step, (jnp.int32(0), jnp.int32(0)))
    early[0] = soon // 2
    late[0] = after // 2

    @pl.loop(0, 6 * UNIT)
    def _(k):
        early[1 + soon + k] = count * 65536 + 2 * count
        late[1 + after + k] = count * 65536 + count

    found = collect(count, lambda p: table[SRC + p] < orbitals, slots)

    def work(slot):
        pair = slots[slot]
        right = dot(blocks[table[SRC + pair]], maps[pair]).astype(jnp.bfloat16)
        return dot(left[pair], right) * scale

    def store(slot, value):
        pair = slots[slot]
        integ[pair] = value
        start[pair] = (value * inverse[pair]).astype(jnp.bfloat16)

    by_twos(found, work, store)


def own_part(table, sizes, shift, near_pairs, blocks, maps, energy, left, scale):
    orbitals = blocks.shape[0]
    count, width, depth = left.shape
    entries = near_pairs.size + 6 * UNIT + 8
    return call(
        functools.partial(own_body, scale, orbitals),
        (
            jax.ShapeDtypeStruct((count, width, width), jnp.float32),
            jax.ShapeDtypeStruct((count, width, width), jnp.bfloat16),
            jax.ShapeDtypeStruct((count, width, width), jnp.float32),
            jax.ShapeDtypeStruct((entries,), jnp.int32),
            jax.ShapeDtypeStruct((entries,), jnp.int32),
        ),
        (VMEM, VMEM, VMEM, SMEM, SMEM),
        [SMEM, SMEM, SMEM, SMEM, VMEM, VMEM, VMEM, VMEM],
        [pltpu.SMEM((count + 1,), jnp.int32)],
        flops=count * depth * depth * width,
        moved=blocks.size * 2,
        limit=28,
        name="own",
    )(table, sizes, shift, near_pairs, blocks, maps, energy, left)


def serve_body(low, table, blocks, maps, out, slots):
    orbitals = blocks.shape[0]
    size = maps.shape[0]
    found = collect(
        slots.shape[0] - 1,
        lambda p: (table[SERVE + p] >= 0) & (table[SERVE + p] < orbitals),
        slots,
    )

    def work(slot):
        return dot(blocks[table[SERVE + slots[low + slot]]], maps[slot]).astype(jnp.bfloat16)

    def store(slot, half):
        out[slot] = half

    by_twos(jnp.clip(found - low, 0, size), work, store)


def serve(table, blocks, maps, low, count):
    orbitals, depth, wide = blocks.shape
    size, _, width = maps.shape
    return call(
        functools.partial(serve_body, low),
        jax.ShapeDtypeStruct((size, depth, width), jnp.bfloat16),
        VMEM,
        [SMEM, VMEM, VMEM],
        [pltpu.SMEM((count + 1,), jnp.int32)],
        flops=2 * size * depth * wide * width,
        moved=size * depth * (wide + 2 * width) * 2,
        limit=20,
        name="serve",
    )(table, blocks, maps)


def carry_over(integ_in, start_in, integ, start):
    @pl.loop(0, integ.shape[0])
    def _(p):
        integ[p] = integ_in[p]
        start[p] = start_in[p]


def beside_body(scale, table, blocks, maps, left, inverse, integ_in, start_in, integ, start, slots):
    carry_over(integ_in, start_in, integ, start)
    orbitals = blocks.shape[0]
    found = collect(
        left.shape[0],
        lambda p: (table[SRC + p] >= orbitals) & (table[SRC + p] < 2 * orbitals),
        slots,
    )

    def work(slot):
        pair = slots[slot]
        right = dot(blocks[table[SRC + pair] - orbitals], maps[pair]).astype(jnp.bfloat16)
        return dot(left[pair], right) * scale

    def store(slot, value):
        pair = slots[slot]
        integ[pair] = value
        start[pair] = (value * inverse[pair]).astype(jnp.bfloat16)

    by_twos(found, work, store)


def across_body(scale, orbitals, table, *refs):
    n = len(refs) - 8
    halves = refs[:n]
    left, inverse, integ_in, start_in, integ, start, joined, slots = refs[n:]
    carry_over(integ_in, start_in, integ, start)
    low = 0
    for half in halves:
        joined[pl.ds(low, half.shape[0])] = half[...]
        low += half.shape[0]
    found = collect(left.shape[0], lambda p: table[SRC + p] >= 2 * orbitals, slots)

    def work(slot):
        return dot(left[slots[slot]], joined[slot]) * scale

    def store(slot, value):
        pair = slots[slot]
        integ[pair] = value
        start[pair] = (value * inverse[pair]).astype(jnp.bfloat16)

    by_twos(found, work, store)


def integrals_part(body, table, operands, left, inverse, integ, start, scratch, limit, name):
    count, width, depth = left.shape
    n = len(operands)
    return call(
        body,
        (
            jax.ShapeDtypeStruct(integ.shape, integ.dtype),
            jax.ShapeDtypeStruct(start.shape, start.dtype),
        ),
        (VMEM, VMEM),
        [SMEM] + [VMEM] * (n + 4),
        scratch + [pltpu.SMEM((count + 1,), jnp.int32)],
        flops=count * depth * depth * width,
        moved=count * depth * width * 2,
        limit=limit,
        name=name,
    )(table, *operands, left, inverse, integ, start)


UNIT = 4


def couple(listed, inter, tables, total, amps, ahead, behind):
    count = total.shape[0] - 1
    width = total.shape[1]
    low = 0
    for table in tables:
        amps[pl.ds(low, table.shape[0])] = table[...]
        low += table.shape[0]
    amps[low] = jnp.zeros(amps.shape[1:], amps.dtype)

    @pl.loop(0, count + 1)
    def _(p):
        total[p] = jnp.zeros(total.shape[1:], jnp.float32)

    def codes(group):
        for k in range(UNIT):
            place = 1 + (group * UNIT + k) * 2
            one, two = listed[place], listed[place + 1]
            yield k, one // 65536, (one // 256) % 256, one % 256, (two // 256) % 256, two % 256

    def first(group, mixed):
        for k, _, one, amp_one, two, amp_two in codes(group):
            mixed[k, :, 0:width] = dot(inter[one], amps[amp_one]).astype(jnp.bfloat16)
            mixed[k, :, width : 2 * width] = dot(inter[two], amps[amp_two]).astype(jnp.bfloat16)

    def second(group, mixed):
        for k, pair, one, _, two, _ in codes(group):
            total[pair] += dot_nt(mixed[k], jnp.concatenate([inter[one], inter[two]], axis=1))

    first(0, ahead)

    @pl.loop(0, (listed[0] + 2 * UNIT - 1) // (2 * UNIT))
    def _(step):
        first(2 * step + 1, behind)
        second(2 * step, ahead)
        first(2 * step + 2, ahead)
        second(2 * step + 1, behind)


def early_body(listed, inter, here, near_by, integ, out, total, *scratch):
    couple(listed, inter, (here, near_by), total, *scratch)

    @pl.loop(0, integ.shape[0])
    def _(p):
        out[p] = integ[p] + COUPLING * total[p]


def late_body(listed, inter, other, so_far, inverse, out, total, *scratch):
    couple(listed, inter, (other,), total, *scratch)

    @pl.loop(0, so_far.shape[0])
    def _(p):
        out[p] = ((so_far[p] + COUPLING * total[p]) * inverse[p]).astype(out.dtype)


def last_body(listed, inter, other, so_far, inverse, integ, out, energy, rows, total, *scratch):
    couple(listed, inter, (other,), total, *scratch)
    width = total.shape[1]

    @pl.loop(0, so_far.shape[0])
    def _(p):
        value = (so_far[p] + COUPLING * total[p]) * inverse[p]
        out[p] = value
        rows[pl.ds(p, 1), :] = jnp.sum(integ[p] * value, axis=0, keepdims=True)

    sums = lax.dot_general(
        jnp.ones((8, width), jnp.float32),
        rows[...],
        (((1,), (1,)), ((), ())),
        precision=lax.Precision.HIGHEST,
        preferred_element_type=jnp.float32,
    )
    energy[...] = sums[0:1, :] * (1.0 / (width * width))


def coupling_scratch(count, width, tables):
    return [
        pltpu.VMEM((count + 1, width, width), jnp.float32),
        pltpu.VMEM((tables * count + 1, width, width), jnp.bfloat16),
        pltpu.VMEM((UNIT, width, 2 * width), jnp.bfloat16),
        pltpu.VMEM((UNIT, width, 2 * width), jnp.bfloat16),
    ]


def early_part(listed, inter, here, other, integ):
    count, width, _ = integ.shape
    return call(
        early_body,
        jax.ShapeDtypeStruct(integ.shape, jnp.float32),
        VMEM,
        [SMEM, VMEM, VMEM, VMEM, VMEM],
        coupling_scratch(count, width, 2),
        flops=2 * inter.shape[0] * width**3,
        moved=inter.size * 2,
        limit=24,
        name="early",
    )(listed, inter, here, other, integ)


def late_part(listed, inter, other, so_far, inverse):
    count, width, _ = so_far.shape
    return call(
        late_body,
        jax.ShapeDtypeStruct(so_far.shape, jnp.bfloat16),
        VMEM,
        [SMEM, VMEM, VMEM, VMEM, VMEM],
        coupling_scratch(count, width, 1),
        flops=inter.shape[0] * width**3,
        moved=inter.size * 2,
        limit=24,
        name="late",
    )(listed, inter, other, so_far, inverse)


def last_part(listed, inter, other, so_far, inverse, integ):
    count, width, _ = so_far.shape
    return call(
        last_body,
        (
            jax.ShapeDtypeStruct(so_far.shape, jnp.float32),
            jax.ShapeDtypeStruct((1, count), jnp.float32),
        ),
        (VMEM, VMEM),
        [SMEM, VMEM, VMEM, VMEM, VMEM, VMEM],
        [pltpu.VMEM((count, width), jnp.float32)] + coupling_scratch(count, width, 1),
        flops=inter.shape[0] * width**3,
        moved=inter.size * 2,
        limit=24,
        name="last",
    )(listed, inter, other, so_far, inverse, integ)


def shards(
    blocks,
    pair_orbitals,
    block_sizes,
    pno_maps,
    pno_sizes,
    pno_energy,
    pair_shift,
    neighbours,
    intersections,
):
    devices = lax.axis_size("pairs")
    count, wide, width = pno_maps.shape
    orbitals, depth, _ = blocks.shape
    near = neighbours.shape[1]
    scale = 1.0 / math.sqrt(depth)
    beside_perm = [(i, i ^ 1) for i in range(devices)]
    across_perm = []
    for i in range(1, devices - 1, 2):
        across_perm += [(i, i + 1), (i + 1, i)]
    swap_beside = lambda x: lax.ppermute(x, "pairs", beside_perm)
    swap_across = lambda x: lax.ppermute(x, "pairs", across_perm)

    inter = intersections.reshape(count * near, width, width)
    table, branch = plan(pair_orbitals, block_sizes, orbitals)

    def after(value, *before):
        return lax.optimization_barrier((value,) + before)[0]

    def integrals_with(slots):
        def run(table, blocks, maps, energy, shift, sizes, near_pairs):
            blocks_beside = swap_beside(blocks)
            packed = pack(table, maps, (slots // 2, slots - slots // 2), orbitals)
            got = [swap_across(x) for x in packed]
            left = left_part(table, blocks, maps)
            integ, start, inverse, early, late = own_part(
                table, sizes, shift, near_pairs, blocks, maps, energy, left, scale
            )
            half_one = serve(after(table, early), blocks, got[0], 0, count)
            back_one = swap_across(half_one)
            integ, start = integrals_part(
                functools.partial(beside_body, scale),
                after(table, half_one),
                (blocks_beside, maps),
                left,
                inverse,
                integ,
                start,
                [],
                24,
                "beside",
            )
            half_two = serve(after(table, start), blocks, got[1], got[0].shape[0], count)
            back_two = swap_across(half_two)
            integ, start = integrals_part(
                functools.partial(across_body, scale, orbitals),
                table,
                (back_one, back_two),
                left,
                inverse,
                integ,
                start,
                [pltpu.VMEM((slots, depth, width), jnp.bfloat16)],
                24,
                "across",
            )
            return integ, start, inverse, early, late

        return run

    integ, amps, inverse, early, late = lax.switch(
        branch[0],
        [integrals_with(s) for s in SLOTS],
        table,
        blocks,
        pno_maps,
        pno_energy,
        pair_shift,
        pno_sizes,
        neighbours.T,
    )
    for iteration in range(ITERS):
        far = swap_across(amps)
        close = swap_beside(amps)
        so_far = early_part(early, inter, amps, close, integ)
        if iteration < ITERS - 1:
            amps = late_part(late, inter, far, so_far, inverse)
        else:
            amps, energies = last_part(late, inter, far, so_far, inverse, integ)
    return (amps, energies.reshape(count))


def solution(mesh):
    in_specs = (
        P("pairs", None, None),
        P(),
        P(),
        P("pairs", None, None),
        P("pairs"),
        P("pairs", None),
        P("pairs"),
        P("pairs", None),
        P("pairs", None, None, None),
    )
    out_specs = (P("pairs", None, None), P("pairs"))
    return jax.shard_map(shards, mesh=mesh, in_specs=in_specs, out_specs=out_specs, check_vma=False)
```

```python
import functools
import math

import jax
import jax.numpy as jnp
from jax import lax
from jax.experimental import pallas as pl
from jax.experimental.pallas import tpu as pltpu
from jax.sharding import PartitionSpec as P

ITERS = 2
COUPLING = 0.35
SLOTS = (16, 18, 20, 24, 32)

ANY = pl.BlockSpec(memory_space=pl.ANY)
VMEM = pl.BlockSpec(memory_space=pltpu.VMEM)
SMEM = pl.BlockSpec(memory_space=pltpu.SMEM)

ONE, SRC, SERVE, LIVE = 0, 32, 64, 96


def call(body, outs, out_specs, in_specs, scratch, flops=0, moved=0, limit=60, aliases=None, name=None):
    return pl.pallas_call(
        body,
        out_shape=outs,
        in_specs=in_specs,
        out_specs=out_specs,
        scratch_shapes=scratch,
        input_output_aliases=aliases or {},
        compiler_params=pltpu.CompilerParams(vmem_limit_bytes=limit * 1024 * 1024),
        cost_estimate=pl.CostEstimate(flops=int(flops), bytes_accessed=int(moved), transcendentals=0),
        name=name,
    )


def dot(left, right):
    return jnp.dot(left, right, preferred_element_type=jnp.float32)


def dot_nt(left, right):
    return lax.dot_general(left, right, (((1,), (1,)), ((), ())), preferred_element_type=jnp.float32)


def dot_tn_nt(left, right):
    return lax.dot_general(left, right, (((0,), (1,)), ((), ())), preferred_element_type=jnp.float32)


def collect(count, wanted, slots, begin=None):
    def step(index, found):
        chosen = wanted(index)
        slots[found] = index
        if begin is not None:
            pl.when(chosen)(lambda: begin(index, found))
        return found + chosen.astype(jnp.int32)

    return lax.fori_loop(0, count, step, jnp.int32(0))


def by_twos(number, work, store):
    @pl.loop(0, (number + 1) // 2)
    def _(step):
        both = (2 * step, jnp.minimum(2 * step + 1, number - 1))
        done = [work(k) for k in both]
        for k, values in zip(both, done):
            store(k, values)


def plan_body(orbitals, everyone, pairs_hbm, sizes, table, branch, mine, theirs, sem):
    count = mine.shape[1] // 4
    lanes = mine.shape[1]
    devices = everyone.shape[1] // count
    device = lax.axis_index("pairs")
    side = 2 * (device % 2) - 1
    partner = device + side
    valid = (partner >= 0) & (partner < devices)
    near_by = jnp.clip(partner, 0, devices - 1)

    def fetch(who, place, k):
        start = pl.multiple_of(who // 4 * lanes, lanes)
        return pltpu.make_async_copy(pairs_hbm.at[:, pl.ds(start, lanes)], place, sem.at[k])

    copies = (fetch(device, mine, 0), fetch(near_by, theirs, 1))
    for copy in copies:
        copy.start()

    groups = devices * count // lanes
    second = jnp.concatenate([everyone[1:2, g * lanes : (g + 1) * lanes] for g in range(groups)], axis=0)
    row = lax.broadcasted_iota(jnp.int32, (groups, lanes), 0)
    lane = lax.broadcasted_iota(jnp.int32, (groups, lanes), 1)
    owner = row * (lanes // count) + lane // count
    crossing = jnp.where(second // orbitals == owner + 2 * (owner % 2) - 1, 1.0, 0.0)
    from_lane = lax.broadcasted_iota(jnp.int32, (lanes, lanes), 0) // count
    to_lane = lax.broadcasted_iota(jnp.int32, (lanes, lanes), 1)
    together = jnp.where(from_lane == to_lane, 1.0, 0.0).astype(jnp.bfloat16)
    most = jnp.max(dot(crossing.astype(jnp.bfloat16), together)).astype(jnp.int32)
    branch[0] = sum((most > s).astype(jnp.int32) for s in SLOTS[:-1])

    for copy in copies:
        copy.wait()
    base = device * orbitals
    here = device % 4 * count
    there = near_by % 4 * count

    @pl.loop(0, count)
    def _(p):
        first = mine[0, here + p]
        second = mine[1, here + p]
        local = second - base
        offset = (local >= orbitals).astype(jnp.int32) - (local < 0).astype(jnp.int32)
        kind = jnp.where(offset == 0, 0, jnp.where(offset == side, 2, 1))
        table[ONE + p] = first - base
        table[SRC + p] = kind * orbitals + local - offset * orbitals
        table[SERVE + p] = jnp.where(valid, theirs[1, there + p] - base, -1)
        table[LIVE + p] = jnp.minimum(sizes[first], sizes[second])


def plan(pair_orbitals, block_sizes, orbitals):
    turned = pair_orbitals.T
    return call(
        functools.partial(plan_body, orbitals),
        (jax.ShapeDtypeStruct((128,), jnp.int32), jax.ShapeDtypeStruct((1,), jnp.int32)),
        (SMEM, SMEM),
        [VMEM, ANY, SMEM],
        [pltpu.SMEM((2, 128), jnp.int32), pltpu.SMEM((2, 128), jnp.int32), pltpu.SemaphoreType.DMA((2,))],
        moved=turned.size * 8,
        limit=4,
        name="plan",
    )(turned, turned, block_sizes)


def pack_body(orbitals, table, maps, *refs):
    outs, slots, sem = refs[:-2], refs[-2], refs[-1]
    count = maps.shape[0]

    def begin(pair, slot):
        low = 0
        for out in outs:
            lo, hi = low, low + out.shape[0]

            @pl.when((slot >= lo) & (slot < hi))
            def _(out=out, lo=lo):
                pltpu.make_async_copy(maps.at[pair], out.at[slot - lo], sem.at[slot]).start()

            low = hi

    found = collect(count, lambda p: table[SRC + p] >= 2 * orbitals, slots, begin)

    @pl.loop(0, found)
    def _(slot):
        pltpu.make_async_copy(maps.at[0], outs[0].at[0], sem.at[slot]).wait()


def pack(table, maps, sizes, orbitals):
    count, depth, width = maps.shape
    return call(
        functools.partial(pack_body, orbitals),
        tuple(jax.ShapeDtypeStruct((s, depth, width), maps.dtype) for s in sizes),
        (VMEM,) * len(sizes),
        [SMEM, ANY],
        [pltpu.SMEM((count + 1,), jnp.int32), pltpu.SemaphoreType.DMA((count,))],
        moved=2 * sum(sizes) * depth * width * 2,
        limit=8,
        name="pack",
    )(table, maps)


def left_body(table, blocks, maps, left):
    count, width, depth = left.shape
    columns = lax.broadcasted_iota(jnp.int32, (width, depth), 1)

    def work(p):
        half = dot_tn_nt(maps[p], blocks[table[ONE + p]])
        return jnp.where(columns < table[LIVE + p], half, 0.0).astype(jnp.bfloat16)

    def store(p, half):
        left[p] = half

    by_twos(count, work, store)


def left_part(table, blocks, maps):
    orbitals, depth, wide = blocks.shape
    count, _, width = maps.shape
    return call(
        left_body,
        jax.ShapeDtypeStruct((count, width, depth), jnp.bfloat16),
        VMEM,
        [SMEM, VMEM, VMEM],
        [],
        flops=2 * count * depth * wide * width,
        moved=blocks.size * 2,
        limit=20,
        name="left",
    )(table, blocks, maps)


def own_body(scale, orbitals, table, sizes, shift, near_pairs, blocks, maps, energy, left,
             integ, start, inverse, early, late, slots):
    count, width, _ = left.shape
    near = near_pairs.shape[0]
    device = lax.axis_index("pairs")
    side = 2 * (device % 2) - 1
    ids = lax.broadcasted_iota(jnp.int32, (width, width), 0)
    across_ids = lax.broadcasted_iota(jnp.int32, (width, width), 1)

    def pair_step(pair, counts):
        soon, after = counts
        for k in range(near):
            entry = pair * near + k
            local = near_pairs[k, pair] - device * count
            offset = (local >= count).astype(jnp.int32) - (local < 0).astype(jnp.int32)
            is_late = (offset == side).astype(jnp.int32)
            code = pair * 65536 + entry * 256 + local - offset * count
            early[1 + soon] = code + jnp.where(offset == 0, 0, count)
            late[1 + after] = code
            soon = soon + 1 - is_late
            after = after + is_late
        spare = pair * 65536 + pair * near * 256
        early[1 + soon] = spare + 2 * count
        late[1 + after] = spare + count
        row = jnp.broadcast_to(energy[pl.ds(pair, 1), :], (width, width))
        bottom = row + row.T + shift[pair]
        size = sizes[pair]
        inverse[pair] = jnp.where((ids < size) & (across_ids < size), -1.0 / bottom, 0.0)
        return soon + soon % 2, after + after % 2

    soon, after = lax.fori_loop(0, count, pair_step, (jnp.int32(0), jnp.int32(0)))
    early[0] = soon // 2
    late[0] = after // 2

    @pl.loop(0, 6 * UNIT)
    def _(k):
        early[1 + soon + k] = count * 65536 + 2 * count
        late[1 + after + k] = count * 65536 + count

    found = collect(count, lambda p: table[SRC + p] < orbitals, slots)

    def work(slot):
        pair = slots[slot]
        right = dot(blocks[table[SRC + pair]], maps[pair]).astype(jnp.bfloat16)
        return dot(left[pair], right) * scale

    def store(slot, value):
        pair = slots[slot]
        integ[pair] = value
        start[pair] = (value * inverse[pair]).astype(jnp.bfloat16)

    by_twos(found, work, store)


def own_part(table, sizes, shift, near_pairs, blocks, maps, energy, left, scale):
    orbitals = blocks.shape[0]
    count, width, depth = left.shape
    entries = near_pairs.size + 6 * UNIT + 8
    return call(
        functools.partial(own_body, scale, orbitals),
        (
            jax.ShapeDtypeStruct((count, width, width), jnp.float32),
            jax.ShapeDtypeStruct((count, width, width), jnp.bfloat16),
            jax.ShapeDtypeStruct((count, width, width), jnp.float32),
            jax.ShapeDtypeStruct((entries,), jnp.int32),
            jax.ShapeDtypeStruct((entries,), jnp.int32),
        ),
        (VMEM, VMEM, VMEM, SMEM, SMEM),
        [SMEM, SMEM, SMEM, SMEM, VMEM, VMEM, VMEM, VMEM],
        [pltpu.SMEM((count + 1,), jnp.int32)],
        flops=count * depth * depth * width,
        moved=blocks.size * 2,
        limit=28,
        name="own",
    )(table, sizes, shift, near_pairs, blocks, maps, energy, left)


def serve_body(low, table, blocks, maps, out, slots):
    orbitals = blocks.shape[0]
    size = maps.shape[0]
    found = collect(
        slots.shape[0] - 1,
        lambda p: (table[SERVE + p] >= 0) & (table[SERVE + p] < orbitals),
        slots,
    )

    def work(slot):
        return dot(blocks[table[SERVE + slots[low + slot]]], maps[slot]).astype(jnp.bfloat16)

    def store(slot, half):
        out[slot] = half

    by_twos(jnp.clip(found - low, 0, size), work, store)


def serve(table, blocks, maps, low, count):
    orbitals, depth, wide = blocks.shape
    size, _, width = maps.shape
    return call(
        functools.partial(serve_body, low),
        jax.ShapeDtypeStruct((size, depth, width), jnp.bfloat16),
        VMEM,
        [SMEM, VMEM, VMEM],
        [pltpu.SMEM((count + 1,), jnp.int32)],
        flops=2 * size * depth * wide * width,
        moved=size * depth * (wide + 2 * width) * 2,
        limit=20,
        name="serve",
    )(table, blocks, maps)


def carry_over(integ_in, start_in, integ, start):
    @pl.loop(0, integ.shape[0])
    def _(p):
        integ[p] = integ_in[p]
        start[p] = start_in[p]


def beside_body(scale, table, blocks, maps, left, inverse, integ_in, start_in, integ, start, slots):
    carry_over(integ_in, start_in, integ, start)
    orbitals = blocks.shape[0]
    found = collect(
        left.shape[0],
        lambda p: (table[SRC + p] >= orbitals) & (table[SRC + p] < 2 * orbitals),
        slots,
    )

    def work(slot):
        pair = slots[slot]
        right = dot(blocks[table[SRC + pair] - orbitals], maps[pair]).astype(jnp.bfloat16)
        return dot(left[pair], right) * scale

    def store(slot, value):
        pair = slots[slot]
        integ[pair] = value
        start[pair] = (value * inverse[pair]).astype(jnp.bfloat16)

    by_twos(found, work, store)


def across_body(scale, orbitals, table, *refs):
    n = len(refs) - 8
    halves = refs[:n]
    left, inverse, integ_in, start_in, integ, start, joined, slots = refs[n:]
    carry_over(integ_in, start_in, integ, start)
    low = 0
    for half in halves:
        joined[pl.ds(low, half.shape[0])] = half[...]
        low += half.shape[0]
    found = collect(left.shape[0], lambda p: table[SRC + p] >= 2 * orbitals, slots)

    def work(slot):
        return dot(left[slots[slot]], joined[slot]) * scale

    def store(slot, value):
        pair = slots[slot]
        integ[pair] = value
        start[pair] = (value * inverse[pair]).astype(jnp.bfloat16)

    by_twos(found, work, store)


def integrals_part(body, table, operands, left, inverse, integ, start, scratch, limit, name):
    count, width, depth = left.shape
    n = len(operands)
    return call(
        body,
        (
            jax.ShapeDtypeStruct(integ.shape, integ.dtype),
            jax.ShapeDtypeStruct(start.shape, start.dtype),
        ),
        (VMEM, VMEM),
        [SMEM] + [VMEM] * (n + 4),
        scratch + [pltpu.SMEM((count + 1,), jnp.int32)],
        flops=count * depth * depth * width,
        moved=count * depth * width * 2,
        limit=limit,
        name=name,
    )(table, *operands, left, inverse, integ, start)


CHUNKS = 8
UNIT = 4


def couple(listed, inter, tables, total, amps, ahead, behind, arrived=None):
    count = total.shape[0] - 1
    width = total.shape[1]
    low = 0
    for table in tables:
        amps[pl.ds(low, table.shape[0])] = table[...]
        low += table.shape[0]
    amps[low] = jnp.zeros(amps.shape[1:], amps.dtype)

    @pl.loop(0, count + 1)
    def _(p):
        total[p] = jnp.zeros(total.shape[1:], jnp.float32)

    def codes(group):
        for k in range(UNIT):
            place = 1 + (group * UNIT + k) * 2
            one, two = listed[place], listed[place + 1]
            yield k, one // 65536, (one // 256) % 256, one % 256, (two // 256) % 256, two % 256

    def first(group, mixed):
        for k, _, one, amp_one, two, amp_two in codes(group):
            mixed[k, :, 0:width] = dot(inter[one], amps[amp_one]).astype(jnp.bfloat16)
            mixed[k, :, width : 2 * width] = dot(inter[two], amps[amp_two]).astype(jnp.bfloat16)

    def second(group, mixed):
        for k, pair, one, _, two, _ in codes(group):
            total[pair] += dot_nt(mixed[k], jnp.concatenate([inter[one], inter[two]], axis=1))

    def ready(group, waited):
        if arrived is None:
            return waited
        return arrived(listed[2 * (group + 1) * UNIT] // 65536, waited)

    waited = ready(0, jnp.int32(0))
    first(0, ahead)

    def step(k, waited):
        waited = ready(2 * k + 2, waited)
        first(2 * k + 1, behind)
        second(2 * k, ahead)
        first(2 * k + 2, ahead)
        second(2 * k + 1, behind)
        return waited

    waited = lax.fori_loop(0, (listed[0] + 2 * UNIT - 1) // (2 * UNIT), step, waited)
    if arrived is not None:
        arrived(total.shape[0] - 1, waited)


def opening_body(listed, inter_hbm, here, near_by, integ_hbm, inverse_hbm,
                 out, inter, integ, inverse, total, amps, ahead, behind, sem, more):
    count = integ.shape[0]
    rows = inter.shape[0] // CHUNKS
    pairs = count // CHUNKS

    def piece(k):
        span = pl.ds(k * rows, rows)
        return pltpu.make_async_copy(inter_hbm.at[span], inter.at[span], sem.at[k])

    for k in range(CHUNKS):
        piece(k).start()
    copies = (
        pltpu.make_async_copy(integ_hbm, integ, more.at[0]),
        pltpu.make_async_copy(inverse_hbm, inverse, more.at[1]),
    )
    for copy in copies:
        copy.start()

    def arrived(pair, waited):
        need = jnp.maximum(waited, jnp.minimum(pair // pairs + 1, CHUNKS))
        pl.loop(waited, need)(lambda k: piece(k).wait())
        return need

    couple(listed, inter, (here, near_by), total, amps, ahead, behind, arrived)
    for copy in copies:
        copy.wait()

    @pl.loop(0, count)
    def _(p):
        out[p] = integ[p] + COUPLING * total[p]


def early_body(listed, inter, here, near_by, integ, out, total, *scratch):
    couple(listed, inter, (here, near_by), total, *scratch)

    @pl.loop(0, integ.shape[0])
    def _(p):
        out[p] = integ[p] + COUPLING * total[p]


def late_body(listed, inter, other, so_far, inverse, out, total, *scratch):
    couple(listed, inter, (other,), total, *scratch)

    @pl.loop(0, so_far.shape[0])
    def _(p):
        out[p] = ((so_far[p] + COUPLING * total[p]) * inverse[p]).astype(out.dtype)


def last_body(listed, inter, other, so_far, inverse, integ, out, energy, rows, kept, sem, total, *scratch):
    couple(listed, inter, (other,), total, *scratch)
    width = total.shape[1]
    count = so_far.shape[0]

    def result(p):
        return pltpu.make_async_copy(kept.at[p], out.at[p], sem.at[p])

    @pl.loop(0, count)
    def _(p):
        value = (so_far[p] + COUPLING * total[p]) * inverse[p]
        kept[p] = value
        result(p).start()
        rows[pl.ds(p, 1), :] = jnp.sum(integ[p] * value, axis=0, keepdims=True)

    sums = lax.dot_general(
        jnp.ones((8, width), jnp.float32),
        rows[...],
        (((1,), (1,)), ((), ())),
        precision=lax.Precision.HIGHEST,
        preferred_element_type=jnp.float32,
    )
    energy[...] = sums[0:1, :] * (1.0 / (width * width))
    pl.loop(0, count)(lambda p: result(p).wait())


def coupling_scratch(count, width, tables):
    return [
        pltpu.VMEM((count + 1, width, width), jnp.float32),
        pltpu.VMEM((tables * count + 1, width, width), jnp.bfloat16),
        pltpu.VMEM((UNIT, width, 2 * width), jnp.bfloat16),
        pltpu.VMEM((UNIT, width, 2 * width), jnp.bfloat16),
    ]


def opening_part(listed, inter, here, other, integ, inverse):
    count, width, _ = integ.shape
    return call(
        opening_body,
        tuple(jax.ShapeDtypeStruct(x.shape, x.dtype) for x in (integ, inter, integ, inverse)),
        (VMEM,) * 4,
        [SMEM, ANY, VMEM, VMEM, ANY, ANY],
        coupling_scratch(count, width, 2)
        + [pltpu.SemaphoreType.DMA((CHUNKS,)), pltpu.SemaphoreType.DMA((2,))],
        flops=2 * inter.shape[0] * width**3,
        moved=inter.size * 2,
        limit=26,
        name="opening",
    )(listed, inter, here, other, integ, inverse)


def early_part(listed, inter, here, other, integ):
    count, width, _ = integ.shape
    return call(
        early_body,
        jax.ShapeDtypeStruct(integ.shape, jnp.float32),
        VMEM,
        [SMEM, VMEM, VMEM, VMEM, VMEM],
        coupling_scratch(count, width, 2),
        flops=2 * inter.shape[0] * width**3,
        moved=inter.size * 2,
        limit=24,
        name="early",
    )(listed, inter, here, other, integ)


def late_part(listed, inter, other, so_far, inverse):
    count, width, _ = so_far.shape
    return call(
        late_body,
        jax.ShapeDtypeStruct(so_far.shape, jnp.bfloat16),
        VMEM,
        [SMEM, VMEM, VMEM, VMEM, VMEM],
        coupling_scratch(count, width, 1),
        flops=inter.shape[0] * width**3,
        moved=inter.size * 2,
        limit=24,
        name="late",
    )(listed, inter, other, so_far, inverse)


def last_part(listed, inter, other, so_far, inverse, integ):
    count, width, _ = so_far.shape
    return call(
        last_body,
        (
            jax.ShapeDtypeStruct(so_far.shape, jnp.float32),
            jax.ShapeDtypeStruct((1, count), jnp.float32),
        ),
        (ANY, VMEM),
        [SMEM, VMEM, VMEM, VMEM, VMEM, VMEM],
        [
            pltpu.VMEM((count, width), jnp.float32),
            pltpu.VMEM((count, width, width), jnp.float32),
            pltpu.SemaphoreType.DMA((count,)),
        ]
        + coupling_scratch(count, width, 1),
        flops=inter.shape[0] * width**3,
        moved=inter.size * 2,
        limit=24,
        name="last",
    )(listed, inter, other, so_far, inverse, integ)


def shards(
    blocks,
    pair_orbitals,
    block_sizes,
    pno_maps,
    pno_sizes,
    pno_energy,
    pair_shift,
    neighbours,
    intersections,
):
    devices = lax.axis_size("pairs")
    count, wide, width = pno_maps.shape
    orbitals, depth, _ = blocks.shape
    near = neighbours.shape[1]
    scale = 1.0 / math.sqrt(depth)
    beside_perm = [(i, i ^ 1) for i in range(devices)]
    across_perm = []
    for i in range(1, devices - 1, 2):
        across_perm += [(i, i + 1), (i + 1, i)]
    swap_beside = lambda x: lax.ppermute(x, "pairs", beside_perm)
    swap_across = lambda x: lax.ppermute(x, "pairs", across_perm)

    inter = intersections.reshape(count * near, width, width)
    table, branch = plan(pair_orbitals, block_sizes, orbitals)

    def after(value, *before):
        return lax.optimization_barrier((value,) + before)[0]

    def integrals_with(slots):
        def run(table, blocks, maps, energy, shift, sizes, near_pairs):
            blocks_beside = swap_beside(blocks)
            packed = pack(table, maps, (slots // 2, slots - slots // 2), orbitals)
            got = [swap_across(x) for x in packed]
            left = left_part(table, blocks, maps)
            half_one = serve(after(table, left), blocks, got[0], 0, count)
            back_one = swap_across(half_one)
            integ, start, inverse, early, late = own_part(
                after(table, half_one), sizes, shift, near_pairs, blocks, maps, energy, left, scale
            )
            half_two = serve(after(table, early), blocks, got[1], got[0].shape[0], count)
            back_two = swap_across(half_two)
            integ, start = integrals_part(
                functools.partial(beside_body, scale),
                after(table, half_two),
                (blocks_beside, maps),
                left,
                inverse,
                integ,
                start,
                [],
                24,
                "beside",
            )
            integ, start = integrals_part(
                functools.partial(across_body, scale, orbitals),
                table,
                (back_one, back_two),
                left,
                inverse,
                integ,
                start,
                [pltpu.VMEM((slots, depth, width), jnp.bfloat16)],
                24,
                "across",
            )
            return integ, start, inverse, early, late

        return run

    integ, amps, inverse, early, late = lax.switch(
        branch[0],
        [integrals_with(s) for s in SLOTS],
        table,
        blocks,
        pno_maps,
        pno_energy,
        pair_shift,
        pno_sizes,
        neighbours.T,
    )
    for iteration in range(ITERS):
        far = swap_across(amps)
        close = swap_beside(amps)
        if iteration == 0:
            so_far, inter, integ, inverse = opening_part(early, inter, amps, close, integ, inverse)
        else:
            so_far = early_part(early, inter, amps, close, integ)
        if iteration < ITERS - 1:
            amps = late_part(late, inter, far, so_far, inverse)
        else:
            amps, energies = last_part(late, inter, far, so_far, inverse, integ)
    return (amps, energies.reshape(count))


def solution(mesh):
    in_specs = (
        P("pairs", None, None),
        P(),
        P(),
        P("pairs", None, None),
        P("pairs"),
        P("pairs", None),
        P("pairs"),
        P("pairs", None),
        P("pairs", None, None, None),
    )
    out_specs = (P("pairs", None, None), P("pairs"))
    return jax.shard_map(shards, mesh=mesh, in_specs=in_specs, out_specs=out_specs, check_vma=False)
```

```python
import functools
import math

import jax
import jax.numpy as jnp
from jax import lax
from jax.experimental import pallas as pl
from jax.experimental.pallas import tpu as pltpu
from jax.sharding import PartitionSpec as P

ITERS = 2
COUPLING = 0.35
SLOTS = (17, 18, 19, 20, 24, 32)

ANY = pl.BlockSpec(memory_space=pl.ANY)
HBM = pl.BlockSpec(memory_space=pltpu.HBM)
VMEM = pl.BlockSpec(memory_space=pltpu.VMEM)
SMEM = pl.BlockSpec(memory_space=pltpu.SMEM)

ONE, SRC, SERVE, LIVE = 0, 32, 64, 96


def call(body, outs, out_specs, in_specs, scratch, flops=0, moved=0, limit=60, aliases=None, name=None):
    return pl.pallas_call(
        body,
        out_shape=outs,
        in_specs=in_specs,
        out_specs=out_specs,
        scratch_shapes=scratch,
        input_output_aliases=aliases or {},
        compiler_params=pltpu.CompilerParams(vmem_limit_bytes=limit * 1024 * 1024),
        cost_estimate=pl.CostEstimate(flops=int(flops), bytes_accessed=int(moved), transcendentals=0),
        name=name,
    )


def dot(left, right):
    return jnp.dot(left, right, preferred_element_type=jnp.float32)


def dot_nt(left, right):
    return lax.dot_general(left, right, (((1,), (1,)), ((), ())), preferred_element_type=jnp.float32)


def dot_tn_nt(left, right):
    return lax.dot_general(left, right, (((0,), (1,)), ((), ())), preferred_element_type=jnp.float32)


def collect(count, wanted, slots, begin=None):
    def step(index, found):
        chosen = wanted(index)
        slots[found] = index
        if begin is not None:
            pl.when(chosen)(lambda: begin(index, found))
        return found + chosen.astype(jnp.int32)

    return lax.fori_loop(0, count, step, jnp.int32(0))


def by_twos(number, work, store):
    @pl.loop(0, (number + 1) // 2)
    def _(step):
        both = (2 * step, jnp.minimum(2 * step + 1, number - 1))
        done = [work(k) for k in both]
        for k, values in zip(both, done):
            store(k, values)


def plan_body(orbitals, pairs_hbm, sizes_hbm, table, branch, everyone, sizes, mine, theirs, sem):
    count = mine.shape[1] // 4
    lanes = mine.shape[1]
    devices = everyone.shape[1] // count
    device = lax.axis_index("pairs")
    side = 2 * (device % 2) - 1
    partner = device + side
    valid = (partner >= 0) & (partner < devices)
    near_by = jnp.clip(partner, 0, devices - 1)

    def fetch(who, place, k):
        start = pl.multiple_of(who // 4 * lanes, lanes)
        return pltpu.make_async_copy(pairs_hbm.at[:, pl.ds(start, lanes)], place, sem.at[k])

    copies = (
        fetch(device, mine, 0),
        fetch(near_by, theirs, 1),
        pltpu.make_async_copy(sizes_hbm, sizes, sem.at[3]),
    )
    whole = pltpu.make_async_copy(pairs_hbm, everyone, sem.at[2])
    whole.start()
    for copy in copies:
        copy.start()
    whole.wait()

    groups = devices * count // lanes
    second = jnp.concatenate([everyone[1:2, g * lanes : (g + 1) * lanes] for g in range(groups)], axis=0)
    row = lax.broadcasted_iota(jnp.int32, (groups, lanes), 0)
    lane = lax.broadcasted_iota(jnp.int32, (groups, lanes), 1)
    owner = row * (lanes // count) + lane // count
    crossing = jnp.where(second // orbitals == owner + 2 * (owner % 2) - 1, 1.0, 0.0)
    from_lane = lax.broadcasted_iota(jnp.int32, (lanes, lanes), 0) // count
    to_lane = lax.broadcasted_iota(jnp.int32, (lanes, lanes), 1)
    together = jnp.where(from_lane == to_lane, 1.0, 0.0).astype(jnp.bfloat16)
    most = jnp.max(dot(crossing.astype(jnp.bfloat16), together)).astype(jnp.int32)
    branch[0] = sum((most > s).astype(jnp.int32) for s in SLOTS[:-1])

    for copy in copies:
        copy.wait()
    base = device * orbitals
    here = device % 4 * count
    there = near_by % 4 * count

    @pl.loop(0, count)
    def _(p):
        first = mine[0, here + p]
        second = mine[1, here + p]
        local = second - base
        offset = (local >= orbitals).astype(jnp.int32) - (local < 0).astype(jnp.int32)
        kind = jnp.where(offset == 0, 0, jnp.where(offset == side, 2, 1))
        table[ONE + p] = first - base
        table[SRC + p] = kind * orbitals + local - offset * orbitals
        table[SERVE + p] = jnp.where(valid, theirs[1, there + p] - base, -1)
        table[LIVE + p] = jnp.minimum(sizes[first], sizes[second])


def plan(pair_orbitals, block_sizes, orbitals):
    turned = pair_orbitals.T
    return call(
        functools.partial(plan_body, orbitals),
        (jax.ShapeDtypeStruct((128,), jnp.int32), jax.ShapeDtypeStruct((1,), jnp.int32)),
        (SMEM, SMEM),
        [HBM, HBM],
        [
            pltpu.VMEM(turned.shape, jnp.int32),
            pltpu.SMEM(block_sizes.shape, jnp.int32),
            pltpu.SMEM((2, 128), jnp.int32),
            pltpu.SMEM((2, 128), jnp.int32),
            pltpu.SemaphoreType.DMA((4,)),
        ],
        moved=turned.size * 8,
        limit=4,
        name="plan",
    )(
        pltpu.with_memory_space_constraint(turned, pltpu.HBM),
        pltpu.with_memory_space_constraint(block_sizes, pltpu.HBM),
    )


def pack_body(orbitals, table, maps, *refs):
    outs, slots, sem = refs[:-2], refs[-2], refs[-1]
    count = maps.shape[0]

    def begin(pair, slot):
        low = 0
        for out in outs:
            lo, hi = low, low + out.shape[0]

            @pl.when((slot >= lo) & (slot < hi))
            def _(out=out, lo=lo):
                pltpu.make_async_copy(maps.at[pair], out.at[slot - lo], sem.at[slot]).start()

            low = hi

    found = collect(count, lambda p: table[SRC + p] >= 2 * orbitals, slots, begin)

    @pl.loop(0, found)
    def _(slot):
        pltpu.make_async_copy(maps.at[0], outs[0].at[0], sem.at[slot]).wait()


def pack(table, maps, sizes, orbitals):
    count, depth, width = maps.shape
    return call(
        functools.partial(pack_body, orbitals),
        tuple(jax.ShapeDtypeStruct((s, depth, width), maps.dtype) for s in sizes),
        (VMEM,) * len(sizes),
        [SMEM, ANY],
        [pltpu.SMEM((count + 1,), jnp.int32), pltpu.SemaphoreType.DMA((count,))],
        moved=2 * sum(sizes) * depth * width * 2,
        limit=8,
        name="pack",
    )(table, maps)


def left_body(table, blocks, maps, left):
    count, width, depth = left.shape
    columns = lax.broadcasted_iota(jnp.int32, (width, depth), 1)

    def work(p):
        half = dot_tn_nt(maps[p], blocks[table[ONE + p]])
        return jnp.where(columns < table[LIVE + p], half, 0.0).astype(jnp.bfloat16)

    def store(p, half):
        left[p] = half

    by_twos(count, work, store)


def left_part(table, blocks, maps):
    orbitals, depth, wide = blocks.shape
    count, _, width = maps.shape
    return call(
        left_body,
        jax.ShapeDtypeStruct((count, width, depth), jnp.bfloat16),
        VMEM,
        [SMEM, VMEM, VMEM],
        [],
        flops=2 * count * depth * wide * width,
        moved=blocks.size * 2,
        limit=20,
        name="left",
    )(table, blocks, maps)


def own_body(scale, orbitals, table, sizes, shift, near_pairs, blocks, maps, energy, left,
             integ, start, inverse, early, late, later, slots):
    count, width, _ = left.shape
    part = count // 2
    near = near_pairs.shape[0]
    device = lax.axis_index("pairs")
    side = 2 * (device % 2) - 1
    ids = lax.broadcasted_iota(jnp.int32, (width, width), 0)
    across_ids = lax.broadcasted_iota(jnp.int32, (width, width), 1)

    def pair_step(pair, counts):
        soon, after, last = counts
        for k in range(near):
            entry = pair * near + k
            local = near_pairs[k, pair] - device * count
            offset = (local >= count).astype(jnp.int32) - (local < 0).astype(jnp.int32)
            is_late = (offset == side).astype(jnp.int32)
            code = pair * 65536 + entry * 256 + local - offset * count
            is_last = ((local - offset * count) // part) * is_late
            early[1 + soon] = code + jnp.where(offset == 0, 0, count)
            late[1 + after] = code
            later[1 + last] = code - part
            soon = soon + 1 - is_late
            after = after + is_late - is_last
            last = last + is_last
        spare = pair * 65536 + pair * near * 256
        early[1 + soon] = spare + 2 * count
        late[1 + after] = spare + part
        later[1 + last] = spare + part
        row = jnp.broadcast_to(energy[pl.ds(pair, 1), :], (width, width))
        bottom = row + row.T + shift[pair]
        size = sizes[pair]
        inverse[pair] = jnp.where((ids < size) & (across_ids < size), -1.0 / bottom, 0.0)
        return soon + soon % 2, after + after % 2, last + last % 2

    soon, after, last = lax.fori_loop(0, count, pair_step, (jnp.int32(0),) * 3)
    early[0] = soon // 2
    late[0] = after // 2
    later[0] = last // 2

    @pl.loop(0, 6 * UNIT)
    def _(k):
        early[1 + soon + k] = count * 65536 + 2 * count
        late[1 + after + k] = count * 65536 + part
        later[1 + last + k] = count * 65536 + part

    found = collect(count, lambda p: table[SRC + p] < orbitals, slots)

    def work(slot):
        pair = slots[slot]
        right = dot(blocks[table[SRC + pair]], maps[pair]).astype(jnp.bfloat16)
        return dot(left[pair], right) * scale

    def store(slot, value):
        pair = slots[slot]
        integ[pair] = value
        start[pair] = (value * inverse[pair]).astype(jnp.bfloat16)

    by_twos(found, work, store)


def own_part(table, sizes, shift, near_pairs, blocks, maps, energy, left, scale):
    orbitals = blocks.shape[0]
    count, width, depth = left.shape
    entries = near_pairs.size + 6 * UNIT + 8
    return call(
        functools.partial(own_body, scale, orbitals),
        (
            jax.ShapeDtypeStruct((count, width, width), jnp.float32),
            jax.ShapeDtypeStruct((count, width, width), jnp.bfloat16),
            jax.ShapeDtypeStruct((count, width, width), jnp.float32),
        )
        + (jax.ShapeDtypeStruct((entries,), jnp.int32),) * 3,
        (VMEM, VMEM, VMEM, SMEM, SMEM, SMEM),
        [SMEM, SMEM, SMEM, SMEM, VMEM, VMEM, VMEM, VMEM],
        [pltpu.SMEM((count + 1,), jnp.int32)],
        flops=count * depth * depth * width,
        moved=blocks.size * 2,
        limit=28,
        name="own",
    )(table, sizes, shift, near_pairs, blocks, maps, energy, left)


def serve_body(low, table, blocks, maps, out, slots):
    orbitals = blocks.shape[0]
    size = maps.shape[0]
    found = collect(
        slots.shape[0] - 1,
        lambda p: (table[SERVE + p] >= 0) & (table[SERVE + p] < orbitals),
        slots,
    )

    def work(slot):
        return dot(blocks[table[SERVE + slots[low + slot]]], maps[slot]).astype(jnp.bfloat16)

    def store(slot, half):
        out[slot] = half

    by_twos(jnp.clip(found - low, 0, size), work, store)


def serve(table, blocks, maps, low, count):
    orbitals, depth, wide = blocks.shape
    size, _, width = maps.shape
    return call(
        functools.partial(serve_body, low),
        jax.ShapeDtypeStruct((size, depth, width), jnp.bfloat16),
        VMEM,
        [SMEM, VMEM, VMEM],
        [pltpu.SMEM((count + 1,), jnp.int32)],
        flops=2 * size * depth * wide * width,
        moved=size * depth * (wide + 2 * width) * 2,
        limit=20,
        name="serve",
    )(table, blocks, maps)


def carry_over(integ_in, start_in, integ, start):
    @pl.loop(0, integ.shape[0])
    def _(p):
        integ[p] = integ_in[p]
        start[p] = start_in[p]


def beside_body(scale, table, blocks, maps, left, inverse, integ_in, start_in, integ, start, slots):
    carry_over(integ_in, start_in, integ, start)
    orbitals = blocks.shape[0]
    found = collect(
        left.shape[0],
        lambda p: (table[SRC + p] >= orbitals) & (table[SRC + p] < 2 * orbitals),
        slots,
    )

    def work(slot):
        pair = slots[slot]
        right = dot(blocks[table[SRC + pair] - orbitals], maps[pair]).astype(jnp.bfloat16)
        return dot(left[pair], right) * scale

    def store(slot, value):
        pair = slots[slot]
        integ[pair] = value
        start[pair] = (value * inverse[pair]).astype(jnp.bfloat16)

    by_twos(found, work, store)


def across_body(scale, orbitals, table, *refs):
    n = len(refs) - 10
    halves = refs[:n]
    left, inverse, integ_in, start_in, integ, start, one, two, joined, slots = refs[n:]
    carry_over(integ_in, start_in, integ, start)
    low = 0
    for half in halves:
        joined[pl.ds(low, half.shape[0])] = half[...]
        low += half.shape[0]
    found = collect(left.shape[0], lambda p: table[SRC + p] >= 2 * orbitals, slots)

    def work(slot):
        return dot(left[slots[slot]], joined[slot]) * scale

    def store(slot, value):
        pair = slots[slot]
        integ[pair] = value
        start[pair] = (value * inverse[pair]).astype(jnp.bfloat16)

    by_twos(found, work, store)
    split(start, one, two)


def split(amps, one, two):
    part = one.shape[0]

    @pl.loop(0, part)
    def _(p):
        one[p] = amps[p]
        two[p] = amps[part + p]


def amps_shapes(start, halved=True):
    parts = (start.shape[0] // 2,) + start.shape[1:]
    shapes = (start.shape,) + ((parts, parts) if halved else ())
    return tuple(jax.ShapeDtypeStruct(shape, jnp.bfloat16) for shape in shapes)


def integrals_part(body, table, operands, left, inverse, integ, start, scratch, limit, name):
    count, width, depth = left.shape
    n = len(operands)
    outs = (jax.ShapeDtypeStruct(integ.shape, integ.dtype),) + amps_shapes(start, name == "across")
    return call(
        body,
        outs,
        (VMEM,) * len(outs),
        [SMEM] + [VMEM] * (n + 4),
        scratch + [pltpu.SMEM((count + 1,), jnp.int32)],
        flops=count * depth * depth * width,
        moved=count * depth * width * 2,
        limit=limit,
        name=name,
    )(table, *operands, left, inverse, integ, start)


CHUNKS = 8
UNIT = 4


def couple(listed, inter, tables, total, amps, ahead, behind, arrived=None):
    count = total.shape[0] - 1
    width = total.shape[1]
    low = 0
    for table in tables:
        amps[pl.ds(low, table.shape[0])] = table[...]
        low += table.shape[0]
    amps[low] = jnp.zeros(amps.shape[1:], amps.dtype)

    @pl.loop(0, count + 1)
    def _(p):
        total[p] = jnp.zeros(total.shape[1:], jnp.float32)

    def codes(group):
        for k in range(UNIT):
            place = 1 + (group * UNIT + k) * 2
            one, two = listed[place], listed[place + 1]
            yield k, one // 65536, (one // 256) % 256, one % 256, (two // 256) % 256, two % 256

    def first(group, mixed):
        for k, _, one, amp_one, two, amp_two in codes(group):
            mixed[k, :, 0:width] = dot(inter[one], amps[amp_one]).astype(jnp.bfloat16)
            mixed[k, :, width : 2 * width] = dot(inter[two], amps[amp_two]).astype(jnp.bfloat16)

    def second(group, mixed):
        for k, pair, one, _, two, _ in codes(group):
            total[pair] += dot_nt(mixed[k], jnp.concatenate([inter[one], inter[two]], axis=1))

    def ready(group, waited):
        if arrived is None:
            return waited
        return arrived(listed[2 * (group + 1) * UNIT] // 65536, waited)

    waited = ready(0, jnp.int32(0))
    first(0, ahead)

    def step(k, waited):
        waited = ready(2 * k + 2, waited)
        first(2 * k + 1, behind)
        second(2 * k, ahead)
        first(2 * k + 2, ahead)
        second(2 * k + 1, behind)
        return waited

    waited = lax.fori_loop(0, (listed[0] + 2 * UNIT - 1) // (2 * UNIT), step, waited)
    if arrived is not None:
        arrived(total.shape[0] - 1, waited)


def opening_body(listed, inter_hbm, here, near_by, integ_hbm, inverse_hbm,
                 out, inter, integ, inverse, total, amps, ahead, behind, sem, more):
    count = integ.shape[0]
    rows = inter.shape[0] // CHUNKS
    pairs = count // CHUNKS

    def piece(k):
        span = pl.ds(k * rows, rows)
        return pltpu.make_async_copy(inter_hbm.at[span], inter.at[span], sem.at[k])

    for k in range(CHUNKS):
        piece(k).start()
    copies = (
        pltpu.make_async_copy(integ_hbm, integ, more.at[0]),
        pltpu.make_async_copy(inverse_hbm, inverse, more.at[1]),
    )
    for copy in copies:
        copy.start()

    def arrived(pair, waited):
        need = jnp.maximum(waited, jnp.minimum(pair // pairs + 1, CHUNKS))
        pl.loop(waited, need)(lambda k: piece(k).wait())
        return need

    couple(listed, inter, (here, near_by), total, amps, ahead, behind, arrived)
    for copy in copies:
        copy.wait()

    @pl.loop(0, count)
    def _(p):
        out[p] = integ[p] + COUPLING * total[p]


def early_body(tables, listed, inter, *refs):
    integ, out, total = refs[tables : tables + 3]
    couple(listed, inter, refs[:tables], total, *refs[tables + 3 :])

    @pl.loop(0, integ.shape[0])
    def _(p):
        out[p] = integ[p] + COUPLING * total[p]


def late_body(listed, inter, other, so_far, inverse, out, one, two, total, *scratch):
    couple(listed, inter, (other,), total, *scratch)

    @pl.loop(0, so_far.shape[0])
    def _(p):
        out[p] = ((so_far[p] + COUPLING * total[p]) * inverse[p]).astype(out.dtype)

    split(out, one, two)


def last_body(listed, inter, other, so_far, inverse, integ, out, energy, rows, kept, sem, total, *scratch):
    couple(listed, inter, (other,), total, *scratch)
    width = total.shape[1]
    count = so_far.shape[0]

    def result(p):
        return pltpu.make_async_copy(kept.at[p], out.at[p], sem.at[p])

    @pl.loop(0, count)
    def _(p):
        value = (so_far[p] + COUPLING * total[p]) * inverse[p]
        kept[p] = value
        result(p).start()
        rows[pl.ds(p, 1), :] = jnp.sum(integ[p] * value, axis=0, keepdims=True)

    sums = lax.dot_general(
        jnp.ones((8, width), jnp.float32),
        rows[...],
        (((1,), (1,)), ((), ())),
        precision=lax.Precision.HIGHEST,
        preferred_element_type=jnp.float32,
    )
    energy[...] = sums[0:1, :] * (1.0 / (width * width))
    pl.loop(0, count)(lambda p: result(p).wait())


def coupling_scratch(count, width, slots):
    return [
        pltpu.VMEM((count + 1, width, width), jnp.float32),
        pltpu.VMEM((slots + 1, width, width), jnp.bfloat16),
        pltpu.VMEM((UNIT, width, 2 * width), jnp.bfloat16),
        pltpu.VMEM((UNIT, width, 2 * width), jnp.bfloat16),
    ]


def opening_part(listed, inter, here, other, integ, inverse):
    count, width, _ = integ.shape
    return call(
        opening_body,
        tuple(jax.ShapeDtypeStruct(x.shape, x.dtype) for x in (integ, inter, integ, inverse)),
        (VMEM,) * 4,
        [SMEM, HBM, VMEM, VMEM, HBM, HBM],
        coupling_scratch(count, width, 2 * count)
        + [pltpu.SemaphoreType.DMA((CHUNKS,)), pltpu.SemaphoreType.DMA((2,))],
        flops=2 * inter.shape[0] * width**3,
        moved=inter.size * 2,
        limit=26,
        name="opening",
    )(listed, inter, here, other, integ, inverse)


def early_part(listed, inter, tables, integ, name):
    count, width, _ = integ.shape
    slots = sum(table.shape[0] for table in tables)
    return call(
        functools.partial(early_body, len(tables)),
        jax.ShapeDtypeStruct(integ.shape, jnp.float32),
        VMEM,
        [SMEM, VMEM, VMEM] + [VMEM] * len(tables),
        coupling_scratch(count, width, slots),
        flops=inter.shape[0] * width**3,
        moved=inter.size * 2,
        limit=24,
        name=name,
    )(listed, inter, *tables, integ)


def late_part(listed, inter, other, so_far, inverse):
    count, width, _ = so_far.shape
    return call(
        late_body,
        amps_shapes(so_far),
        (VMEM,) * 3,
        [SMEM, VMEM, VMEM, VMEM, VMEM],
        coupling_scratch(count, width, count // 2),
        flops=inter.shape[0] * width**3,
        moved=inter.size * 2,
        limit=24,
        name="later",
    )(listed, inter, other, so_far, inverse)


def last_part(listed, inter, other, so_far, inverse, integ):
    count, width, _ = so_far.shape
    return call(
        last_body,
        (
            jax.ShapeDtypeStruct(so_far.shape, jnp.float32),
            jax.ShapeDtypeStruct((1, count), jnp.float32),
        ),
        (ANY, VMEM),
        [SMEM, VMEM, VMEM, VMEM, VMEM, VMEM],
        [
            pltpu.VMEM((count, width), jnp.float32),
            pltpu.VMEM((count, width, width), jnp.float32),
            pltpu.SemaphoreType.DMA((count,)),
        ]
        + coupling_scratch(count, width, count // 2),
        flops=inter.shape[0] * width**3,
        moved=inter.size * 2,
        limit=24,
        name="last",
    )(listed, inter, other, so_far, inverse, integ)


def shards(
    blocks,
    pair_orbitals,
    block_sizes,
    pno_maps,
    pno_sizes,
    pno_energy,
    pair_shift,
    neighbours,
    intersections,
):
    devices = lax.axis_size("pairs")
    count, wide, width = pno_maps.shape
    orbitals, depth, _ = blocks.shape
    near = neighbours.shape[1]
    scale = 1.0 / math.sqrt(depth)
    beside_perm = [(i, i ^ 1) for i in range(devices)]
    across_perm = []
    for i in range(1, devices - 1, 2):
        across_perm += [(i, i + 1), (i + 1, i)]
    swap_beside = lambda x: lax.ppermute(x, "pairs", beside_perm)
    swap_across = lambda x: lax.ppermute(x, "pairs", across_perm)

    inter = intersections.reshape(count * near, width, width)
    table, branch = plan(
        pair_orbitals,
        block_sizes,
        orbitals,
    )

    def after(value, *before):
        return lax.optimization_barrier((value,) + before)[0]

    def integrals_with(slots):
        def run(table, blocks, maps, energy, shift, sizes, near_pairs):
            blocks_beside = swap_beside(blocks)
            packed = pack(table, maps, (slots // 2, slots - slots // 2), orbitals)
            got = [swap_across(x) for x in packed]
            left = left_part(table, blocks, maps)
            half_one = serve(after(table, left), blocks, got[0], 0, count)
            back_one = swap_across(half_one)
            integ, start, inverse, *lists = own_part(
                after(table, half_one), sizes, shift, near_pairs, blocks, maps, energy, left, scale
            )
            half_two = serve(after(table, lists[0]), blocks, got[1], got[0].shape[0], count)
            back_two = swap_across(half_two)
            integ, start = integrals_part(
                functools.partial(beside_body, scale),
                after(table, half_two),
                (blocks_beside, maps),
                left,
                inverse,
                integ,
                start,
                [],
                24,
                "beside",
            )
            integ, *start = integrals_part(
                functools.partial(across_body, scale, orbitals),
                table,
                (back_one, back_two),
                left,
                inverse,
                integ,
                start,
                [pltpu.VMEM((slots, depth, width), jnp.bfloat16)],
                24,
                "across",
            )
            return integ, start, inverse, lists

        return run

    integ, amps, inverse, lists = lax.switch(
        branch[0],
        [integrals_with(s) for s in SLOTS],
        table,
        blocks,
        pno_maps,
        pno_energy,
        pair_shift,
        pno_sizes,
        neighbours.T,
    )
    early, late, later = lists
    for iteration in range(ITERS):
        whole, one, two = amps
        far = swap_across(one)
        farther = swap_across(two)
        close = swap_beside(whole)
        if iteration == 0:
            stay = pltpu.with_memory_space_constraint(inter, pltpu.HBM)
            so_far, inter, integ, inverse = opening_part(early, stay, whole, close, integ, inverse)
        else:
            so_far = early_part(early, inter, (whole, close), integ, "early")
        so_far = early_part(late, inter, (far,), so_far, "late")
        if iteration < ITERS - 1:
            amps = late_part(later, inter, farther, so_far, inverse)
        else:
            amps, energies = last_part(later, inter, farther, so_far, inverse, integ)
    return (amps, energies.reshape(count))


def solution(mesh):
    in_specs = (
        P("pairs", None, None),
        P(),
        P(),
        P("pairs", None, None),
        P("pairs"),
        P("pairs", None),
        P("pairs"),
        P("pairs", None),
        P("pairs", None, None, None),
    )
    out_specs = (P("pairs", None, None), P("pairs"))
    return jax.shard_map(shards, mesh=mesh, in_specs=in_specs, out_specs=out_specs, check_vma=False)
```

```python
import functools
import math

import jax
import jax.numpy as jnp
from jax import lax
from jax.experimental import pallas as pl
from jax.experimental.pallas import tpu as pltpu
from jax.sharding import PartitionSpec as P

ITERS = 2
COUPLING = 0.35
SLOTS = (17, 18, 19, 20, 24, 32)

ANY = pl.BlockSpec(memory_space=pl.ANY)
HBM = pl.BlockSpec(memory_space=pltpu.HBM)
VMEM = pl.BlockSpec(memory_space=pltpu.VMEM)
SMEM = pl.BlockSpec(memory_space=pltpu.SMEM)

ONE, SRC, SERVE, LIVE = 0, 32, 64, 96


def call(body, outs, out_specs, in_specs, scratch, flops=0, moved=0, limit=60, aliases=None, name=None):
    return pl.pallas_call(
        body,
        out_shape=outs,
        in_specs=in_specs,
        out_specs=out_specs,
        scratch_shapes=scratch,
        input_output_aliases=aliases or {},
        compiler_params=pltpu.CompilerParams(vmem_limit_bytes=limit * 1024 * 1024),
        cost_estimate=pl.CostEstimate(flops=int(flops), bytes_accessed=int(moved), transcendentals=0),
        name=name,
    )


def dot(left, right):
    return jnp.dot(left, right, preferred_element_type=jnp.float32)


def dot_nt(left, right):
    return lax.dot_general(left, right, (((1,), (1,)), ((), ())), preferred_element_type=jnp.float32)


def dot_tn_nt(left, right):
    return lax.dot_general(left, right, (((0,), (1,)), ((), ())), preferred_element_type=jnp.float32)


def collect(count, wanted, slots, begin=None):
    def step(index, found):
        chosen = wanted(index)
        slots[found] = index
        if begin is not None:
            pl.when(chosen)(lambda: begin(index, found))
        return found + chosen.astype(jnp.int32)

    return lax.fori_loop(0, count, step, jnp.int32(0))


def by_twos(number, work, store):
    @pl.loop(0, (number + 1) // 2)
    def _(step):
        both = (2 * step, jnp.minimum(2 * step + 1, number - 1))
        done = [work(k) for k in both]
        for k, values in zip(both, done):
            store(k, values)


def plan_body(orbitals, pairs_hbm, sizes_hbm, table, branch, everyone, sizes, mine, theirs, sem):
    count = mine.shape[1] // 4
    lanes = mine.shape[1]
    devices = everyone.shape[1] // count
    device = lax.axis_index("pairs")
    side = 2 * (device % 2) - 1
    partner = device + side
    valid = (partner >= 0) & (partner < devices)
    near_by = jnp.clip(partner, 0, devices - 1)

    def fetch(who, place, k):
        start = pl.multiple_of(who // 4 * lanes, lanes)
        return pltpu.make_async_copy(pairs_hbm.at[:, pl.ds(start, lanes)], place, sem.at[k])

    copies = (
        fetch(device, mine, 0),
        fetch(near_by, theirs, 1),
        pltpu.make_async_copy(sizes_hbm, sizes, sem.at[3]),
    )
    whole = pltpu.make_async_copy(pairs_hbm, everyone, sem.at[2])
    whole.start()
    for copy in copies:
        copy.start()
    whole.wait()

    groups = devices * count // lanes
    second = jnp.concatenate([everyone[1:2, g * lanes : (g + 1) * lanes] for g in range(groups)], axis=0)
    row = lax.broadcasted_iota(jnp.int32, (groups, lanes), 0)
    lane = lax.broadcasted_iota(jnp.int32, (groups, lanes), 1)
    owner = row * (lanes // count) + lane // count
    crossing = jnp.where(second // orbitals == owner + 2 * (owner % 2) - 1, 1.0, 0.0)
    from_lane = lax.broadcasted_iota(jnp.int32, (lanes, lanes), 0) // count
    to_lane = lax.broadcasted_iota(jnp.int32, (lanes, lanes), 1)
    together = jnp.where(from_lane == to_lane, 1.0, 0.0).astype(jnp.bfloat16)
    most = jnp.max(dot(crossing.astype(jnp.bfloat16), together)).astype(jnp.int32)
    branch[0] = sum((most > s).astype(jnp.int32) for s in SLOTS[:-1])

    for copy in copies:
        copy.wait()
    base = device * orbitals
    here = device % 4 * count
    there = near_by % 4 * count

    @pl.loop(0, count)
    def _(p):
        first = mine[0, here + p]
        second = mine[1, here + p]
        local = second - base
        offset = (local >= orbitals).astype(jnp.int32) - (local < 0).astype(jnp.int32)
        kind = jnp.where(offset == 0, 0, jnp.where(offset == side, 2, 1))
        table[ONE + p] = first - base
        table[SRC + p] = kind * orbitals + local - offset * orbitals
        table[SERVE + p] = jnp.where(valid, theirs[1, there + p] - base, -1)
        table[LIVE + p] = jnp.minimum(sizes[first], sizes[second])


def plan(pair_orbitals, block_sizes, orbitals):
    turned = pair_orbitals.T
    return call(
        functools.partial(plan_body, orbitals),
        (jax.ShapeDtypeStruct((128,), jnp.int32), jax.ShapeDtypeStruct((1,), jnp.int32)),
        (SMEM, SMEM),
        [HBM, HBM],
        [
            pltpu.VMEM(turned.shape, jnp.int32),
            pltpu.SMEM(block_sizes.shape, jnp.int32),
            pltpu.SMEM((2, 128), jnp.int32),
            pltpu.SMEM((2, 128), jnp.int32),
            pltpu.SemaphoreType.DMA((4,)),
        ],
        moved=turned.size * 8,
        limit=4,
        name="plan",
    )(
        pltpu.with_memory_space_constraint(turned, pltpu.HBM),
        pltpu.with_memory_space_constraint(block_sizes, pltpu.HBM),
    )


def pack_body(orbitals, table, maps, *refs):
    outs, slots, sem = refs[:-2], refs[-2], refs[-1]
    count = maps.shape[0]

    def begin(pair, slot):
        low = 0
        for out in outs:
            lo, hi = low, low + out.shape[0]

            @pl.when((slot >= lo) & (slot < hi))
            def _(out=out, lo=lo):
                pltpu.make_async_copy(maps.at[pair], out.at[slot - lo], sem.at[slot]).start()

            low = hi

    found = collect(count, lambda p: table[SRC + p] >= 2 * orbitals, slots, begin)

    @pl.loop(0, found)
    def _(slot):
        pltpu.make_async_copy(maps.at[0], outs[0].at[0], sem.at[slot]).wait()


def pack(table, maps, sizes, orbitals):
    count, depth, width = maps.shape
    return call(
        functools.partial(pack_body, orbitals),
        tuple(jax.ShapeDtypeStruct((s, depth, width), maps.dtype) for s in sizes),
        (VMEM,) * len(sizes),
        [SMEM, ANY],
        [pltpu.SMEM((count + 1,), jnp.int32), pltpu.SemaphoreType.DMA((count,))],
        moved=2 * sum(sizes) * depth * width * 2,
        limit=8,
        name="pack",
    )(table, maps)


def left_body(table, blocks, maps, left):
    count, width, depth = left.shape
    columns = lax.broadcasted_iota(jnp.int32, (width, depth), 1)

    def work(p):
        half = dot_tn_nt(maps[p], blocks[table[ONE + p]])
        return jnp.where(columns < table[LIVE + p], half, 0.0).astype(jnp.bfloat16)

    def store(p, half):
        left[p] = half

    by_twos(count, work, store)


def left_part(table, blocks, maps):
    orbitals, depth, wide = blocks.shape
    count, _, width = maps.shape
    return call(
        left_body,
        jax.ShapeDtypeStruct((count, width, depth), jnp.bfloat16),
        VMEM,
        [SMEM, VMEM, VMEM],
        [],
        flops=2 * count * depth * wide * width,
        moved=blocks.size * 2,
        limit=20,
        name="left",
    )(table, blocks, maps)


def own_body(scale, orbitals, table, sizes, shift, near_pairs, blocks, maps, energy, left,
             integ, start, inverse, early, late, slots):
    count, width, _ = left.shape
    near = near_pairs.shape[0]
    device = lax.axis_index("pairs")
    side = 2 * (device % 2) - 1
    ids = lax.broadcasted_iota(jnp.int32, (width, width), 0)
    across_ids = lax.broadcasted_iota(jnp.int32, (width, width), 1)

    def pair_step(pair, counts):
        soon, after = counts
        for k in range(near):
            entry = pair * near + k
            local = near_pairs[k, pair] - device * count
            offset = (local >= count).astype(jnp.int32) - (local < 0).astype(jnp.int32)
            is_late = (offset == side).astype(jnp.int32)
            code = pair * 65536 + entry * 256 + local - offset * count
            early[1 + soon] = code + jnp.where(offset == 0, 0, count)
            late[1 + after] = code
            soon = soon + 1 - is_late
            after = after + is_late
        spare = pair * 65536 + pair * near * 256
        early[1 + soon] = spare + 2 * count
        late[1 + after] = spare + count
        row = jnp.broadcast_to(energy[pl.ds(pair, 1), :], (width, width))
        bottom = row + row.T + shift[pair]
        size = sizes[pair]
        inverse[pair] = jnp.where((ids < size) & (across_ids < size), -1.0 / bottom, 0.0)
        return soon + soon % 2, after + after % 2

    soon, after = lax.fori_loop(0, count, pair_step, (jnp.int32(0), jnp.int32(0)))
    early[0] = soon // 2
    late[0] = after // 2

    @pl.loop(0, 6 * UNIT)
    def _(k):
        early[1 + soon + k] = count * 65536 + 2 * count
        late[1 + after + k] = count * 65536 + count

    found = collect(count, lambda p: table[SRC + p] < orbitals, slots)

    def work(slot):
        pair = slots[slot]
        right = dot(blocks[table[SRC + pair]], maps[pair]).astype(jnp.bfloat16)
        return dot(left[pair], right) * scale

    def store(slot, value):
        pair = slots[slot]
        integ[pair] = value
        start[pair] = (value * inverse[pair]).astype(jnp.bfloat16)

    by_twos(found, work, store)


def own_part(table, sizes, shift, near_pairs, blocks, maps, energy, left, scale):
    orbitals = blocks.shape[0]
    count, width, depth = left.shape
    entries = near_pairs.size + 6 * UNIT + 8
    return call(
        functools.partial(own_body, scale, orbitals),
        (
            jax.ShapeDtypeStruct((count, width, width), jnp.float32),
            jax.ShapeDtypeStruct((count, width, width), jnp.bfloat16),
            jax.ShapeDtypeStruct((count, width, width), jnp.float32),
            jax.ShapeDtypeStruct((entries,), jnp.int32),
            jax.ShapeDtypeStruct((entries,), jnp.int32),
        ),
        (VMEM, VMEM, VMEM, SMEM, SMEM),
        [SMEM, SMEM, SMEM, SMEM, VMEM, VMEM, VMEM, VMEM],
        [pltpu.SMEM((count + 1,), jnp.int32)],
        flops=count * depth * depth * width,
        moved=blocks.size * 2,
        limit=28,
        name="own",
    )(table, sizes, shift, near_pairs, blocks, maps, energy, left)


def serve_body(low, table, blocks, maps, out, slots):
    orbitals = blocks.shape[0]
    size = maps.shape[0]
    found = collect(
        slots.shape[0] - 1,
        lambda p: (table[SERVE + p] >= 0) & (table[SERVE + p] < orbitals),
        slots,
    )

    def work(slot):
        return dot(blocks[table[SERVE + slots[low + slot]]], maps[slot]).astype(jnp.bfloat16)

    def store(slot, half):
        out[slot] = half

    by_twos(jnp.clip(found - low, 0, size), work, store)


def serve(table, blocks, maps, low, count):
    orbitals, depth, wide = blocks.shape
    size, _, width = maps.shape
    return call(
        functools.partial(serve_body, low),
        jax.ShapeDtypeStruct((size, depth, width), jnp.bfloat16),
        VMEM,
        [SMEM, VMEM, VMEM],
        [pltpu.SMEM((count + 1,), jnp.int32)],
        flops=2 * size * depth * wide * width,
        moved=size * depth * (wide + 2 * width) * 2,
        limit=20,
        name="serve",
    )(table, blocks, maps)


def carry_over(integ_in, start_in, integ, start):
    @pl.loop(0, integ.shape[0])
    def _(p):
        integ[p] = integ_in[p]
        start[p] = start_in[p]


def beside_body(scale, table, blocks, maps, left, inverse, integ_in, start_in, integ, start, slots):
    carry_over(integ_in, start_in, integ, start)
    orbitals = blocks.shape[0]
    found = collect(
        left.shape[0],
        lambda p: (table[SRC + p] >= orbitals) & (table[SRC + p] < 2 * orbitals),
        slots,
    )

    def work(slot):
        pair = slots[slot]
        right = dot(blocks[table[SRC + pair] - orbitals], maps[pair]).astype(jnp.bfloat16)
        return dot(left[pair], right) * scale

    def store(slot, value):
        pair = slots[slot]
        integ[pair] = value
        start[pair] = (value * inverse[pair]).astype(jnp.bfloat16)

    by_twos(found, work, store)


def across_body(scale, orbitals, table, *refs):
    n = len(refs) - 8
    halves = refs[:n]
    left, inverse, integ_in, start_in, integ, start, joined, slots = refs[n:]
    carry_over(integ_in, start_in, integ, start)
    low = 0
    for half in halves:
        joined[pl.ds(low, half.shape[0])] = half[...]
        low += half.shape[0]
    found = collect(left.shape[0], lambda p: table[SRC + p] >= 2 * orbitals, slots)

    def work(slot):
        return dot(left[slots[slot]], joined[slot]) * scale

    def store(slot, value):
        pair = slots[slot]
        integ[pair] = value
        start[pair] = (value * inverse[pair]).astype(jnp.bfloat16)

    by_twos(found, work, store)


def integrals_part(body, table, operands, left, inverse, integ, start, scratch, limit, name):
    count, width, depth = left.shape
    n = len(operands)
    return call(
        body,
        (
            jax.ShapeDtypeStruct(integ.shape, integ.dtype),
            jax.ShapeDtypeStruct(start.shape, start.dtype),
        ),
        (VMEM, VMEM),
        [SMEM] + [VMEM] * (n + 4),
        scratch + [pltpu.SMEM((count + 1,), jnp.int32)],
        flops=count * depth * depth * width,
        moved=count * depth * width * 2,
        limit=limit,
        name=name,
    )(table, *operands, left, inverse, integ, start)


CHUNKS = 8
UNIT = 4


def couple(listed, inter, tables, total, amps, ahead, behind, arrived=None):
    count = total.shape[0] - 1
    width = total.shape[1]
    low = 0
    for table in tables:
        amps[pl.ds(low, table.shape[0])] = table[...]
        low += table.shape[0]
    amps[low] = jnp.zeros(amps.shape[1:], amps.dtype)

    @pl.loop(0, count + 1)
    def _(p):
        total[p] = jnp.zeros(total.shape[1:], jnp.float32)

    def codes(group):
        for k in range(UNIT):
            place = 1 + (group * UNIT + k) * 2
            one, two = listed[place], listed[place + 1]
            yield k, one // 65536, (one // 256) % 256, one % 256, (two // 256) % 256, two % 256

    def first(group, mixed):
        for k, _, one, amp_one, two, amp_two in codes(group):
            mixed[k, :, 0:width] = dot(inter[one], amps[amp_one]).astype(jnp.bfloat16)
            mixed[k, :, width : 2 * width] = dot(inter[two], amps[amp_two]).astype(jnp.bfloat16)

    def second(group, mixed):
        for k, pair, one, _, two, _ in codes(group):
            total[pair] += dot_nt(mixed[k], jnp.concatenate([inter[one], inter[two]], axis=1))

    def ready(group, waited):
        if arrived is None:
            return waited
        return arrived(listed[2 * (group + 1) * UNIT] // 65536, waited)

    waited = ready(0, jnp.int32(0))
    first(0, ahead)

    def step(k, waited):
        waited = ready(2 * k + 2, waited)
        first(2 * k + 1, behind)
        second(2 * k, ahead)
        first(2 * k + 2, ahead)
        second(2 * k + 1, behind)
        return waited

    waited = lax.fori_loop(0, (listed[0] + 2 * UNIT - 1) // (2 * UNIT), step, waited)
    if arrived is not None:
        arrived(total.shape[0] - 1, waited)


def opening_body(listed, inter_hbm, here, near_by, integ_hbm, inverse_hbm,
                 out, inter, integ, inverse, total, amps, ahead, behind, sem, more):
    count = integ.shape[0]
    rows = inter.shape[0] // CHUNKS
    pairs = count // CHUNKS

    def piece(k):
        span = pl.ds(k * rows, rows)
        return pltpu.make_async_copy(inter_hbm.at[span], inter.at[span], sem.at[k])

    for k in range(CHUNKS):
        piece(k).start()
    copies = (
        pltpu.make_async_copy(integ_hbm, integ, more.at[0]),
        pltpu.make_async_copy(inverse_hbm, inverse, more.at[1]),
    )
    for copy in copies:
        copy.start()

    def arrived(pair, waited):
        need = jnp.maximum(waited, jnp.minimum(pair // pairs + 1, CHUNKS))
        pl.loop(waited, need)(lambda k: piece(k).wait())
        return need

    couple(listed, inter, (here, near_by), total, amps, ahead, behind, arrived)
    for copy in copies:
        copy.wait()

    @pl.loop(0, count)
    def _(p):
        out[p] = integ[p] + COUPLING * total[p]


def early_body(listed, inter, here, near_by, integ, out, total, *scratch):
    couple(listed, inter, (here, near_by), total, *scratch)

    @pl.loop(0, integ.shape[0])
    def _(p):
        out[p] = integ[p] + COUPLING * total[p]


def late_body(listed, inter, other, so_far, inverse, out, total, *scratch):
    couple(listed, inter, (other,), total, *scratch)

    @pl.loop(0, so_far.shape[0])
    def _(p):
        out[p] = ((so_far[p] + COUPLING * total[p]) * inverse[p]).astype(out.dtype)


def last_body(listed, inter, other, so_far, inverse, integ, out, energy, rows, kept, sem, total, *scratch):
    couple(listed, inter, (other,), total, *scratch)
    width = total.shape[1]
    count = so_far.shape[0]

    def result(p):
        return pltpu.make_async_copy(kept.at[p], out.at[p], sem.at[p])

    @pl.loop(0, count)
    def _(p):
        value = (so_far[p] + COUPLING * total[p]) * inverse[p]
        kept[p] = value
        result(p).start()
        rows[pl.ds(p, 1), :] = jnp.sum(integ[p] * value, axis=0, keepdims=True)

    sums = lax.dot_general(
        jnp.ones((8, width), jnp.float32),
        rows[...],
        (((1,), (1,)), ((), ())),
        precision=lax.Precision.HIGHEST,
        preferred_element_type=jnp.float32,
    )
    energy[...] = sums[0:1, :] * (1.0 / (width * width))
    pl.loop(0, count)(lambda p: result(p).wait())


def coupling_scratch(count, width, tables):
    return [
        pltpu.VMEM((count + 1, width, width), jnp.float32),
        pltpu.VMEM((tables * count + 1, width, width), jnp.bfloat16),
        pltpu.VMEM((UNIT, width, 2 * width), jnp.bfloat16),
        pltpu.VMEM((UNIT, width, 2 * width), jnp.bfloat16),
    ]


def opening_part(listed, inter, here, other, integ, inverse):
    count, width, _ = integ.shape
    return call(
        opening_body,
        tuple(jax.ShapeDtypeStruct(x.shape, x.dtype) for x in (integ, inter, integ, inverse)),
        (VMEM,) * 4,
        [SMEM, HBM, VMEM, VMEM, ANY, ANY],
        coupling_scratch(count, width, 2)
        + [pltpu.SemaphoreType.DMA((CHUNKS,)), pltpu.SemaphoreType.DMA((2,))],
        flops=2 * inter.shape[0] * width**3,
        moved=inter.size * 2,
        limit=26,
        name="opening",
    )(listed, inter, here, other, integ, inverse)


def early_part(listed, inter, here, other, integ):
    count, width, _ = integ.shape
    return call(
        early_body,
        jax.ShapeDtypeStruct(integ.shape, jnp.float32),
        VMEM,
        [SMEM, VMEM, VMEM, VMEM, VMEM],
        coupling_scratch(count, width, 2),
        flops=2 * inter.shape[0] * width**3,
        moved=inter.size * 2,
        limit=24,
        name="early",
    )(listed, inter, here, other, integ)


def late_part(listed, inter, other, so_far, inverse):
    count, width, _ = so_far.shape
    return call(
        late_body,
        jax.ShapeDtypeStruct(so_far.shape, jnp.bfloat16),
        VMEM,
        [SMEM, VMEM, VMEM, VMEM, VMEM],
        coupling_scratch(count, width, 1),
        flops=inter.shape[0] * width**3,
        moved=inter.size * 2,
        limit=24,
        name="late",
    )(listed, inter, other, so_far, inverse)


def last_part(listed, inter, other, so_far, inverse, integ):
    count, width, _ = so_far.shape
    return call(
        last_body,
        (
            jax.ShapeDtypeStruct(so_far.shape, jnp.float32),
            jax.ShapeDtypeStruct((1, count), jnp.float32),
        ),
        (ANY, VMEM),
        [SMEM, VMEM, VMEM, VMEM, VMEM, VMEM],
        [
            pltpu.VMEM((count, width), jnp.float32),
            pltpu.VMEM((count, width, width), jnp.float32),
            pltpu.SemaphoreType.DMA((count,)),
        ]
        + coupling_scratch(count, width, 1),
        flops=inter.shape[0] * width**3,
        moved=inter.size * 2,
        limit=24,
        name="last",
    )(listed, inter, other, so_far, inverse, integ)


def shards(
    blocks,
    pair_orbitals,
    block_sizes,
    pno_maps,
    pno_sizes,
    pno_energy,
    pair_shift,
    neighbours,
    intersections,
):
    devices = lax.axis_size("pairs")
    count, wide, width = pno_maps.shape
    orbitals, depth, _ = blocks.shape
    near = neighbours.shape[1]
    scale = 1.0 / math.sqrt(depth)
    beside_perm = [(i, i ^ 1) for i in range(devices)]
    across_perm = []
    for i in range(1, devices - 1, 2):
        across_perm += [(i, i + 1), (i + 1, i)]
    swap_beside = lambda x: lax.ppermute(x, "pairs", beside_perm)
    swap_across = lambda x: lax.ppermute(x, "pairs", across_perm)

    inter = intersections.reshape(count * near, width, width)
    table, branch = plan(pair_orbitals, block_sizes, orbitals)

    def after(value, *before):
        return lax.optimization_barrier((value,) + before)[0]

    def integrals_with(slots):
        def run(table, blocks, maps, energy, shift, sizes, near_pairs):
            blocks_beside = swap_beside(blocks)
            packed = pack(table, maps, (slots - slots // 2, slots // 2), orbitals)
            got = [swap_across(x) for x in packed]
            left = left_part(table, blocks, maps)
            half_one = serve(after(table, left), blocks, got[0], 0, count)
            back_one = swap_across(half_one)
            integ, start, inverse, early, late = own_part(
                after(table, half_one), sizes, shift, near_pairs, blocks, maps, energy, left, scale
            )
            half_two = serve(after(table, early), blocks, got[1], got[0].shape[0], count)
            back_two = swap_across(half_two)
            integ, start = integrals_part(
                functools.partial(beside_body, scale),
                after(table, half_two),
                (blocks_beside, maps),
                left,
                inverse,
                integ,
                start,
                [],
                24,
                "beside",
            )
            integ, start = integrals_part(
                functools.partial(across_body, scale, orbitals),
                table,
                (back_one, back_two),
                left,
                inverse,
                integ,
                start,
                [pltpu.VMEM((slots, depth, width), jnp.bfloat16)],
                24,
                "across",
            )
            return integ, start, inverse, early, late

        return run

    integ, amps, inverse, early, late = lax.switch(
        branch[0],
        [integrals_with(s) for s in SLOTS],
        table,
        blocks,
        pno_maps,
        pno_energy,
        pair_shift,
        pno_sizes,
        neighbours.T,
    )
    for iteration in range(ITERS):
        far = swap_across(amps)
        close = swap_beside(amps)
        if iteration == 0:
            stay = pltpu.with_memory_space_constraint(inter, pltpu.HBM)
            so_far, inter, integ, inverse = opening_part(early, stay, amps, close, integ, inverse)
        else:
            so_far = early_part(early, inter, amps, close, integ)
        if iteration < ITERS - 1:
            amps = late_part(late, inter, far, so_far, inverse)
        else:
            amps, energies = last_part(late, inter, far, so_far, inverse, integ)
    return (amps, energies.reshape(count))


def solution(mesh):
    in_specs = (
        P("pairs", None, None),
        P(),
        P(),
        P("pairs", None, None),
        P("pairs"),
        P("pairs", None),
        P("pairs"),
        P("pairs", None),
        P("pairs", None, None, None),
    )
    out_specs = (P("pairs", None, None), P("pairs"))
    return jax.shard_map(shards, mesh=mesh, in_specs=in_specs, out_specs=out_specs, check_vma=False)
```

```python
import functools
import math

import jax
import jax.numpy as jnp
from jax import lax
from jax.experimental import pallas as pl
from jax.experimental.pallas import tpu as pltpu
from jax.sharding import PartitionSpec as P

ITERS = 2
COUPLING = 0.35
SLOTS = (17, 18, 19, 20, 24, 32)

ANY = pl.BlockSpec(memory_space=pl.ANY)
HBM = pl.BlockSpec(memory_space=pltpu.HBM)
VMEM = pl.BlockSpec(memory_space=pltpu.VMEM)
SMEM = pl.BlockSpec(memory_space=pltpu.SMEM)

ONE, SRC, SERVE, LIVE = 0, 32, 64, 96


def call(body, outs, out_specs, in_specs, scratch, flops=0, moved=0, limit=60, aliases=None, name=None):
    return pl.pallas_call(
        body,
        out_shape=outs,
        in_specs=in_specs,
        out_specs=out_specs,
        scratch_shapes=scratch,
        input_output_aliases=aliases or {},
        compiler_params=pltpu.CompilerParams(vmem_limit_bytes=limit * 1024 * 1024),
        cost_estimate=pl.CostEstimate(flops=int(flops), bytes_accessed=int(moved), transcendentals=0),
        name=name,
    )


def dot(left, right):
    return jnp.dot(left, right, preferred_element_type=jnp.float32)


def dot_nt(left, right):
    return lax.dot_general(left, right, (((1,), (1,)), ((), ())), preferred_element_type=jnp.float32)


def dot_tn_nt(left, right):
    return lax.dot_general(left, right, (((0,), (1,)), ((), ())), preferred_element_type=jnp.float32)


def collect(count, wanted, slots, begin=None):
    def step(index, found):
        chosen = wanted(index)
        slots[found] = index
        if begin is not None:
            pl.when(chosen)(lambda: begin(index, found))
        return found + chosen.astype(jnp.int32)

    return lax.fori_loop(0, count, step, jnp.int32(0))


def by_twos(number, work, store):
    @pl.loop(0, (number + 1) // 2)
    def _(step):
        both = (2 * step, jnp.minimum(2 * step + 1, number - 1))
        done = [work(k) for k in both]
        for k, values in zip(both, done):
            store(k, values)


def plan_body(orbitals, pairs_hbm, sizes_hbm, table, branch, everyone, sizes, mine, theirs, sem):
    count = mine.shape[1] // 4
    lanes = mine.shape[1]
    devices = everyone.shape[1] // count
    device = lax.axis_index("pairs")
    side = 2 * (device % 2) - 1
    partner = device + side
    valid = (partner >= 0) & (partner < devices)
    near_by = jnp.clip(partner, 0, devices - 1)

    def fetch(who, place, k):
        start = pl.multiple_of(who // 4 * lanes, lanes)
        return pltpu.make_async_copy(pairs_hbm.at[:, pl.ds(start, lanes)], place, sem.at[k])

    copies = (
        fetch(device, mine, 0),
        fetch(near_by, theirs, 1),
        pltpu.make_async_copy(sizes_hbm, sizes, sem.at[3]),
    )
    whole = pltpu.make_async_copy(pairs_hbm, everyone, sem.at[2])
    whole.start()
    for copy in copies:
        copy.start()
    whole.wait()

    groups = devices * count // lanes
    second = jnp.concatenate([everyone[1:2, g * lanes : (g + 1) * lanes] for g in range(groups)], axis=0)
    row = lax.broadcasted_iota(jnp.int32, (groups, lanes), 0)
    lane = lax.broadcasted_iota(jnp.int32, (groups, lanes), 1)
    owner = row * (lanes // count) + lane // count
    crossing = jnp.where(second // orbitals == owner + 2 * (owner % 2) - 1, 1.0, 0.0)
    from_lane = lax.broadcasted_iota(jnp.int32, (lanes, lanes), 0) // count
    to_lane = lax.broadcasted_iota(jnp.int32, (lanes, lanes), 1)
    together = jnp.where(from_lane == to_lane, 1.0, 0.0).astype(jnp.bfloat16)
    most = jnp.max(dot(crossing.astype(jnp.bfloat16), together)).astype(jnp.int32)
    branch[0] = sum((most > s).astype(jnp.int32) for s in SLOTS[:-1])

    for copy in copies:
        copy.wait()
    base = device * orbitals
    here = device % 4 * count
    there = near_by % 4 * count

    @pl.loop(0, count)
    def _(p):
        first = mine[0, here + p]
        second = mine[1, here + p]
        local = second - base
        offset = (local >= orbitals).astype(jnp.int32) - (local < 0).astype(jnp.int32)
        kind = jnp.where(offset == 0, 0, jnp.where(offset == side, 2, 1))
        table[ONE + p] = first - base
        table[SRC + p] = kind * orbitals + local - offset * orbitals
        table[SERVE + p] = jnp.where(valid, theirs[1, there + p] - base, -1)
        table[LIVE + p] = jnp.minimum(sizes[first], sizes[second])


def plan(pair_orbitals, block_sizes, orbitals):
    turned = pair_orbitals.T
    return call(
        functools.partial(plan_body, orbitals),
        (jax.ShapeDtypeStruct((128,), jnp.int32), jax.ShapeDtypeStruct((1,), jnp.int32)),
        (SMEM, SMEM),
        [HBM, HBM],
        [
            pltpu.VMEM(turned.shape, jnp.int32),
            pltpu.SMEM(block_sizes.shape, jnp.int32),
            pltpu.SMEM((2, 128), jnp.int32),
            pltpu.SMEM((2, 128), jnp.int32),
            pltpu.SemaphoreType.DMA((4,)),
        ],
        moved=turned.size * 8,
        limit=4,
        name="plan",
    )(
        pltpu.with_memory_space_constraint(turned, pltpu.HBM),
        pltpu.with_memory_space_constraint(block_sizes, pltpu.HBM),
    )


def pack_body(orbitals, table, maps, *refs):
    outs, slots, sem = refs[:-2], refs[-2], refs[-1]
    count = maps.shape[0]

    def begin(pair, slot):
        low = 0
        for out in outs:
            lo, hi = low, low + out.shape[0]

            @pl.when((slot >= lo) & (slot < hi))
            def _(out=out, lo=lo):
                pltpu.make_async_copy(maps.at[pair], out.at[slot - lo], sem.at[slot]).start()

            low = hi

    found = collect(count, lambda p: table[SRC + p] >= 2 * orbitals, slots, begin)

    @pl.loop(0, found)
    def _(slot):
        pltpu.make_async_copy(maps.at[0], outs[0].at[0], sem.at[slot]).wait()


def pack(table, maps, sizes, orbitals):
    count, depth, width = maps.shape
    return call(
        functools.partial(pack_body, orbitals),
        tuple(jax.ShapeDtypeStruct((s, depth, width), maps.dtype) for s in sizes),
        (VMEM,) * len(sizes),
        [SMEM, ANY],
        [pltpu.SMEM((count + 1,), jnp.int32), pltpu.SemaphoreType.DMA((count,))],
        moved=2 * sum(sizes) * depth * width * 2,
        limit=8,
        name="pack",
    )(table, maps)


def left_body(table, blocks, maps, left):
    count, width, depth = left.shape
    columns = lax.broadcasted_iota(jnp.int32, (width, depth), 1)

    def work(p):
        half = dot_tn_nt(maps[p], blocks[table[ONE + p]])
        return jnp.where(columns < table[LIVE + p], half, 0.0).astype(jnp.bfloat16)

    def store(p, half):
        left[p] = half

    by_twos(count, work, store)


def left_part(table, blocks, maps):
    orbitals, depth, wide = blocks.shape
    count, _, width = maps.shape
    return call(
        left_body,
        jax.ShapeDtypeStruct((count, width, depth), jnp.bfloat16),
        VMEM,
        [SMEM, VMEM, VMEM],
        [],
        flops=2 * count * depth * wide * width,
        moved=blocks.size * 2,
        limit=20,
        name="left",
    )(table, blocks, maps)


def prepare_body(table, sizes, shift, near_pairs, energy, inverse, early, late):
    count, width, _ = inverse.shape
    near = near_pairs.shape[0]
    device = lax.axis_index("pairs")
    side = 2 * (device % 2) - 1
    ids = lax.broadcasted_iota(jnp.int32, (width, width), 0)
    across_ids = lax.broadcasted_iota(jnp.int32, (width, width), 1)

    def pair_step(pair, counts):
        soon, after = counts
        for k in range(near):
            entry = pair * near + k
            local = near_pairs[k, pair] - device * count
            offset = (local >= count).astype(jnp.int32) - (local < 0).astype(jnp.int32)
            is_late = (offset == side).astype(jnp.int32)
            code = pair * 65536 + entry * 256 + local - offset * count
            early[1 + soon] = code + jnp.where(offset == 0, 0, count)
            late[1 + after] = code
            soon = soon + 1 - is_late
            after = after + is_late
        spare = pair * 65536 + pair * near * 256
        early[1 + soon] = spare + 2 * count
        late[1 + after] = spare + count
        row = jnp.broadcast_to(energy[pl.ds(pair, 1), :], (width, width))
        bottom = row + row.T + shift[pair]
        size = sizes[pair]
        inverse[pair] = jnp.where((ids < size) & (across_ids < size), -1.0 / bottom, 0.0)
        return soon + soon % 2, after + after % 2

    soon, after = lax.fori_loop(0, count, pair_step, (jnp.int32(0), jnp.int32(0)))
    early[0] = soon // 2
    late[0] = after // 2

    @pl.loop(0, 6 * UNIT)
    def _(k):
        early[1 + soon + k] = count * 65536 + 2 * count
        late[1 + after + k] = count * 65536 + count


def prepare(table, sizes, shift, near_pairs, energy):
    count, width = energy.shape
    entries = near_pairs.size + 6 * UNIT + 8
    return call(
        prepare_body,
        (
            jax.ShapeDtypeStruct((count, width, width), jnp.float32),
            jax.ShapeDtypeStruct((entries,), jnp.int32),
            jax.ShapeDtypeStruct((entries,), jnp.int32),
        ),
        (VMEM, SMEM, SMEM),
        [SMEM, SMEM, SMEM, SMEM, VMEM],
        [],
        flops=count * width * width * 10,
        moved=count * width * width * 4,
        limit=8,
        name="prepare",
    )(table, sizes, shift, near_pairs, energy)


def own_body(scale, orbitals, table, blocks, maps, left, inverse, integ, start, slots):
    count = left.shape[0]
    found = collect(count, lambda p: table[SRC + p] < orbitals, slots)

    def work(slot):
        pair = slots[slot]
        right = dot(blocks[table[SRC + pair]], maps[pair]).astype(jnp.bfloat16)
        return dot(left[pair], right) * scale

    def store(slot, value):
        pair = slots[slot]
        integ[pair] = value
        start[pair] = (value * inverse[pair]).astype(jnp.bfloat16)

    by_twos(found, work, store)


def own_part(table, blocks, maps, left, inverse, scale):
    orbitals = blocks.shape[0]
    count, width, depth = left.shape
    return call(
        functools.partial(own_body, scale, orbitals),
        (
            jax.ShapeDtypeStruct((count, width, width), jnp.float32),
            jax.ShapeDtypeStruct((count, width, width), jnp.bfloat16),
        ),
        (VMEM, VMEM),
        [SMEM, VMEM, VMEM, VMEM, VMEM],
        [pltpu.SMEM((count + 1,), jnp.int32)],
        flops=count * depth * depth * width,
        moved=blocks.size * 2,
        limit=24,
        name="own",
    )(table, blocks, maps, left, inverse)


def serve_body(low, table, blocks, maps, out, slots):
    orbitals = blocks.shape[0]
    size = maps.shape[0]
    found = collect(
        slots.shape[0] - 1,
        lambda p: (table[SERVE + p] >= 0) & (table[SERVE + p] < orbitals),
        slots,
    )

    def work(slot):
        return dot(blocks[table[SERVE + slots[low + slot]]], maps[slot]).astype(jnp.bfloat16)

    def store(slot, half):
        out[slot] = half

    by_twos(jnp.clip(found - low, 0, size), work, store)


def serve(table, blocks, maps, low, count):
    orbitals, depth, wide = blocks.shape
    size, _, width = maps.shape
    return call(
        functools.partial(serve_body, low),
        jax.ShapeDtypeStruct((size, depth, width), jnp.bfloat16),
        VMEM,
        [SMEM, VMEM, VMEM],
        [pltpu.SMEM((count + 1,), jnp.int32)],
        flops=2 * size * depth * wide * width,
        moved=size * depth * (wide + 2 * width) * 2,
        limit=20,
        name="serve",
    )(table, blocks, maps)


def carry_over(integ_in, start_in, integ, start):
    @pl.loop(0, integ.shape[0])
    def _(p):
        integ[p] = integ_in[p]
        start[p] = start_in[p]


def beside_body(scale, table, blocks, maps, left, inverse, integ_in, start_in, integ, start, slots):
    carry_over(integ_in, start_in, integ, start)
    orbitals = blocks.shape[0]
    found = collect(
        left.shape[0],
        lambda p: (table[SRC + p] >= orbitals) & (table[SRC + p] < 2 * orbitals),
        slots,
    )

    def work(slot):
        pair = slots[slot]
        right = dot(blocks[table[SRC + pair] - orbitals], maps[pair]).astype(jnp.bfloat16)
        return dot(left[pair], right) * scale

    def store(slot, value):
        pair = slots[slot]
        integ[pair] = value
        start[pair] = (value * inverse[pair]).astype(jnp.bfloat16)

    by_twos(found, work, store)


def across_body(scale, orbitals, table, *refs):
    n = len(refs) - 7
    halves = refs[:n]
    left, inverse, integ_in, start_in, integ, start, slots = refs[n:]
    carry_over(integ_in, start_in, integ, start)
    found = collect(left.shape[0], lambda p: table[SRC + p] >= 2 * orbitals, slots)
    low = 0
    for half in halves:

        def work(slot, half=half, low=low):
            return dot(left[slots[low + slot]], half[slot]) * scale

        def store(slot, value, low=low):
            pair = slots[low + slot]
            integ[pair] = value
            start[pair] = (value * inverse[pair]).astype(jnp.bfloat16)

        by_twos(jnp.clip(found - low, 0, half.shape[0]), work, store)
        low += half.shape[0]


def integrals_part(body, table, operands, left, inverse, integ, start, scratch, limit, name):
    count, width, depth = left.shape
    n = len(operands)
    return call(
        body,
        (
            jax.ShapeDtypeStruct(integ.shape, integ.dtype),
            jax.ShapeDtypeStruct(start.shape, start.dtype),
        ),
        (VMEM, VMEM),
        [SMEM] + [VMEM] * (n + 4),
        scratch + [pltpu.SMEM((count + 1,), jnp.int32)],
        flops=count * depth * depth * width,
        moved=count * depth * width * 2,
        limit=limit,
        name=name,
    )(table, *operands, left, inverse, integ, start)


CHUNKS = 8
UNIT = 4


def couple(listed, inter, tables, total, amps, ahead, behind, arrived=None):
    count = total.shape[0] - 1
    width = total.shape[1]
    low = 0
    for table in tables:
        amps[pl.ds(low, table.shape[0])] = table[...]
        low += table.shape[0]
    amps[low] = jnp.zeros(amps.shape[1:], amps.dtype)

    @pl.loop(0, count + 1)
    def _(p):
        total[p] = jnp.zeros(total.shape[1:], jnp.float32)

    def codes(group):
        for k in range(UNIT):
            place = 1 + (group * UNIT + k) * 2
            one, two = listed[place], listed[place + 1]
            yield k, one // 65536, (one // 256) % 256, one % 256, (two // 256) % 256, two % 256

    def first(group, mixed):
        for k, _, one, amp_one, two, amp_two in codes(group):
            mixed[k, :, 0:width] = dot(inter[one], amps[amp_one]).astype(jnp.bfloat16)
            mixed[k, :, width : 2 * width] = dot(inter[two], amps[amp_two]).astype(jnp.bfloat16)

    def second(group, mixed):
        for k, pair, one, _, two, _ in codes(group):
            total[pair] += dot_nt(mixed[k], jnp.concatenate([inter[one], inter[two]], axis=1))

    def ready(group, waited):
        if arrived is None:
            return waited
        return arrived(listed[2 * (group + 1) * UNIT] // 65536, waited)

    waited = ready(0, jnp.int32(0))
    first(0, ahead)

    def step(k, waited):
        waited = ready(2 * k + 2, waited)
        first(2 * k + 1, behind)
        second(2 * k, ahead)
        first(2 * k + 2, ahead)
        second(2 * k + 1, behind)
        return waited

    waited = lax.fori_loop(0, (listed[0] + 2 * UNIT - 1) // (2 * UNIT), step, waited)
    if arrived is not None:
        arrived(total.shape[0] - 1, waited)


def opening_body(listed, inter_hbm, here, near_by, integ_hbm, inverse_hbm,
                 out, inter, integ, inverse, total, amps, ahead, behind, sem, more):
    count = integ.shape[0]
    rows = inter.shape[0] // CHUNKS
    pairs = count // CHUNKS

    def piece(k):
        span = pl.ds(k * rows, rows)
        return pltpu.make_async_copy(inter_hbm.at[span], inter.at[span], sem.at[k])

    for k in range(CHUNKS):
        piece(k).start()
    copies = (
        pltpu.make_async_copy(integ_hbm, integ, more.at[0]),
        pltpu.make_async_copy(inverse_hbm, inverse, more.at[1]),
    )
    for copy in copies:
        copy.start()

    def arrived(pair, waited):
        need = jnp.maximum(waited, jnp.minimum(pair // pairs + 1, CHUNKS))
        pl.loop(waited, need)(lambda k: piece(k).wait())
        return need

    couple(listed, inter, (here, near_by), total, amps, ahead, behind, arrived)
    for copy in copies:
        copy.wait()

    @pl.loop(0, count)
    def _(p):
        out[p] = integ[p] + COUPLING * total[p]


def early_body(listed, inter, here, near_by, integ, out, total, *scratch):
    couple(listed, inter, (here, near_by), total, *scratch)

    @pl.loop(0, integ.shape[0])
    def _(p):
        out[p] = integ[p] + COUPLING * total[p]


def late_body(listed, inter, other, so_far, inverse, out, total, *scratch):
    couple(listed, inter, (other,), total, *scratch)

    @pl.loop(0, so_far.shape[0])
    def _(p):
        out[p] = ((so_far[p] + COUPLING * total[p]) * inverse[p]).astype(out.dtype)


def last_body(listed, inter, other, so_far, inverse, integ, out, energy, rows, kept, sem, total, *scratch):
    couple(listed, inter, (other,), total, *scratch)
    width = total.shape[1]
    count = so_far.shape[0]

    def result(p):
        return pltpu.make_async_copy(kept.at[p], out.at[p], sem.at[p])

    @pl.loop(0, count)
    def _(p):
        value = (so_far[p] + COUPLING * total[p]) * inverse[p]
        kept[p] = value
        result(p).start()
        rows[pl.ds(p, 1), :] = jnp.sum(integ[p] * value, axis=0, keepdims=True)

    sums = lax.dot_general(
        jnp.ones((8, width), jnp.float32),
        rows[...],
        (((1,), (1,)), ((), ())),
        precision=lax.Precision.HIGHEST,
        preferred_element_type=jnp.float32,
    )
    energy[...] = sums[0:1, :] * (1.0 / (width * width))
    pl.loop(0, count)(lambda p: result(p).wait())


def coupling_scratch(count, width, tables):
    return [
        pltpu.VMEM((count + 1, width, width), jnp.float32),
        pltpu.VMEM((tables * count + 1, width, width), jnp.bfloat16),
        pltpu.VMEM((UNIT, width, 2 * width), jnp.bfloat16),
        pltpu.VMEM((UNIT, width, 2 * width), jnp.bfloat16),
    ]


def opening_part(listed, inter, here, other, integ, inverse):
    count, width, _ = integ.shape
    return call(
        opening_body,
        tuple(jax.ShapeDtypeStruct(x.shape, x.dtype) for x in (integ, inter, integ, inverse)),
        (VMEM,) * 4,
        [SMEM, HBM, VMEM, VMEM, ANY, ANY],
        coupling_scratch(count, width, 2)
        + [pltpu.SemaphoreType.DMA((CHUNKS,)), pltpu.SemaphoreType.DMA((2,))],
        flops=2 * inter.shape[0] * width**3,
        moved=inter.size * 2,
        limit=26,
        name="opening",
    )(listed, inter, here, other, integ, inverse)


def early_part(listed, inter, here, other, integ):
    count, width, _ = integ.shape
    return call(
        early_body,
        jax.ShapeDtypeStruct(integ.shape, jnp.float32),
        VMEM,
        [SMEM, VMEM, VMEM, VMEM, VMEM],
        coupling_scratch(count, width, 2),
        flops=2 * inter.shape[0] * width**3,
        moved=inter.size * 2,
        limit=24,
        name="early",
    )(listed, inter, here, other, integ)


def late_part(listed, inter, other, so_far, inverse):
    count, width, _ = so_far.shape
    return call(
        late_body,
        jax.ShapeDtypeStruct(so_far.shape, jnp.bfloat16),
        VMEM,
        [SMEM, VMEM, VMEM, VMEM, VMEM],
        coupling_scratch(count, width, 1),
        flops=inter.shape[0] * width**3,
        moved=inter.size * 2,
        limit=24,
        name="late",
    )(listed, inter, other, so_far, inverse)


def last_part(listed, inter, other, so_far, inverse, integ):
    count, width, _ = so_far.shape
    return call(
        last_body,
        (
            jax.ShapeDtypeStruct(so_far.shape, jnp.float32),
            jax.ShapeDtypeStruct((1, count), jnp.float32),
        ),
        (ANY, VMEM),
        [SMEM, VMEM, VMEM, VMEM, VMEM, VMEM],
        [
            pltpu.VMEM((count, width), jnp.float32),
            pltpu.VMEM((count, width, width), jnp.float32),
            pltpu.SemaphoreType.DMA((count,)),
        ]
        + coupling_scratch(count, width, 1),
        flops=inter.shape[0] * width**3,
        moved=inter.size * 2,
        limit=24,
        name="last",
    )(listed, inter, other, so_far, inverse, integ)


def shards(
    blocks,
    pair_orbitals,
    block_sizes,
    pno_maps,
    pno_sizes,
    pno_energy,
    pair_shift,
    neighbours,
    intersections,
):
    devices = lax.axis_size("pairs")
    count, wide, width = pno_maps.shape
    orbitals, depth, _ = blocks.shape
    near = neighbours.shape[1]
    scale = 1.0 / math.sqrt(depth)
    beside_perm = [(i, i ^ 1) for i in range(devices)]
    across_perm = []
    for i in range(1, devices - 1, 2):
        across_perm += [(i, i + 1), (i + 1, i)]
    swap_beside = lambda x: lax.ppermute(x, "pairs", beside_perm)
    swap_across = lambda x: lax.ppermute(x, "pairs", across_perm)

    inter = intersections.reshape(count * near, width, width)
    table, branch = plan(pair_orbitals, block_sizes, orbitals)

    def after(value, *before):
        return lax.optimization_barrier((value,) + before)[0]

    def integrals_with(slots):
        def run(table, blocks, maps, energy, shift, sizes, near_pairs):
            blocks_beside = swap_beside(blocks)
            packed = pack(table, maps, (slots - slots // 2, slots // 2), orbitals)
            got = [swap_across(x) for x in packed]
            left = left_part(table, blocks, maps)
            half_one = serve(after(table, left), blocks, got[0], 0, count)
            back_one = swap_across(half_one)
            inverse, early, late = prepare(after(table, half_one), sizes, shift, near_pairs, energy)
            half_two = serve(after(table, early), blocks, got[1], got[0].shape[0], count)
            back_two = swap_across(half_two)
            integ, start = own_part(after(table, half_two), blocks, maps, left, inverse, scale)
            integ, start = integrals_part(
                functools.partial(beside_body, scale),
                after(table, start),
                (blocks_beside, maps),
                left,
                inverse,
                integ,
                start,
                [],
                24,
                "beside",
            )
            integ, start = integrals_part(
                functools.partial(across_body, scale, orbitals),
                table,
                (back_one, back_two),
                left,
                inverse,
                integ,
                start,
                [],
                24,
                "across",
            )
            return integ, start, inverse, early, late

        return run

    integ, amps, inverse, early, late = lax.switch(
        branch[0],
        [integrals_with(s) for s in SLOTS],
        table,
        blocks,
        pno_maps,
        pno_energy,
        pair_shift,
        pno_sizes,
        neighbours.T,
    )
    for iteration in range(ITERS):
        far = swap_across(amps)
        close = swap_beside(amps)
        if iteration == 0:
            stay = pltpu.with_memory_space_constraint(inter, pltpu.HBM)
            so_far, inter, integ, inverse = opening_part(early, stay, amps, close, integ, inverse)
        else:
            so_far = early_part(early, inter, amps, close, integ)
        if iteration < ITERS - 1:
            amps = late_part(late, inter, far, so_far, inverse)
        else:
            amps, energies = last_part(late, inter, far, so_far, inverse, integ)
    return (amps, energies.reshape(count))


def solution(mesh):
    in_specs = (
        P("pairs", None, None),
        P(),
        P(),
        P("pairs", None, None),
        P("pairs"),
        P("pairs", None),
        P("pairs"),
        P("pairs", None),
        P("pairs", None, None, None),
    )
    out_specs = (P("pairs", None, None), P("pairs"))
    return jax.shard_map(shards, mesh=mesh, in_specs=in_specs, out_specs=out_specs, check_vma=False)
```

```python
import functools
import math

import jax
import jax.numpy as jnp
from jax import lax
from jax.experimental import pallas as pl
from jax.experimental.pallas import tpu as pltpu
from jax.sharding import PartitionSpec as P

ITERS = 2
COUPLING = 0.35
SLOTS = (17, 18, 19, 20, 24, 32)

ANY = pl.BlockSpec(memory_space=pl.ANY)
HBM = pl.BlockSpec(memory_space=pltpu.HBM)
VMEM = pl.BlockSpec(memory_space=pltpu.VMEM)
SMEM = pl.BlockSpec(memory_space=pltpu.SMEM)

ONE, SRC, SERVE, LIVE = 0, 32, 64, 96


def call(body, outs, out_specs, in_specs, scratch, flops=0, moved=0, limit=60, aliases=None, name=None):
    return pl.pallas_call(
        body,
        out_shape=outs,
        in_specs=in_specs,
        out_specs=out_specs,
        scratch_shapes=scratch,
        input_output_aliases=aliases or {},
        compiler_params=pltpu.CompilerParams(vmem_limit_bytes=limit * 1024 * 1024),
        cost_estimate=pl.CostEstimate(flops=int(flops), bytes_accessed=int(moved), transcendentals=0),
        name=name,
    )


def dot(left, right):
    return jnp.dot(left, right, preferred_element_type=jnp.float32)


def dot_nt(left, right):
    return lax.dot_general(left, right, (((1,), (1,)), ((), ())), preferred_element_type=jnp.float32)


def dot_tn_nt(left, right):
    return lax.dot_general(left, right, (((0,), (1,)), ((), ())), preferred_element_type=jnp.float32)


def collect(count, wanted, slots, begin=None):
    def step(index, found):
        chosen = wanted(index)
        slots[found] = index
        if begin is not None:
            pl.when(chosen)(lambda: begin(index, found))
        return found + chosen.astype(jnp.int32)

    return lax.fori_loop(0, count, step, jnp.int32(0))


def by_twos(number, work, store):
    @pl.loop(0, (number + 1) // 2)
    def _(step):
        both = (2 * step, jnp.minimum(2 * step + 1, number - 1))
        done = [work(k) for k in both]
        for k, values in zip(both, done):
            store(k, values)


def plan_body(orbitals, pairs_hbm, sizes_hbm, table, branch, everyone, sizes, mine, theirs, sem):
    count = mine.shape[1] // 4
    lanes = mine.shape[1]
    devices = everyone.shape[1] // count
    device = lax.axis_index("pairs")
    side = 2 * (device % 2) - 1
    partner = device + side
    valid = (partner >= 0) & (partner < devices)
    near_by = jnp.clip(partner, 0, devices - 1)

    def fetch(who, place, k):
        start = pl.multiple_of(who // 4 * lanes, lanes)
        return pltpu.make_async_copy(pairs_hbm.at[:, pl.ds(start, lanes)], place, sem.at[k])

    copies = (
        fetch(device, mine, 0),
        fetch(near_by, theirs, 1),
        pltpu.make_async_copy(sizes_hbm, sizes, sem.at[3]),
    )
    whole = pltpu.make_async_copy(pairs_hbm, everyone, sem.at[2])
    whole.start()
    for copy in copies:
        copy.start()
    whole.wait()

    groups = devices * count // lanes
    second = jnp.concatenate([everyone[1:2, g * lanes : (g + 1) * lanes] for g in range(groups)], axis=0)
    row = lax.broadcasted_iota(jnp.int32, (groups, lanes), 0)
    lane = lax.broadcasted_iota(jnp.int32, (groups, lanes), 1)
    owner = row * (lanes // count) + lane // count
    crossing = jnp.where(second // orbitals == owner + 2 * (owner % 2) - 1, 1.0, 0.0)
    from_lane = lax.broadcasted_iota(jnp.int32, (lanes, lanes), 0) // count
    to_lane = lax.broadcasted_iota(jnp.int32, (lanes, lanes), 1)
    together = jnp.where(from_lane == to_lane, 1.0, 0.0).astype(jnp.bfloat16)
    most = jnp.max(dot(crossing.astype(jnp.bfloat16), together)).astype(jnp.int32)
    branch[0] = sum((most > s).astype(jnp.int32) for s in SLOTS[:-1])

    for copy in copies:
        copy.wait()
    base = device * orbitals
    here = device % 4 * count
    there = near_by % 4 * count

    @pl.loop(0, count)
    def _(p):
        first = mine[0, here + p]
        second = mine[1, here + p]
        local = second - base
        offset = (local >= orbitals).astype(jnp.int32) - (local < 0).astype(jnp.int32)
        kind = jnp.where(offset == 0, 0, jnp.where(offset == side, 2, 1))
        table[ONE + p] = first - base
        table[SRC + p] = kind * orbitals + local - offset * orbitals
        table[SERVE + p] = jnp.where(valid, theirs[1, there + p] - base, -1)
        table[LIVE + p] = jnp.minimum(sizes[first], sizes[second])


def plan(pair_orbitals, block_sizes, orbitals):
    turned = pair_orbitals.T
    return call(
        functools.partial(plan_body, orbitals),
        (jax.ShapeDtypeStruct((128,), jnp.int32), jax.ShapeDtypeStruct((1,), jnp.int32)),
        (SMEM, SMEM),
        [HBM, HBM],
        [
            pltpu.VMEM(turned.shape, jnp.int32),
            pltpu.SMEM(block_sizes.shape, jnp.int32),
            pltpu.SMEM((2, 128), jnp.int32),
            pltpu.SMEM((2, 128), jnp.int32),
            pltpu.SemaphoreType.DMA((4,)),
        ],
        moved=turned.size * 8,
        limit=4,
        name="plan",
    )(
        pltpu.with_memory_space_constraint(turned, pltpu.HBM),
        pltpu.with_memory_space_constraint(block_sizes, pltpu.HBM),
    )


def pack_body(orbitals, table, maps, *refs):
    outs, slots, sem = refs[:-2], refs[-2], refs[-1]
    count = maps.shape[0]

    def begin(pair, slot):
        low = 0
        for out in outs:
            lo, hi = low, low + out.shape[0]

            @pl.when((slot >= lo) & (slot < hi))
            def _(out=out, lo=lo):
                pltpu.make_async_copy(maps.at[pair], out.at[slot - lo], sem.at[slot]).start()

            low = hi

    found = collect(count, lambda p: table[SRC + p] >= 2 * orbitals, slots, begin)

    @pl.loop(0, found)
    def _(slot):
        pltpu.make_async_copy(maps.at[0], outs[0].at[0], sem.at[slot]).wait()


def pack(table, maps, sizes, orbitals):
    count, depth, width = maps.shape
    return call(
        functools.partial(pack_body, orbitals),
        tuple(jax.ShapeDtypeStruct((s, depth, width), maps.dtype) for s in sizes),
        (VMEM,) * len(sizes),
        [SMEM, ANY],
        [pltpu.SMEM((count + 1,), jnp.int32), pltpu.SemaphoreType.DMA((count,))],
        moved=2 * sum(sizes) * depth * width * 2,
        limit=8,
        name="pack",
    )(table, maps)


def left_body(table, blocks, maps, left):
    count, width, depth = left.shape
    columns = lax.broadcasted_iota(jnp.int32, (width, depth), 1)

    def work(p):
        half = dot_tn_nt(maps[p], blocks[table[ONE + p]])
        return jnp.where(columns < table[LIVE + p], half, 0.0).astype(jnp.bfloat16)

    def store(p, half):
        left[p] = half

    by_twos(count, work, store)


def left_part(table, blocks, maps):
    orbitals, depth, wide = blocks.shape
    count, _, width = maps.shape
    return call(
        left_body,
        jax.ShapeDtypeStruct((count, width, depth), jnp.bfloat16),
        VMEM,
        [SMEM, VMEM, VMEM],
        [],
        flops=2 * count * depth * wide * width,
        moved=blocks.size * 2,
        limit=20,
        name="left",
    )(table, blocks, maps)


def prepare_body(table, sizes, shift, near_pairs, energy, inverse, early, late):
    count, width, _ = inverse.shape
    near = near_pairs.shape[0]
    device = lax.axis_index("pairs")
    side = 2 * (device % 2) - 1
    ids = lax.broadcasted_iota(jnp.int32, (width, width), 0)
    across_ids = lax.broadcasted_iota(jnp.int32, (width, width), 1)

    def pair_step(pair, counts):
        soon, after = counts
        for k in range(near):
            entry = pair * near + k
            local = near_pairs[k, pair] - device * count
            offset = (local >= count).astype(jnp.int32) - (local < 0).astype(jnp.int32)
            is_late = (offset == side).astype(jnp.int32)
            code = pair * 65536 + entry * 256 + local - offset * count
            early[1 + soon] = code + jnp.where(offset == 0, 0, count)
            late[1 + after] = code
            soon = soon + 1 - is_late
            after = after + is_late
        spare = pair * 65536 + pair * near * 256
        early[1 + soon] = spare + 2 * count
        late[1 + after] = spare + count
        row = jnp.broadcast_to(energy[pl.ds(pair, 1), :], (width, width))
        bottom = row + row.T + shift[pair]
        size = sizes[pair]
        inverse[pair] = jnp.where((ids < size) & (across_ids < size), -1.0 / bottom, 0.0)
        return soon + soon % 2, after + after % 2

    soon, after = lax.fori_loop(0, count, pair_step, (jnp.int32(0), jnp.int32(0)))
    early[0] = soon // 2
    late[0] = after // 2

    @pl.loop(0, 6 * UNIT)
    def _(k):
        early[1 + soon + k] = count * 65536 + 2 * count
        late[1 + after + k] = count * 65536 + count


def prepare(table, sizes, shift, near_pairs, energy):
    count, width = energy.shape
    entries = near_pairs.size + 6 * UNIT + 8
    return call(
        prepare_body,
        (
            jax.ShapeDtypeStruct((count, width, width), jnp.float32),
            jax.ShapeDtypeStruct((entries,), jnp.int32),
            jax.ShapeDtypeStruct((entries,), jnp.int32),
        ),
        (VMEM, SMEM, SMEM),
        [SMEM, SMEM, SMEM, SMEM, VMEM],
        [],
        flops=count * width * width * 10,
        moved=count * width * width * 4,
        limit=8,
        name="prepare",
    )(table, sizes, shift, near_pairs, energy)


def own_body(scale, orbitals, table, blocks, maps, left, inverse, integ, start, slots):
    count = left.shape[0]
    found = collect(count, lambda p: table[SRC + p] < orbitals, slots)

    def work(slot):
        pair = slots[slot]
        right = dot(blocks[table[SRC + pair]], maps[pair]).astype(jnp.bfloat16)
        return dot(left[pair], right) * scale

    def store(slot, value):
        pair = slots[slot]
        integ[pair] = value
        start[pair] = (value * inverse[pair]).astype(jnp.bfloat16)

    by_twos(found, work, store)


def own_part(table, blocks, maps, left, inverse, scale):
    orbitals = blocks.shape[0]
    count, width, depth = left.shape
    return call(
        functools.partial(own_body, scale, orbitals),
        (
            jax.ShapeDtypeStruct((count, width, width), jnp.float32),
            jax.ShapeDtypeStruct((count, width, width), jnp.bfloat16),
        ),
        (VMEM, VMEM),
        [SMEM, VMEM, VMEM, VMEM, VMEM],
        [pltpu.SMEM((count + 1,), jnp.int32)],
        flops=count * depth * depth * width,
        moved=blocks.size * 2,
        limit=24,
        name="own",
    )(table, blocks, maps, left, inverse)


def serve_body(low, table, blocks, maps, out, slots):
    orbitals = blocks.shape[0]
    size = maps.shape[0]
    found = collect(
        slots.shape[0] - 1,
        lambda p: (table[SERVE + p] >= 0) & (table[SERVE + p] < orbitals),
        slots,
    )

    def work(slot):
        return dot(blocks[table[SERVE + slots[low + slot]]], maps[slot]).astype(jnp.bfloat16)

    def store(slot, half):
        out[slot] = half

    by_twos(jnp.clip(found - low, 0, size), work, store)


def serve(table, blocks, maps, low, count):
    orbitals, depth, wide = blocks.shape
    size, _, width = maps.shape
    return call(
        functools.partial(serve_body, low),
        jax.ShapeDtypeStruct((size, depth, width), jnp.bfloat16),
        VMEM,
        [SMEM, VMEM, VMEM],
        [pltpu.SMEM((count + 1,), jnp.int32)],
        flops=2 * size * depth * wide * width,
        moved=size * depth * (wide + 2 * width) * 2,
        limit=20,
        name="serve",
    )(table, blocks, maps)


def carry_over(integ_in, start_in, integ, start):
    @pl.loop(0, integ.shape[0])
    def _(p):
        integ[p] = integ_in[p]
        start[p] = start_in[p]


def beside_body(scale, table, blocks, maps, left, inverse, integ_in, start_in, integ, start, slots):
    carry_over(integ_in, start_in, integ, start)
    orbitals = blocks.shape[0]
    found = collect(
        left.shape[0],
        lambda p: (table[SRC + p] >= orbitals) & (table[SRC + p] < 2 * orbitals),
        slots,
    )

    def work(slot):
        pair = slots[slot]
        right = dot(blocks[table[SRC + pair] - orbitals], maps[pair]).astype(jnp.bfloat16)
        return dot(left[pair], right) * scale

    def store(slot, value):
        pair = slots[slot]
        integ[pair] = value
        start[pair] = (value * inverse[pair]).astype(jnp.bfloat16)

    by_twos(found, work, store)


def across_body(scale, orbitals, table, *refs):
    n = len(refs) - 8
    halves = refs[:n]
    left, inverse, integ_in, start_in, integ, start, joined, slots = refs[n:]
    carry_over(integ_in, start_in, integ, start)
    low = 0
    for half in halves:
        joined[pl.ds(low, half.shape[0])] = half[...]
        low += half.shape[0]
    found = collect(left.shape[0], lambda p: table[SRC + p] >= 2 * orbitals, slots)

    def work(slot):
        return dot(left[slots[slot]], joined[slot]) * scale

    def store(slot, value):
        pair = slots[slot]
        integ[pair] = value
        start[pair] = (value * inverse[pair]).astype(jnp.bfloat16)

    by_twos(found, work, store)


def integrals_part(body, table, operands, left, inverse, integ, start, scratch, limit, name):
    count, width, depth = left.shape
    n = len(operands)
    return call(
        body,
        (
            jax.ShapeDtypeStruct(integ.shape, integ.dtype),
            jax.ShapeDtypeStruct(start.shape, start.dtype),
        ),
        (VMEM, VMEM),
        [SMEM] + [VMEM] * (n + 4),
        scratch + [pltpu.SMEM((count + 1,), jnp.int32)],
        flops=count * depth * depth * width,
        moved=count * depth * width * 2,
        limit=limit,
        name=name,
    )(table, *operands, left, inverse, integ, start)


CHUNKS = 8
UNIT = 4


def couple(listed, inter, tables, total, amps, ahead, behind, arrived=None):
    count = total.shape[0] - 1
    width = total.shape[1]
    low = 0
    for table in tables:
        amps[pl.ds(low, table.shape[0])] = table[...]
        low += table.shape[0]
    amps[low] = jnp.zeros(amps.shape[1:], amps.dtype)

    @pl.loop(0, count + 1)
    def _(p):
        total[p] = jnp.zeros(total.shape[1:], jnp.float32)

    def codes(group):
        for k in range(UNIT):
            place = 1 + (group * UNIT + k) * 2
            one, two = listed[place], listed[place + 1]
            yield k, one // 65536, (one // 256) % 256, one % 256, (two // 256) % 256, two % 256

    def first(group, mixed):
        for k, _, one, amp_one, two, amp_two in codes(group):
            mixed[k, :, 0:width] = dot(inter[one], amps[amp_one]).astype(jnp.bfloat16)
            mixed[k, :, width : 2 * width] = dot(inter[two], amps[amp_two]).astype(jnp.bfloat16)

    def second(group, mixed):
        for k, pair, one, _, two, _ in codes(group):
            total[pair] += dot_nt(mixed[k], jnp.concatenate([inter[one], inter[two]], axis=1))

    def ready(group, waited):
        if arrived is None:
            return waited
        return arrived(listed[2 * (group + 1) * UNIT] // 65536, waited)

    waited = ready(0, jnp.int32(0))
    first(0, ahead)

    def step(k, waited):
        waited = ready(2 * k + 2, waited)
        first(2 * k + 1, behind)
        second(2 * k, ahead)
        first(2 * k + 2, ahead)
        second(2 * k + 1, behind)
        return waited

    waited = lax.fori_loop(0, (listed[0] + 2 * UNIT - 1) // (2 * UNIT), step, waited)
    if arrived is not None:
        arrived(total.shape[0] - 1, waited)


def opening_body(listed, inter_hbm, here, near_by, integ_hbm, inverse_hbm,
                 out, inter, integ, inverse, total, amps, ahead, behind, sem, more):
    count = integ.shape[0]
    rows = inter.shape[0] // CHUNKS
    pairs = count // CHUNKS

    def piece(k):
        span = pl.ds(k * rows, rows)
        return pltpu.make_async_copy(inter_hbm.at[span], inter.at[span], sem.at[k])

    for k in range(CHUNKS):
        piece(k).start()
    copies = (
        pltpu.make_async_copy(integ_hbm, integ, more.at[0]),
        pltpu.make_async_copy(inverse_hbm, inverse, more.at[1]),
    )
    for copy in copies:
        copy.start()

    def arrived(pair, waited):
        need = jnp.maximum(waited, jnp.minimum(pair // pairs + 1, CHUNKS))
        pl.loop(waited, need)(lambda k: piece(k).wait())
        return need

    couple(listed, inter, (here, near_by), total, amps, ahead, behind, arrived)
    for copy in copies:
        copy.wait()

    @pl.loop(0, count)
    def _(p):
        out[p] = integ[p] + COUPLING * total[p]


def early_body(listed, inter, here, near_by, integ, out, total, *scratch):
    couple(listed, inter, (here, near_by), total, *scratch)

    @pl.loop(0, integ.shape[0])
    def _(p):
        out[p] = integ[p] + COUPLING * total[p]


def late_body(listed, inter, other, so_far, inverse, out, total, *scratch):
    couple(listed, inter, (other,), total, *scratch)

    @pl.loop(0, so_far.shape[0])
    def _(p):
        out[p] = ((so_far[p] + COUPLING * total[p]) * inverse[p]).astype(out.dtype)


def last_body(listed, inter, other, so_far, inverse, integ, out, energy, rows, kept, sem, total, *scratch):
    couple(listed, inter, (other,), total, *scratch)
    width = total.shape[1]
    count = so_far.shape[0]

    def result(p):
        return pltpu.make_async_copy(kept.at[p], out.at[p], sem.at[p])

    @pl.loop(0, count)
    def _(p):
        value = (so_far[p] + COUPLING * total[p]) * inverse[p]
        kept[p] = value
        result(p).start()
        rows[pl.ds(p, 1), :] = jnp.sum(integ[p] * value, axis=0, keepdims=True)

    sums = lax.dot_general(
        jnp.ones((8, width), jnp.float32),
        rows[...],
        (((1,), (1,)), ((), ())),
        precision=lax.Precision.HIGHEST,
        preferred_element_type=jnp.float32,
    )
    energy[...] = sums[0:1, :] * (1.0 / (width * width))
    pl.loop(0, count)(lambda p: result(p).wait())


def coupling_scratch(count, width, tables):
    return [
        pltpu.VMEM((count + 1, width, width), jnp.float32),
        pltpu.VMEM((tables * count + 1, width, width), jnp.bfloat16),
        pltpu.VMEM((UNIT, width, 2 * width), jnp.bfloat16),
        pltpu.VMEM((UNIT, width, 2 * width), jnp.bfloat16),
    ]


def opening_part(listed, inter, here, other, integ, inverse):
    count, width, _ = integ.shape
    return call(
        opening_body,
        tuple(jax.ShapeDtypeStruct(x.shape, x.dtype) for x in (integ, inter, integ, inverse)),
        (VMEM,) * 4,
        [SMEM, HBM, VMEM, VMEM, ANY, ANY],
        coupling_scratch(count, width, 2)
        + [pltpu.SemaphoreType.DMA((CHUNKS,)), pltpu.SemaphoreType.DMA((2,))],
        flops=2 * inter.shape[0] * width**3,
        moved=inter.size * 2,
        limit=26,
        name="opening",
    )(listed, inter, here, other, integ, inverse)


def early_part(listed, inter, here, other, integ):
    count, width, _ = integ.shape
    return call(
        early_body,
        jax.ShapeDtypeStruct(integ.shape, jnp.float32),
        VMEM,
        [SMEM, VMEM, VMEM, VMEM, VMEM],
        coupling_scratch(count, width, 2),
        flops=2 * inter.shape[0] * width**3,
        moved=inter.size * 2,
        limit=24,
        name="early",
    )(listed, inter, here, other, integ)


def late_part(listed, inter, other, so_far, inverse):
    count, width, _ = so_far.shape
    return call(
        late_body,
        jax.ShapeDtypeStruct(so_far.shape, jnp.bfloat16),
        VMEM,
        [SMEM, VMEM, VMEM, VMEM, VMEM],
        coupling_scratch(count, width, 1),
        flops=inter.shape[0] * width**3,
        moved=inter.size * 2,
        limit=24,
        name="late",
    )(listed, inter, other, so_far, inverse)


def last_part(listed, inter, other, so_far, inverse, integ):
    count, width, _ = so_far.shape
    return call(
        last_body,
        (
            jax.ShapeDtypeStruct(so_far.shape, jnp.float32),
            jax.ShapeDtypeStruct((1, count), jnp.float32),
        ),
        (ANY, VMEM),
        [SMEM, VMEM, VMEM, VMEM, VMEM, VMEM],
        [
            pltpu.VMEM((count, width), jnp.float32),
            pltpu.VMEM((count, width, width), jnp.float32),
            pltpu.SemaphoreType.DMA((count,)),
        ]
        + coupling_scratch(count, width, 1),
        flops=inter.shape[0] * width**3,
        moved=inter.size * 2,
        limit=24,
        name="last",
    )(listed, inter, other, so_far, inverse, integ)


def shards(
    blocks,
    pair_orbitals,
    block_sizes,
    pno_maps,
    pno_sizes,
    pno_energy,
    pair_shift,
    neighbours,
    intersections,
):
    devices = lax.axis_size("pairs")
    count, wide, width = pno_maps.shape
    orbitals, depth, _ = blocks.shape
    near = neighbours.shape[1]
    scale = 1.0 / math.sqrt(depth)
    beside_perm = [(i, i ^ 1) for i in range(devices)]
    across_perm = []
    for i in range(1, devices - 1, 2):
        across_perm += [(i, i + 1), (i + 1, i)]
    swap_beside = lambda x: lax.ppermute(x, "pairs", beside_perm)
    swap_across = lambda x: lax.ppermute(x, "pairs", across_perm)

    inter = intersections.reshape(count * near, width, width)
    table, branch = plan(pair_orbitals, block_sizes, orbitals)

    def after(value, *before):
        return lax.optimization_barrier((value,) + before)[0]

    def integrals_with(slots):
        def run(table, blocks, maps, energy, shift, sizes, near_pairs):
            blocks_beside = swap_beside(blocks)
            packed = pack(table, maps, (slots - slots // 2, slots // 2), orbitals)
            got = [swap_across(x) for x in packed]
            left = left_part(table, blocks, maps)
            half_one = serve(after(table, left), blocks, got[0], 0, count)
            back_one = swap_across(half_one)
            inverse, early, late = prepare(after(table, half_one), sizes, shift, near_pairs, energy)
            half_two = serve(after(table, early), blocks, got[1], got[0].shape[0], count)
            back_two = swap_across(half_two)
            integ, start = own_part(after(table, half_two), blocks, maps, left, inverse, scale)
            integ, start = integrals_part(
                functools.partial(beside_body, scale),
                after(table, start),
                (blocks_beside, maps),
                left,
                inverse,
                integ,
                start,
                [],
                24,
                "beside",
            )
            integ, start = integrals_part(
                functools.partial(across_body, scale, orbitals),
                table,
                (back_one, back_two),
                left,
                inverse,
                integ,
                start,
                [pltpu.VMEM((slots, depth, width), jnp.bfloat16)],
                24,
                "across",
            )
            return integ, start, inverse, early, late

        return run

    integ, amps, inverse, early, late = lax.switch(
        branch[0],
        [integrals_with(s) for s in SLOTS],
        table,
        blocks,
        pno_maps,
        pno_energy,
        pair_shift,
        pno_sizes,
        neighbours.T,
    )
    for iteration in range(ITERS):
        far = swap_across(amps)
        close = swap_beside(amps)
        if iteration == 0:
            stay = pltpu.with_memory_space_constraint(inter, pltpu.HBM)
            so_far, inter, integ, inverse = opening_part(early, stay, amps, close, integ, inverse)
        else:
            so_far = early_part(early, inter, amps, close, integ)
        if iteration < ITERS - 1:
            amps = late_part(late, inter, far, so_far, inverse)
        else:
            amps, energies = last_part(late, inter, far, so_far, inverse, integ)
    return (amps, energies.reshape(count))


def solution(mesh):
    in_specs = (
        P("pairs", None, None),
        P(),
        P(),
        P("pairs", None, None),
        P("pairs"),
        P("pairs", None),
        P("pairs"),
        P("pairs", None),
        P("pairs", None, None, None),
    )
    out_specs = (P("pairs", None, None), P("pairs"))
    return jax.shard_map(shards, mesh=mesh, in_specs=in_specs, out_specs=out_specs, check_vma=False)
```
